512 devices in a mesh: ent: 128 (over z, y, core), rep: 4 (over x).
Axes of the slice: x: 4, y: 4, z: 16, core: 2. Of those that a mesh axis runs over, the one named last changes fastest.
Arguments:
- entity_table: float32 [65536, 400], P('ent'), may hold values from -1.8 to 1.8
- adagrad_state: float32 [65536], P('ent'), may hold values from 0.05 to 0.5
- head_owner: int32 [65536, 1], P(('ent', 'rep')), may hold values from 0 to 127; in each aligned block of 128 rows (0 to 127, 128 to 255, ...) at most 2 rows name the same one
- head_row: int32 [65536], P(('ent', 'rep')), may hold values from 0 to 511
- relation_ids: int32 [65536], P(('ent', 'rep')), may hold values from 0 to 63
- tail_owner: int32 [65536, 1], P(('ent', 'rep')), may hold values from 0 to 127; in each aligned block of 128 rows (0 to 127, 128 to 255, ...) at most 2 rows name the same one
- tail_row: int32 [65536], P(('ent', 'rep')), may hold values from 0 to 511
- neg_rows: int32 [512], P('ent'), may hold values from 0 to 511
- relations: float32 [64, 400], replicated, may hold values from -6 to 6
Outputs:
- table_new: float32 [65536, 400], P('ent')
- state_new: float32 [65536], P('ent')
The draws below stay inside these ranges and needn't reach their ends.
Inputs may be any that keep to these rules, and one draw needn't show every extreme that they name: `head_owner`: among the 128 rows of one device no owner is named more than 2 times; in some device one owner is named exactly 2 times. `tail_owner`: among the 128 rows of one device no owner is named more than 2 times; in some device one owner is named exactly 2 times.
All inputs are finite; a program needn't handle non-finite values.
Results may differ from the reference program's by a relative error of at most 0.0001.
Values sent between devices are 32-bit elements; how exact they have to be, the bound alone decides.
No kernel may reach another device: no remote copies, remote signals or barrier semaphores. Data moves between devices by JAX's collectives and lax.ppermute only.
A program may use at most 64 MiB of HBM per device.

```python
import math
import jax
import jax.numpy as jnp
import numpy as np
from jax import lax

W = 400
ROWS_DEV = 512
EDGES_DEV = 128
NEG = 512
RELS = 64
CAP = 2
NEG_DEV = 4
ENTITIES = 65536
EDGES = 65536
N_ENT = 128
N_REP = 4


def with_ends(values, rng, low, high):
    shape = values.shape
    spot = [jax.random.randint(jax.random.fold_in(rng, axis), (), 0, shape[axis]) for axis in range(len(shape))]
    values = values.at[tuple(spot)].set(low)
    longest = shape.index(max(shape))
    spot[longest] = (spot[longest] + 1) % shape[longest]
    return values.at[tuple(spot)].set(high)


def block_scale(stream_key, shape, cuts, least, largest):
    loudness = 1.0
    for axis_at, shards_of in cuts:
        heights = jax.random.uniform(jax.random.fold_in(jax.random.fold_in(stream_key, 6), axis_at), (shards_of,), jnp.float32, least / len(cuts), largest / len(cuts))
        loudness = loudness * jnp.repeat(jnp.exp(heights), shape[axis_at] // shards_of).reshape((-1,) + (1,) * (len(shape) - 1 - axis_at))
    return loudness


def shared_out(key, own, number, rows, count, top, limit, slope):
    ranking = jax.random.permutation(key, count)
    crowded, common = portions_of(count, rows * top, limit, slope, True), portions_of(count, rows * top, limit, slope, False)
    places = jnp.arange(count)

    def named(lengths, offset_by):
        used = int((lengths > 0).sum())
        fixed = max(1, used // 4)
        passed = fixed + (places - fixed + offset_by * (used - fixed)) % max(1, count - fixed)
        return jnp.zeros((count,), jnp.int32).at[ranking[jnp.where(places < fixed, places, passed)]].set(jnp.asarray(lengths, jnp.int32))

    lengths = jnp.where(number % 4 == 0, named(crowded, number // 4), named(common, number - number // 4 - 1))
    mixed = jax.random.permutation(jax.random.fold_in(own, 3), count)
    donor, receiver = mixed[0:count // 2 * 2:2], mixed[1:count // 2 * 2:2]
    room = jnp.minimum(lengths[donor] - 1, limit - lengths[receiver]) // 2
    room = jnp.where((donor == ranking[0]) | (receiver == ranking[0]) | (lengths[receiver] == 0), 0, jnp.maximum(room, 0))
    passed = jax.random.randint(jax.random.fold_in(own, 4), (count // 2,), 0, 1 << 20) % (room + 1)
    lengths = lengths.at[donor].add(-passed).at[receiver].add(passed)
    items = jnp.searchsorted(jnp.cumsum(lengths), jnp.arange(rows * top), side="right").astype(jnp.int32)
    table = items.reshape(top, rows).T
    table = table[jax.random.permutation(jax.random.fold_in(own, 1), rows)]
    offset_by = jax.random.randint(jax.random.fold_in(own, 2), (rows, 1), 0, top)
    return jnp.take_along_axis(table, (jnp.arange(top)[None, :] + offset_by) % top, axis=1)


def portions_of(count, total, most, skew, full):
    loads = [(1 << 20) // math.isqrt(grade ** skew) + 1 for grade in range(1, count + 1)]
    largest = most if full else min(most, max(-(-total // count), total * loads[0] // sum(loads)))
    least = 1 if total - largest >= count - 1 else 0
    counts, rest = [largest] + [least] * (count - 1), total - largest - least * (count - 1)
    while rest > 0:
        movable = [i for i in range(1, count) if counts[i] < largest] or [i for i in range(1, count) if counts[i] < most]
        pool, left = sum([loads[i] for i in movable]), rest
        for i in movable:
            more = min(most - counts[i], max(1, left * loads[i] // pool), rest)
            counts[i] = counts[i] + more
            rest = rest - more
    return np.array(counts)


def centred(own_key, shape, deviation, most, shards=(), kind=jnp.bfloat16):
    result = deviation * jax.random.normal(own_key, shape, jnp.float32)
    if shards:
        result = result * block_scale(own_key, shape, shards, -0.22, 0.18)
    return jnp.clip(result, -most, most).astype(kind)


def setup_inputs(seed: int = 0) -> dict:
    streams_of = jax.random.split(jax.random.key(seed), 10)
    entity_table = centred(streams_of[0], (ENTITIES, W), 0.3, 1.8, ((0, 128),), jnp.float32)
    adagrad_state = jnp.clip(jnp.exp(math.log(0.5) - 2.3025851 * jax.random.uniform(streams_of[1], (ENTITIES,), jnp.float32) ** block_scale(streams_of[1], (ENTITIES,), ((0, 128),), -0.2, 0.2)), 0.05, 0.5)
    head_owner_keys = jax.random.split(jax.random.fold_in(streams_of[2], 1), EDGES // EDGES_DEV)
    head_owner_turns = jax.random.permutation(jax.random.fold_in(streams_of[2], 3), EDGES // EDGES_DEV)
    head_owner = jax.vmap(lambda own, number: shared_out(jax.random.fold_in(streams_of[2], 2), own, number, EDGES_DEV, N_ENT, 1, CAP, 2))(head_owner_keys, head_owner_turns).reshape((EDGES, 1))
    head_row = with_ends(jax.random.randint(streams_of[3], (EDGES,), 0, ROWS_DEV), jax.random.fold_in(streams_of[3], 1), 0, ROWS_DEV - 1).astype(jnp.int32)
    relation_ids = with_ends(jax.random.randint(streams_of[4], (EDGES,), 0, RELS), jax.random.fold_in(streams_of[4], 1), 0, RELS - 1).astype(jnp.int32)
    tail_owner_keys = jax.random.split(jax.random.fold_in(streams_of[5], 1), EDGES // EDGES_DEV)
    tail_owner_turns = jax.random.permutation(jax.random.fold_in(streams_of[5], 3), EDGES // EDGES_DEV)
    tail_owner = jax.vmap(lambda own, number: shared_out(jax.random.fold_in(streams_of[5], 2), own, number, EDGES_DEV, N_ENT, 1, CAP, 2))(tail_owner_keys, tail_owner_turns).reshape((EDGES, 1))
    tail_row = with_ends(jax.random.randint(streams_of[6], (EDGES,), 0, ROWS_DEV), jax.random.fold_in(streams_of[6], 1), 0, ROWS_DEV - 1).astype(jnp.int32)
    neg_rows = with_ends(jax.random.randint(streams_of[7], (NEG,), 0, ROWS_DEV), jax.random.fold_in(streams_of[7], 1), 0, ROWS_DEV - 1).astype(jnp.int32)
    relations = centred(streams_of[8], (RELS, W), 1.0, 6.0, (), jnp.float32)
    return {"entity_table": entity_table, "adagrad_state": adagrad_state, "head_owner": head_owner, "head_row": head_row, "relation_ids": relation_ids, "tail_owner": tail_owner, "tail_row": tail_row, "neg_rows": neg_rows, "relations": relations}


learn_rate = 0.1

def complex_mul(left_re, left_im, right_re, right_im):
    return (left_re * right_re - left_im * right_im, left_re * right_im + left_im * right_re)

def edge_terms(heads, tails, rel_vecs, negatives):
    half = heads.shape[1] // 2
    head_re, head_im = (heads[:, :half], heads[:, half:])
    tail_re, tail_im = (tails[:, :half], tails[:, half:])
    rel_re, rel_im = (rel_vecs[:, :half], rel_vecs[:, half:])
    query = jnp.concatenate(complex_mul(head_re, head_im, rel_re, rel_im), 1)
    probe = jnp.concatenate(complex_mul(rel_re, -rel_im, tail_re, tail_im), 1)
    pos_score = lax.optimization_barrier(jnp.sum(heads * probe, 1))
    dims = (((1,), (1,)), ((), ()))
    tail_scores = lax.dot_general(query, negatives, dims, precision=lax.Precision.HIGHEST)
    head_scores = lax.dot_general(probe, negatives, dims, precision=lax.Precision.HIGHEST)
    neg_weight = 1.0 / math.sqrt(negatives.shape[0])
    tail_coef = jax.nn.sigmoid(tail_scores) * neg_weight
    head_coef = jax.nn.sigmoid(head_scores) * neg_weight
    pos_coef = -jax.nn.sigmoid(-pos_score)[:, None]
    query_grad = jnp.dot(tail_coef, negatives, precision=lax.Precision.HIGHEST)
    probe_grad = jnp.dot(head_coef, negatives, precision=lax.Precision.HIGHEST)
    head_grad = pos_coef * probe + jnp.concatenate(complex_mul(query_grad[:, :half], query_grad[:, half:], rel_re, -rel_im), 1)
    tail_grad = pos_coef * query + jnp.concatenate(complex_mul(probe_grad[:, :half], probe_grad[:, half:], rel_re, rel_im), 1)
    back = (((0,), (0,)), ((), ()))
    negs_grad = lax.dot_general(tail_coef, query, back, precision=lax.Precision.HIGHEST)
    negs_grad = negs_grad + lax.dot_general(head_coef, probe, back, precision=lax.Precision.HIGHEST)
    return (head_grad, tail_grad, negs_grad)

def reference(entity_table, adagrad_state, head_owner, head_row, relation_ids, tail_owner, tail_row, neg_rows, relations):
    buckets = N_ENT * N_REP
    head_ids = (head_owner[:, 0] * ROWS_DEV + head_row).astype(jnp.int32).reshape(buckets, EDGES_DEV)
    tail_ids = (tail_owner[:, 0] * ROWS_DEV + tail_row).astype(jnp.int32).reshape(buckets, EDGES_DEV)
    rel_ids = relation_ids.astype(jnp.int32).reshape(buckets, EDGES_DEV)
    block_of = jnp.arange(NEG, dtype=jnp.int32) // NEG_DEV * ROWS_DEV
    neg_ids = (block_of + neg_rows).astype(jnp.int32)
    negatives = entity_table[neg_ids]

    def advance(running, inputs):
        grad_table, grad_negs = running
        head_idx, tail_idx, rel_idx = inputs
        head_grad, tail_grad, negs_grad = edge_terms(entity_table[head_idx], entity_table[tail_idx], relations[rel_idx], negatives)
        grad_table = grad_table.at[head_idx].add(head_grad).at[tail_idx].add(tail_grad)
        return ((grad_table, grad_negs + negs_grad), None)
    start = (jnp.zeros_like(entity_table), jnp.zeros_like(negatives))
    (grad_table, grad_negs), _ = lax.scan(advance, start, (head_ids, tail_ids, rel_ids))
    grad_table = grad_table.at[neg_ids].add(grad_negs)
    state_new = adagrad_state + lax.optimization_barrier(jnp.mean(grad_table * grad_table, 1))
    table_new = entity_table - learn_rate * grad_table / jnp.sqrt(state_new)[:, None]
    return (table_new, state_new)
```

```python
import math

import jax
import jax.numpy as jnp
from jax import lax
from jax.experimental import pallas as pl
from jax.experimental.pallas import tpu as pltpu
from jax.sharding import PartitionSpec as P

learn_rate = 0.1

LANE = 128
f32 = jnp.float32
bf16 = jnp.bfloat16
NN = (((1,), (0,)), ((), ()))
NT = (((1,), (1,)), ((), ()))
TN = (((0,), (0,)), ((), ()))
TILES1 = 4
TILES2 = 13
TILES3 = 16


def dot(a, b, dims):
    return lax.dot_general(a, b, dims, preferred_element_type=f32)


def parts(x, count):
    out = []
    for _ in range(count):
        head = x.astype(bf16)
        out.append(head)
        x = x - head.astype(f32)
    return out


def pick(onehot, pieces, dims):
    total = dot(onehot, pieces[0], dims)
    for piece in pieces[1:]:
        total = total + dot(onehot, piece, dims)
    return total


def dot3(a, b, dims):
    a0, a1 = parts(a, 2)
    b0, b1 = parts(b, 2)
    return dot(a0, b0, dims) + (dot(a0, b1, dims) + dot(a1, b0, dims))


def lanes(shape):
    return lax.broadcasted_iota(jnp.int32, shape, len(shape) - 1)


def cmul(a, b):
    return (a[0] * b[0] - a[1] * b[1], a[0] * b[1] + a[1] * b[0])


def conj(a):
    return (a[0], -a[1])


def sigmoid(x):
    return 1.0 / (1.0 + jnp.exp(-x))


def column(tile, lane):
    return jnp.sum(jnp.where(lanes(tile.shape) == lane, tile, 0.0), 1, keepdims=True)


def pack(ref, tiles, halves):
    n = halves[0].shape[0]
    at = lanes((n, LANE))
    tail = jnp.zeros((n, LANE), f32)
    for i, half in enumerate(halves):
        ref[pl.ds(i, n, stride=tiles), :] = half[:, :LANE]
        rest = half[:, LANE:]
        shift = (8 * i - 64) % LANE
        moved = pltpu.roll(rest, shift, 1) if shift else rest
        tail = jnp.where((at >= 8 * i) & (at < 8 * i + 8), moved, tail)
    for i in range(0, len(halves), 2):
        low, high = halves[i][:, LANE:], halves[i + 1][:, LANE:]
        ref[pl.ds(len(halves) + i // 2, n, stride=tiles), :] = jnp.where(
            at < 64, low, pltpu.roll(high, 64, 1)
        )
    ref[pl.ds(len(halves) * 3 // 2, n, stride=tiles), :] = tail


def unpack(ref, tiles, count, n):
    at = lanes((n, LANE))
    tail = ref[pl.ds(count * 3 // 2, n, stride=tiles), :]
    out = []
    for i in range(count):
        full = ref[pl.ds(i, n, stride=tiles), :]
        pair = ref[pl.ds(count + i // 2, n, stride=tiles), :]
        if i % 2:
            pair = pltpu.roll(pair, 64, 1)
        shift = (64 - 8 * i) % LANE
        moved = pltpu.roll(tail, shift, 1) if shift else tail
        rest = jnp.where(at < 64, pair, jnp.where(at < 72, moved, 0.0))
        out.append(jnp.concatenate([full, rest], 1))
    return out


def ask_kernel(neg_at, ints, table_t, send, head_edge, tail_edge):
    n = LANE
    vals = ints[...].astype(f32)
    sub = lax.broadcasted_iota(jnp.int32, (n, n), 0)
    lane = lanes((n, n))

    def row(i):
        return jnp.broadcast_to(vals[i : i + 1, :], (n, n))

    head_owner, head_row, rel, tail_owner, tail_row = (row(i) for i in range(5))
    owner_id = sub.astype(f32)
    columns = []

    def slots(owner, named):
        owner_c = owner.T
        rank = jnp.sum(jnp.where((owner == owner_c) & (sub < lane), 1.0, 0.0), 0, keepdims=True)
        rank = jnp.broadcast_to(rank, (n, n))
        edges = []
        for s in range(2):
            here = (owner == owner_id) & (rank == float(s))
            columns.append(jnp.sum(jnp.where(here, named + 1.0, 0.0), 1, keepdims=True) - 1.0)
            columns.append(jnp.sum(jnp.where(here, rel, 0.0), 1, keepdims=True))
            edges.append(
                jnp.sum(jnp.where(here, lane.astype(f32) + 1.0, 0.0), 1, keepdims=True) - 1.0
            )
        return edges

    edges = slots(head_owner, head_row)
    head_edge[...] = jnp.where(lane == 0, edges[0], jnp.where(lane == 1, edges[1], -1.0))
    edges = slots(tail_owner, tail_row)
    both = jnp.where(lane == 0, edges[0], jnp.where(lane == 1, edges[1], -1.0)).T
    tail_edge[...] = jnp.where(both[:8, :] < 0.0, -2.0, both[:8, :])

    hot = jnp.where(lanes((8, 512)) == neg_at[0], 1.0, 0.0).astype(bf16)
    re = pick(hot, parts(table_t[0:200, :], 3), NT)[0:1, :]
    im = pick(hot, parts(table_t[200:400, :], 3), NT)[0:1, :]

    def wide(x):
        return jnp.broadcast_to(x, (n, x.shape[1]))

    send[pl.ds(0, n, stride=TILES1), :] = wide(re[:, :LANE])
    send[pl.ds(2, n, stride=TILES1), :] = wide(im[:, :LANE])
    pad = jnp.zeros((1, 56), f32)
    tile = wide(jnp.concatenate([re[:, LANE:], pad], 1))
    for i, col in enumerate(columns):
        tile = jnp.where(lane == 72 + i, col, tile)
    send[pl.ds(1, n, stride=TILES1), :] = tile
    send[pl.ds(3, n, stride=TILES1), :] = wide(jnp.concatenate([im[:, LANE:], pad], 1))


def table_halves(table_t):
    pad = jnp.zeros((56, table_t.shape[1]), f32)
    return [jnp.concatenate([table_t[i : i + 200, :], pad], 0) for i in (0, 200)]


def rel_vectors(tile, slot, rel_ref):
    ids = column(tile, 72 + 2 * slot + 1)
    hot = jnp.where(lanes((tile.shape[0], 64)).astype(f32) == ids, 1.0, 0.0).astype(bf16)
    both = pick(hot, parts(rel_ref[...], 3), NN)
    return (both[:, :256], both[:, 256:])


def fetch_kernel(recv, table_t, rel_ref, send, rows):
    n = LANE
    tile = recv[pl.ds(1, n, stride=TILES1), :]
    pieces = [parts(half, 3) for half in table_halves(table_t)]
    halves = []
    for s in range(4):
        at = column(tile, 72 + 2 * s)
        hot = jnp.where(lanes((n, 512)).astype(f32) == at, 1.0, 0.0).astype(bf16)
        vec = tuple(pick(hot, p, NT) for p in pieces)
        if s < 2:
            vec = cmul(vec, rel_vectors(tile, s, rel_ref))
        halves += vec
        rows[s * n : (s + 1) * n, 0:256] = vec[0]
        rows[s * n : (s + 1) * n, 256:512] = vec[1]
    pack(send, TILES2, halves)


def negatives_kernel(recv, rows, rel_ref, neg0, neg1, neg2, neg3, near, far, rels, out0, out1, out2, out3):
    n = LANE
    tile = recv[pl.ds(1, n, stride=TILES1), :]
    negs = []
    keep = lanes((n, LANE)) < 72
    for ref in (neg0, neg1, neg2, neg3):
        got = [ref[pl.ds(i, n, stride=TILES1), :] for i in range(4)]
        got[1] = jnp.where(keep, got[1], 0.0)
        negs.append(jnp.concatenate(got, 1))
    negs = jnp.concatenate(negs, 0)
    weight = 1.0 / math.sqrt(512.0)
    total = None
    for side in range(2):
        x, rel, valid = [], [], []
        for s in (2 * side, 2 * side + 1):
            vec = (rows[s * n : (s + 1) * n, 0:256], rows[s * n : (s + 1) * n, 256:512])
            rv = rel_vectors(tile, s, rel_ref)
            if side:
                vec = cmul(conj(rv), vec)
            x.append(jnp.concatenate(vec, 1))
            rel.append(rv)
            valid.append(column(tile, 72 + 2 * s))
        x = jnp.concatenate(x, 0)
        valid = jnp.concatenate(valid, 0)
        scores = dot3(x, negs, NT)
        coef = jnp.where(valid >= 0.0, sigmoid(scores) * weight, 0.0)
        back = dot3(coef, negs, NN)
        for i in range(2):
            part = (back[i * n : (i + 1) * n, 0:256], back[i * n : (i + 1) * n, 256:512])
            s = 2 * side + i
            rv = rel[i]
            if side:
                part = cmul(part, rv)
                far[i * n : (i + 1) * n, 0:256] = part[0]
                far[i * n : (i + 1) * n, 256:512] = part[1]
            else:
                near[i * n : (i + 1) * n, 0:256] = part[0]
                near[i * n : (i + 1) * n, 256:512] = part[1]
                rels[i * n : (i + 1) * n, 0:256] = rv[0]
                rels[i * n : (i + 1) * n, 256:512] = rv[1]
        grad = dot3(coef, x, TN)
        total = grad if total is None else total + grad
    for i, ref in enumerate((out0, out1, out2, out3)):
        ref[...] = total[i * n : (i + 1) * n, :]


def edge_kernel(recv, head_edge, tail_edge, sum0, sum1, sum2, sum3, send):
    n = LANE
    halves = unpack(recv, TILES2, 8, n)
    head_at = jnp.concatenate([head_edge[:, 0:1], head_edge[:, 1:2]], 0)
    tail_at = jnp.concatenate([tail_edge[0:1, :], tail_edge[1:2, :]], 1)
    same = jnp.where(head_at == tail_at, 1.0, 0.0).astype(bf16)
    query = jnp.concatenate(
        [jnp.concatenate(halves[0:2], 1), jnp.concatenate(halves[2:4], 1)], 0
    )
    tails = jnp.concatenate(
        [jnp.concatenate(halves[4:6], 1), jnp.concatenate(halves[6:8], 1)], 0
    )
    met = pick(same, parts(tails, 3), NN)
    pos = jnp.sum(query * met, 1, keepdims=True)
    coef = jnp.where(head_at >= 0.0, -sigmoid(-pos), 0.0)
    to_head = coef * met
    to_tail = pick(same, parts(coef * query, 3), TN)
    neg = sum0[...] + sum1[...] + (sum2[...] + sum3[...])
    out = []
    for block in (to_head[:n], to_head[n:], to_tail[:n], to_tail[n:], neg):
        out += [block[:, :256], block[:, 256:]]
    pack(send, TILES3, out)


def scatter_kernel(neg_at, recv, asks, near, far, rels, out):
    n = LANE
    halves = unpack(recv, TILES3, 10, n)
    tile = asks[pl.ds(1, n, stride=TILES1), :]
    hots, grads = [], []
    for s in range(4):
        vec = (halves[2 * s], halves[2 * s + 1])
        base = (s % 2) * n
        other = near if s < 2 else far
        vec = tuple(
            v + other[base : base + n, i * 256 : (i + 1) * 256] for i, v in enumerate(vec)
        )
        if s < 2:
            rv = (rels[base : base + n, 0:256], rels[base : base + n, 256:512])
            vec = cmul(vec, conj(rv))
        at = column(tile, 72 + 2 * s)
        hots.append(jnp.where(lanes((n, 512)).astype(f32) == at, 1.0, 0.0).astype(bf16))
        grads.append(vec)
    hots.append(jnp.where(lanes((n, 512)) == neg_at[0], 1.0, 0.0).astype(bf16))
    grads.append((halves[8], halves[9]))
    hot = jnp.concatenate(hots, 0)
    for i in range(2):
        grad = jnp.concatenate([g[i] for g in grads], 0)
        pieces = parts(grad, 3)
        total = dot(pieces[0], hot, TN)
        for piece in pieces[1:]:
            total = total + dot(piece, hot, TN)
        for q in range(4):
            out[q, i * 200 : (i + 1) * 200, :] = total[0:200, q * n : (q + 1) * n]


def update_kernel(rep, grads, table_t, state, out):
    n = LANE
    grad = grads[0] + grads[1] + (grads[2] + grads[3])
    start = pl.multiple_of(rep[0] * n, n)
    mean = jnp.sum(grad * grad, 0, keepdims=True) * (1.0 / 400.0)
    new = state[:, pl.ds(start, n)] + mean
    out[0:400, :] = table_t[:, pl.ds(start, n)] - learn_rate * grad / jnp.sqrt(new)
    out[400:408, :] = jnp.broadcast_to(new, (8, n))


def call(kernel, outs, args, scalars=0, name=None):
    space = pl.BlockSpec(memory_space=pltpu.VMEM)
    specs = [pl.BlockSpec(memory_space=pltpu.SMEM)] * scalars + [space] * (len(args) - scalars)
    return pl.pallas_call(
        kernel,
        out_shape=[jax.ShapeDtypeStruct(s, f32) for s in outs],
        in_specs=specs,
        out_specs=[space] * len(outs),
        name=name,
    )(*args)


def exchange(x, axis, tiles):
    n = lax.axis_size(axis)
    x = x.reshape(n, 1, tiles * LANE)
    x = lax.all_to_all(x, axis, split_axis=0, concat_axis=0, tiled=True)
    return x.reshape(n * tiles, LANE)


def shift(x, by):
    n = lax.axis_size("rep")
    return lax.ppermute(x, "rep", [(i, (i + by) % n) for i in range(n)])


def on_device(
    entity_table,
    adagrad_state,
    head_owner,
    head_row,
    relation_ids,
    tail_owner,
    tail_row,
    neg_rows,
    relations,
):
    rep = lax.axis_index("rep")
    table_t = entity_table.T
    neg_at = lax.dynamic_slice(neg_rows, (rep,), (1,))
    ints = jnp.stack([head_owner[:, 0], head_row, relation_ids, tail_owner[:, 0], tail_row])
    zero = jnp.zeros((relations.shape[0], 56), f32)
    rel_wide = jnp.concatenate([relations[:, :200], zero, relations[:, 200:], zero], 1)

    n = LANE
    send1, head_edge, tail_edge = call(
        ask_kernel,
        [(n * TILES1, n), (n, n), (8, n)],
        (neg_at, ints, table_t),
        1,
        "ask",
    )
    recv1 = exchange(send1, "ent", TILES1)
    send2, rows = call(
        fetch_kernel, [(n * TILES2, n), (4 * n, 512)], (recv1, table_t, rel_wide), 0, "fetch"
    )
    recv2 = exchange(send2, "ent", TILES2)
    negs = [recv1] + [shift(recv1, -j) for j in (1, 2, 3)]
    near, far, rels, *owned = call(
        negatives_kernel,
        [(2 * n, 512)] * 3 + [(n, 512)] * 4,
        (recv1, rows, rel_wide, *negs),
        0,
        "negatives",
    )
    sums = [owned[0]] + [shift(owned[j], j) for j in (1, 2, 3)]
    (send3,) = call(
        edge_kernel, [(n * TILES3, n)], (recv2, head_edge, tail_edge, *sums), 0, "edge"
    )
    recv3 = exchange(send3, "ent", TILES3)
    (grads,) = call(
        scatter_kernel, [(4, 400, n)], (neg_at, recv3, recv1, near, far, rels), 1, "scatter"
    )
    grads = lax.all_to_all(grads, "rep", split_axis=0, concat_axis=0, tiled=True)
    (fresh,) = call(
        update_kernel,
        [(408, n)],
        (rep.reshape(1).astype(jnp.int32), grads, table_t, adagrad_state.reshape(1, 512)),
        1,
        "update",
    )
    fresh = lax.all_gather(fresh, "rep", axis=0, tiled=False)
    table_new = fresh[:, :400, :].transpose(0, 2, 1).reshape(512, 400)
    state_new = fresh[:, 400, :].reshape(512)
    return (table_new, state_new)


def solution(mesh):
    placed = (
        P("ent", None),
        P("ent"),
        P(("ent", "rep"), None),
        P(("ent", "rep")),
        P(("ent", "rep")),
        P(("ent", "rep"), None),
        P(("ent", "rep")),
        P("ent"),
        P(),
    )
    return jax.shard_map(
        on_device, mesh=mesh, in_specs=placed, out_specs=(P("ent", None), P("ent")), check_vma=False
    )
```

```python
import math

import jax
import jax.numpy as jnp
from jax import lax
from jax.experimental import pallas as pl
from jax.experimental.pallas import tpu as pltpu
from jax.sharding import PartitionSpec as P

learn_rate = 0.1

LANE = 128
f32 = jnp.float32
bf16 = jnp.bfloat16
NN = (((1,), (0,)), ((), ()))
NT = (((1,), (1,)), ((), ()))
TN = (((0,), (0,)), ((), ()))
PIECES = 2
TILES1 = 4
TILES2 = 13
TILES3 = 16
GROUP = 32


def dot(a, b, dims):
    return lax.dot_general(a, b, dims, preferred_element_type=f32)


def parts(x, count):
    out = []
    for _ in range(count):
        head = x.astype(bf16)
        out.append(head)
        x = x - head.astype(f32)
    return out


def pick(onehot, pieces, dims):
    total = dot(onehot, pieces[0], dims)
    for piece in pieces[1:]:
        total = total + dot(onehot, piece, dims)
    return total


def dot3(a, b, dims):
    a0, a1 = parts(a, 2)
    b0, b1 = parts(b, 2)
    return dot(a0, b0, dims) + (dot(a0, b1, dims) + dot(a1, b0, dims))


def lanes(shape):
    return lax.broadcasted_iota(jnp.int32, shape, len(shape) - 1)


def cmul(a, b):
    return (a[0] * b[0] - a[1] * b[1], a[0] * b[1] + a[1] * b[0])


def conj(a):
    return (a[0], -a[1])


def sigmoid(x):
    return 1.0 / (1.0 + jnp.exp(-x))


def column(tile, lane):
    return jnp.sum(jnp.where(lanes(tile.shape) == lane, tile, 0.0), 1, keepdims=True)


def pack(ref, tiles, halves, base=0):
    n = halves[0].shape[0]
    at = lanes((n, LANE))
    tail = jnp.zeros((n, LANE), f32)
    for i, half in enumerate(halves):
        ref[pl.ds(base + i, n, stride=tiles), :] = half[:, :LANE]
        rest = half[:, LANE:]
        shift = (8 * i - 64) % LANE
        moved = pltpu.roll(rest, shift, 1) if shift else rest
        tail = jnp.where((at >= 8 * i) & (at < 8 * i + 8), moved, tail)
    for i in range(0, len(halves), 2):
        low, high = halves[i][:, LANE:], halves[i + 1][:, LANE:]
        ref[pl.ds(base + len(halves) + i // 2, n, stride=tiles), :] = jnp.where(
            at < 64, low, pltpu.roll(high, 64, 1)
        )
    ref[pl.ds(base + len(halves) * 3 // 2, n, stride=tiles), :] = tail


def unpack(ref, tiles, count, n):
    at = lanes((n, LANE))
    tail = ref[pl.ds(count * 3 // 2, n, stride=tiles), :]
    out = []
    for i in range(count):
        full = ref[pl.ds(i, n, stride=tiles), :]
        pair = ref[pl.ds(count + i // 2, n, stride=tiles), :]
        if i % 2:
            pair = pltpu.roll(pair, 64, 1)
        shift = (64 - 8 * i) % LANE
        moved = pltpu.roll(tail, shift, 1) if shift else tail
        rest = jnp.where(at < 64, pair, jnp.where(at < 72, moved, 0.0))
        out.append(jnp.concatenate([full, rest], 1))
    return out


def ask_kernel(rep, neg_rows, head_owner, head_row, rel, tail_owner, tail_row, table_t, send, head_edge, tail_edge):
    n = LANE
    sub = lax.broadcasted_iota(jnp.int32, (n, n), 0)
    lane = lanes((n, n))

    def wide(x):
        return jnp.broadcast_to(x, (n, x.shape[1]))

    head_owner, head_row, rel, tail_owner, tail_row = (
        wide(ref[...].astype(f32)) for ref in (head_owner, head_row, rel, tail_owner, tail_row)
    )
    owner_id = sub.astype(f32)
    columns = []

    def slots(owner, named):
        owner_c = owner.T
        rank = jnp.sum(jnp.where((owner == owner_c) & (sub < lane), 1.0, 0.0), 0, keepdims=True)
        edges = []
        for s in range(2):
            here = (owner == owner_id) & (wide(rank) == float(s))
            columns.append(jnp.sum(jnp.where(here, named + 1.0, 0.0), 1, keepdims=True) - 1.0)
            columns.append(jnp.sum(jnp.where(here, rel, 0.0), 1, keepdims=True))
            edges.append(
                jnp.sum(jnp.where(here, lane.astype(f32) + 1.0, 0.0), 1, keepdims=True) - 1.0
            )
        return jnp.where(lane == 0, edges[0], jnp.where(lane == 1, edges[1], -1.0))

    head_edge[...] = slots(head_owner, head_row)
    tail_edge[...] = slots(tail_owner, tail_row)

    neg_at = neg_rows[rep[0]]
    block = table_t[:, pl.ds(pl.multiple_of(neg_at // n * n, n), n)]
    pad = jnp.zeros((56, n), f32)
    for i in range(2):
        half = jnp.concatenate([block[200 * i : 200 * i + 200, :], pad], 0).T
        picked = lax.broadcasted_iota(jnp.int32, (n, 256), 0) == neg_at % n
        line = jnp.sum(jnp.where(picked, half, 0.0), 0, keepdims=True)
        send[pl.ds(2 * i, n, stride=TILES1), :] = wide(line[:, :n])
        tile = wide(line[:, n:])
        if i == 0:
            for j, col in enumerate(columns):
                tile = jnp.where(lane == 72 + j, col, tile)
        send[pl.ds(2 * i + 1, n, stride=TILES1), :] = tile


def ahead_kernel(table_t, relations, head_edge, tail_edge, *outs):
    pad = jnp.zeros((56, 512), f32)
    whole = jnp.concatenate([table_t[0:200, :], pad, table_t[200:400, :], pad], 0).T
    for ref, piece in zip(outs[:PIECES], parts(whole, PIECES), strict=True):
        ref[...] = piece
    pad = jnp.zeros((64, 56), f32)
    whole = jnp.concatenate([relations[:, :200], pad, relations[:, 200:], pad], 1)
    for ref, piece in zip(outs[PIECES : 2 * PIECES], parts(whole, PIECES), strict=True):
        ref[...] = piece
    same, same_t = outs[2 * PIECES :]

    def stack(ref, by_rows):
        if by_rows:
            turned = ref[...].T
            return jnp.concatenate([turned[0:1, :], turned[1:2, :]], 1)
        return jnp.concatenate([ref[:, 0:1], ref[:, 1:2]], 0)

    for ref, one, other in ((same, head_edge, tail_edge), (same_t, tail_edge, head_edge)):
        col, row = stack(one, False), stack(other, True)
        ref[...] = jnp.where((col == row) & (col >= 0.0), 1.0, 0.0).astype(bf16)


def rel_vectors(tile, slots, pieces):
    ids = jnp.concatenate([column(tile, 72 + 2 * s + 1) for s in slots], 0)
    hot = jnp.where(lanes((ids.shape[0], 64)).astype(f32) == ids, 1.0, 0.0).astype(bf16)
    both = pick(hot, [p[...] for p in pieces], NN)
    return (both[:, :256], both[:, 256:])


def split(x):
    return (x[:, :256], x[:, 256:])


def fetch_kernel(recv, *refs):
    n = LANE
    table, rel = refs[:PIECES], refs[PIECES : 2 * PIECES]
    send, rows = refs[2 * PIECES :]
    tile = recv[pl.ds(1, n, stride=TILES1), :]
    halves = []
    for side in range(2):
        slots = (2 * side, 2 * side + 1)
        at = jnp.concatenate([column(tile, 72 + 2 * s) for s in slots], 0)
        hot = jnp.where(lanes((2 * n, 512)).astype(f32) == at, 1.0, 0.0).astype(bf16)
        vec = split(pick(hot, [p[...] for p in table], NN))
        if side == 0:
            vec = cmul(vec, rel_vectors(tile, slots, rel))
        for i in range(2):
            halves += [v[i * n : (i + 1) * n, :] for v in vec]
        for i in range(2):
            rows[2 * n * side : 2 * n * (side + 1), i * 256 : (i + 1) * 256] = vec[i]
    pack(send, TILES2, halves)


def negatives_kernel(recv, rows, *refs):
    n = LANE
    rel = refs[:PIECES]
    *negs, near, far, rels, out0, out1, out2, out3 = refs[PIECES:]
    tile = recv[pl.ds(1, n, stride=TILES1), :]
    keep = lanes((n, LANE)) < 72
    tiles = []
    for ref in negs:
        got = [ref[pl.ds(i, n, stride=TILES1), :] for i in range(4)]
        got[1] = jnp.where(keep, got[1], 0.0)
        tiles.append(jnp.concatenate(got, 1))
    negs = jnp.concatenate(tiles, 0)
    weight = 1.0 / math.sqrt(512.0)
    total = None
    for side in range(2):
        slots = (2 * side, 2 * side + 1)
        x = rows[2 * n * side : 2 * n * (side + 1), :]
        rv = rel_vectors(tile, slots, rel)
        if side:
            x = jnp.concatenate(cmul(conj(rv), split(x)), 1)
        valid = jnp.concatenate([column(tile, 72 + 2 * s) for s in slots], 0)
        scores = dot3(x, negs, NT)
        coef = jnp.where(valid >= 0.0, sigmoid(scores) * weight, 0.0)
        back = dot3(coef, negs, NN)
        if side:
            far[...] = jnp.concatenate(cmul(split(back), rv), 1)
        else:
            near[...] = back
            rels[...] = jnp.concatenate(rv, 1)
        grad = dot3(coef, x, TN)
        total = grad if total is None else total + grad
    for i, ref in enumerate((out0, out1, out2, out3)):
        ref[...] = total[i * n : (i + 1) * n, :]


def edge_kernel(recv, same, same_t, head_edge, sum0, sum1, sum2, sum3, send, token):
    n = LANE
    halves = unpack(recv, TILES2, 8, n)
    head_at = jnp.concatenate([head_edge[:, 0:1], head_edge[:, 1:2]], 0)
    query, tails = (
        jnp.concatenate(
            [jnp.concatenate(halves[i : i + 2], 1), jnp.concatenate(halves[i + 2 : i + 4], 1)], 0
        )
        for i in (0, 4)
    )
    met = pick(same[...], parts(tails, PIECES), NN)
    pos = jnp.sum(query * met, 1, keepdims=True)
    coef = jnp.where(head_at >= 0.0, -sigmoid(-pos), 0.0)
    to_head = coef * met
    to_tail = pick(same_t[...], parts(coef * query, PIECES), NN)
    neg = sum0[...] + sum1[...] + (sum2[...] + sum3[...])
    out = []
    for block in (to_head[:n], to_head[n:], to_tail[:n], to_tail[n:], neg):
        out += [block[:, :256], block[:, 256:]]
    pack(send, TILES3, out)
    token[...] = neg[0:8, 0:128]


def place_kernel(rep, neg_rows, asks, token, *refs):
    n = LANE
    *sides, side, hot = refs
    for i, source in enumerate(sides):
        side[i * 2 * n : (i + 1) * 2 * n, :] = source[...]
    turned = asks[pl.ds(1, n, stride=TILES1), :].T
    sub = lax.broadcasted_iota(jnp.int32, (512, n), 0)
    for s in range(4):
        at = turned[72 + 2 * s : 73 + 2 * s, :]
        hot[:, s * n : (s + 1) * n] = jnp.where(sub.astype(f32) == at, 1.0, 0.0).astype(bf16)
    hot[:, 4 * n :] = jnp.where(sub == neg_rows[rep[0]], 1.0, 0.0).astype(bf16)


def scatter_kernel(recv, hot, side, out):
    n = LANE
    halves = unpack(recv, TILES3, 10, n)
    blocks = [jnp.concatenate(halves[i : i + 2], 1) for i in range(0, 10, 2)]
    head = split(jnp.concatenate(blocks[0:2], 0) + side[0 : 2 * n, :])
    head = jnp.concatenate(cmul(head, conj(split(side[4 * n :, :]))), 1)
    tail = jnp.concatenate(blocks[2:4], 0) + side[2 * n : 4 * n, :]
    grad = jnp.concatenate([head, tail, blocks[4]], 0)
    total = pick(hot[...], parts(grad, PIECES), NN)
    for q in range(4):
        groups = []
        for g in range(4):
            start = q * n + g * GROUP
            groups += split(total[start : start + GROUP, :])
        pack(out, TILES2, groups, q * TILES2 * GROUP)


def update_kernel(rep, grads, table_t, state, out, sums):
    n = LANE
    rows = TILES2 * GROUP
    sums[...] = (
        grads[0:rows, :] + grads[rows : 2 * rows, :]
        + (grads[2 * rows : 3 * rows, :] + grads[3 * rows :, :])
    )
    halves = unpack(sums, TILES2, 8, GROUP)
    grad = jnp.concatenate(
        [jnp.concatenate(halves[i::2], 0).T[0:200, :] for i in range(2)], 0
    )
    start = pl.multiple_of(rep[0] * n, n)
    mean = jnp.sum(grad * grad, 0, keepdims=True) * (1.0 / 400.0)
    new = state[:, pl.ds(start, n)] + mean
    out[0:400, :] = table_t[:, pl.ds(start, n)] - learn_rate * grad / jnp.sqrt(new)
    out[400:408, :] = jnp.broadcast_to(new, (8, n))


def join_kernel(parts_in, table_new, state_new):
    for q in range(4):
        table_new[:, q * LANE : (q + 1) * LANE] = parts_in[q, 0:400, :]
        state_new[:, q * LANE : (q + 1) * LANE] = parts_in[q, 400:401, :]


def call(kernel, outs, args, scalars=(), name=None, scratch=()):
    space = pl.BlockSpec(memory_space=pltpu.VMEM)
    return pl.pallas_call(
        kernel,
        out_shape=[
            (pltpu.VMEM if near else pltpu.HBM)(shape, kind)
            for shape, kind, near in outs
        ],
        in_specs=[pl.BlockSpec(memory_space=pltpu.SMEM)] * len(scalars) + [space] * len(args),
        out_specs=[space] * len(outs),
        scratch_shapes=list(scratch),
        compiler_params=pltpu.CompilerParams(vmem_limit_bytes=24 << 20),
        name=name,
    )(*scalars, *args)


def near(x):
    return pltpu.with_memory_space_constraint(x, pltpu.VMEM)


def far(x):
    return pltpu.with_memory_space_constraint(x, pltpu.HBM)


def exchange(x, axis, tiles):
    n = lax.axis_size(axis)
    x = x.reshape(n, 1, tiles * LANE)
    x = lax.all_to_all(x, axis, split_axis=0, concat_axis=0, tiled=True)
    return x.reshape(n * tiles, LANE)


def shift(x, by):
    n = lax.axis_size("rep")
    return lax.ppermute(x, "rep", [(i, (i + by) % n) for i in range(n)])


def on_device(
    entity_table,
    adagrad_state,
    head_owner,
    head_row,
    relation_ids,
    tail_owner,
    tail_row,
    neg_rows,
    relations,
):
    rep = lax.axis_index("rep").reshape(1).astype(jnp.int32)
    table_t = entity_table.T
    n = LANE

    def line(x):
        return x.reshape(1, n)

    send1, head_edge, tail_edge = call(
        ask_kernel,
        [((n * TILES1, n), f32, False), ((n, n), f32, False), ((n, n), f32, False)],
        (
            line(head_owner),
            line(head_row),
            line(relation_ids),
            line(tail_owner),
            line(tail_row),
            table_t,
        ),
        (rep, neg_rows),
        "ask",
    )
    recv1 = exchange(send1, "ent", TILES1)
    *pieces, same, same_t = call(
        ahead_kernel,
        [((4 * n, 512), bf16, True)] * PIECES
        + [((64, 512), bf16, True)] * PIECES
        + [((2 * n, 2 * n), bf16, False)] * 2,
        (table_t, relations, far(head_edge), far(tail_edge)),
        name="ahead",
    )
    rel_pieces = pieces[PIECES:]
    send2, rows = call(
        fetch_kernel,
        [((n * TILES2, n), f32, False), ((4 * n, 512), f32, True)],
        (near(recv1), *map(near, pieces)),
        name="fetch",
    )
    recv2 = exchange(send2, "ent", TILES2)
    negs = [recv1] + [shift(recv1, -j) for j in (1, 2, 3)]
    query_side, tail_side, rels, *owned = call(
        negatives_kernel,
        [((2 * n, 512), f32, False)] * 3 + [((n, 512), f32, i > 0) for i in range(4)],
        (near(recv1), near(rows), *map(far, rel_pieces), *map(near, negs)),
        name="negatives",
    )
    sums = [owned[0]] + [shift(owned[j], j) for j in (1, 2, 3)]
    send3, token = call(
        edge_kernel,
        [((n * TILES3, n), f32, False), ((8, n), f32, False)],
        (near(recv2), far(same), far(same_t), far(head_edge), far(sums[0]), *map(near, sums[1:])),
        name="edge",
    )
    recv3 = exchange(send3, "ent", TILES3)
    side, hot = call(
        place_kernel,
        [((6 * n, 512), f32, True), ((4 * n, 5 * n), bf16, True)],
        (recv1, far(token), far(query_side), far(tail_side), far(rels)),
        (rep, neg_rows),
        "place",
    )
    (grads,) = call(
        scatter_kernel,
        [((4 * TILES2 * GROUP, n), f32, False)],
        (near(recv3), near(hot), near(side)),
        name="scatter",
    )
    grads = lax.all_to_all(grads, "rep", split_axis=0, concat_axis=0, tiled=True)
    (fresh,) = call(
        update_kernel,
        [((408, n), f32, True)],
        (near(grads), table_t, adagrad_state.reshape(1, 512)),
        (rep,),
        "update",
        (pltpu.VMEM((TILES2 * GROUP, n), f32),),
    )
    fresh = lax.all_gather(fresh, "rep", axis=0, tiled=False)
    table_new, state_new = call(
        join_kernel, [((400, 512), f32, False), ((1, 512), f32, False)], (near(fresh),), name="join"
    )
    return (table_new.T, state_new.reshape(512))


def solution(mesh):
    placed = (
        P("ent", None),
        P("ent"),
        P(("ent", "rep"), None),
        P(("ent", "rep")),
        P(("ent", "rep")),
        P(("ent", "rep"), None),
        P(("ent", "rep")),
        P("ent"),
        P(),
    )
    return jax.shard_map(
        on_device, mesh=mesh, in_specs=placed, out_specs=(P("ent", None), P("ent")), check_vma=False
    )
```

```python
import math

import jax
import jax.numpy as jnp
from jax import lax
from jax.experimental import pallas as pl
from jax.experimental.pallas import tpu as pltpu
from jax.sharding import PartitionSpec as P

learn_rate = 0.1

LANE = 128
f32 = jnp.float32
bf16 = jnp.bfloat16
NN = (((1,), (0,)), ((), ()))
NT = (((1,), (1,)), ((), ()))
TN = (((0,), (0,)), ((), ()))
PIECES = 2
TILES1 = 2
TILES2 = 13
TILES3 = 15
GROUP = 32


def dot(a, b, dims):
    return lax.dot_general(a, b, dims, preferred_element_type=f32)


def parts(x, count):
    out = []
    for _ in range(count):
        head = x.astype(bf16)
        out.append(head)
        x = x - head.astype(f32)
    return out


def pick(onehot, pieces, dims):
    total = dot(onehot, pieces[0], dims)
    for piece in pieces[1:]:
        total = total + dot(onehot, piece, dims)
    return total


def dot3(a, b, dims):
    a0, a1 = parts(a, 2)
    b0, b1 = parts(b, 2)
    return dot(a0, b0, dims) + (dot(a0, b1, dims) + dot(a1, b0, dims))


def lanes(shape):
    return lax.broadcasted_iota(jnp.int32, shape, len(shape) - 1)


def cmul(a, b):
    return (a[0] * b[0] - a[1] * b[1], a[0] * b[1] + a[1] * b[0])


def conj(a):
    return (a[0], -a[1])


def sigmoid(x):
    return 1.0 / (1.0 + jnp.exp(-x))


def column(tile, lane):
    return jnp.sum(jnp.where(lanes(tile.shape) == lane, tile, 0.0), 1, keepdims=True)


def pack(ref, tiles, halves, base=0):
    n = halves[0].shape[0]
    at = lanes((n, LANE))
    tail = jnp.zeros((n, LANE), f32)
    for i, half in enumerate(halves):
        ref[pl.ds(base + i, n, stride=tiles), :] = half[:, :LANE]
        rest = half[:, LANE:]
        shift = (8 * i - 64) % LANE
        moved = pltpu.roll(rest, shift, 1) if shift else rest
        tail = jnp.where((at >= 8 * i) & (at < 8 * i + 8), moved, tail)
    for i in range(0, len(halves), 2):
        pair = halves[i][:, LANE:]
        if i + 1 < len(halves):
            pair = jnp.where(at < 64, pair, pltpu.roll(halves[i + 1][:, LANE:], 64, 1))
        ref[pl.ds(base + len(halves) + i // 2, n, stride=tiles), :] = pair
    ref[pl.ds(base + tiles - 1, n, stride=tiles), :] = tail


def unpack(ref, tiles, count, n):
    at = lanes((n, LANE))
    tail = ref[pl.ds(tiles - 1, n, stride=tiles), :]
    out = []
    for i in range(count):
        full = ref[pl.ds(i, n, stride=tiles), :]
        pair = ref[pl.ds(count + i // 2, n, stride=tiles), :]
        if i % 2:
            pair = pltpu.roll(pair, 64, 1)
        shift = (64 - 8 * i) % LANE
        moved = pltpu.roll(tail, shift, 1) if shift else tail
        rest = jnp.where(at < 64, pair, jnp.where(at < 72, moved, 0.0))
        out.append(jnp.concatenate([full, rest], 1))
    return out


def ask_kernel(
    rep, neg_rows, head_owner, head_row, rel, tail_owner, tail_row, table_t,
    send, head_edge, tail_edge, block, done,
):
    n = LANE
    neg_at = neg_rows[rep[0]]
    copy = pltpu.make_async_copy(
        table_t.at[:, pl.ds(pl.multiple_of(neg_at // n * n, n), n)], block, done
    )
    copy.start()
    sub = lax.broadcasted_iota(jnp.int32, (n, n), 0)
    lane = lanes((n, n))

    def wide(x):
        return jnp.broadcast_to(x, (n, x.shape[1]))

    head_owner, head_row, rel, tail_owner, tail_row = (
        wide(ref[...].astype(f32)) for ref in (head_owner, head_row, rel, tail_owner, tail_row)
    )
    owner_id = sub.astype(f32)
    columns = []

    def slots(owner, named):
        owner_c = owner.T
        rank = jnp.sum(jnp.where((owner == owner_c) & (sub < lane), 1.0, 0.0), 0, keepdims=True)
        edges = []
        for s in range(2):
            here = (owner == owner_id) & (wide(rank) == float(s))
            columns.append(jnp.sum(jnp.where(here, named + 1.0, 0.0), 1, keepdims=True) - 1.0)
            columns.append(jnp.sum(jnp.where(here, rel, 0.0), 1, keepdims=True))
            edges.append(
                jnp.sum(jnp.where(here, lane.astype(f32) + 1.0, 0.0), 1, keepdims=True) - 1.0
            )
        return jnp.where(lane == 0, edges[0], jnp.where(lane == 1, edges[1], -1.0))

    head_edge[...] = slots(head_owner, head_row)
    tail_edge[...] = slots(tail_owner, tail_row)

    copy.wait()
    pad = jnp.zeros((56, n), f32)
    line = []
    for i in range(2):
        half = jnp.concatenate([block[200 * i : 200 * i + 200, :], pad], 0).T
        picked = lax.broadcasted_iota(jnp.int32, (n, 256), 0) == neg_at % n
        line.append(jnp.sum(jnp.where(picked, half, 0.0), 0, keepdims=True))
    even = sub % 2 == 0
    send[pl.ds(0, n, stride=TILES1), :] = jnp.where(even, wide(line[0][:, :n]), wide(line[1][:, :n]))
    tile = jnp.where(even, wide(line[0][:, n:]), wide(line[1][:, n:]))
    for j, col in enumerate(columns):
        tile = jnp.where(lane == 72 + j, col, tile)
    send[pl.ds(1, n, stride=TILES1), :] = tile


def ahead_kernel(table_t, relations, head_edge, tail_edge, *outs):
    pad = jnp.zeros((56, 512), f32)
    whole = jnp.concatenate([table_t[0:200, :], pad, table_t[200:400, :], pad], 0).T
    for ref, piece in zip(outs[:PIECES], parts(whole, PIECES), strict=True):
        ref[...] = piece
    pad = jnp.zeros((64, 56), f32)
    whole = jnp.concatenate([relations[:, :200], pad, relations[:, 200:], pad], 1)
    for ref, piece in zip(outs[PIECES : 2 * PIECES], parts(whole, PIECES), strict=True):
        ref[...] = piece
    same, same_t = outs[2 * PIECES :]

    def stack(ref, by_rows):
        if by_rows:
            turned = ref[...].T
            return jnp.concatenate([turned[0:1, :], turned[1:2, :]], 1)
        return jnp.concatenate([ref[:, 0:1], ref[:, 1:2]], 0)

    for ref, one, other in ((same, head_edge, tail_edge), (same_t, tail_edge, head_edge)):
        col, row = stack(one, False), stack(other, True)
        ref[...] = jnp.where((col == row) & (col >= 0.0), 1.0, 0.0).astype(bf16)


def rel_vectors(tile, slots, pieces):
    ids = jnp.concatenate([column(tile, 72 + 2 * s + 1) for s in slots], 0)
    hot = jnp.where(lanes((ids.shape[0], 64)).astype(f32) == ids, 1.0, 0.0).astype(bf16)
    both = pick(hot, [p[...] for p in pieces], NN)
    return (both[:, :256], both[:, 256:])


def split(x):
    return (x[:, :256], x[:, 256:])


def fetch_kernel(recv, *refs):
    n = LANE
    table, rel = refs[:PIECES], refs[PIECES : 2 * PIECES]
    send, rows = refs[2 * PIECES :]
    tile = recv[pl.ds(1, n, stride=TILES1), :]
    halves = []
    for side in range(2):
        slots = (2 * side, 2 * side + 1)
        at = jnp.concatenate([column(tile, 72 + 2 * s) for s in slots], 0)
        hot = jnp.where(lanes((2 * n, 512)).astype(f32) == at, 1.0, 0.0).astype(bf16)
        vec = split(pick(hot, [p[...] for p in table], NN))
        if side == 0:
            vec = cmul(vec, rel_vectors(tile, slots, rel))
        for i in range(2):
            halves += [v[i * n : (i + 1) * n, :] for v in vec]
        for i in range(2):
            rows[2 * n * side : 2 * n * (side + 1), i * 256 : (i + 1) * 256] = vec[i]
    pack(send, TILES2, halves)


def join_rows_kernel(*refs):
    *ins, out = refs
    for i, ref in enumerate(ins):
        out[i * ref.shape[0] : (i + 1) * ref.shape[0], :] = ref[...]


def negatives_kernel(odd, recv, rows, *refs):
    n = LANE
    rel = refs[:PIECES]
    mine, other, query_side, tail_side, rels, keep, give = refs[PIECES:]
    tile = recv[pl.ds(1, n, stride=TILES1), :]
    mask = lanes((n, LANE)) < 72

    def half(ref, base):
        low = ref[pl.ds(base, n, stride=TILES1), :]
        high = jnp.where(mask, ref[pl.ds(base + 1, n, stride=TILES1), :], 0.0)
        return jnp.concatenate([low, high], 1)

    flip = odd[0] > 0
    own, got = (
        jnp.concatenate([half(ref, TILES1 * n * j) for j in range(4)], 0) for ref in (mine, other)
    )
    negs = jnp.concatenate([jnp.where(flip, got, own), jnp.where(flip, own, got)], 1)
    weight = 1.0 / math.sqrt(512.0)
    total = None
    for side in range(2):
        slots = (2 * side, 2 * side + 1)
        x = rows[2 * n * side : 2 * n * (side + 1), :]
        rv = rel_vectors(tile, slots, rel)
        if side:
            x = jnp.concatenate(cmul(conj(rv), split(x)), 1)
        valid = jnp.concatenate([column(tile, 72 + 2 * s) for s in slots], 0)
        scores = dot3(x, negs, NT)
        coef = jnp.where(valid >= 0.0, sigmoid(scores) * weight, 0.0)
        back = dot3(coef, negs, NN)
        if side:
            tail_side[...] = jnp.concatenate(cmul(split(back), rv), 1)
        else:
            query_side[...] = back
            rels[...] = jnp.concatenate(rv, 1)
        grad = dot3(coef, x, TN)
        total = grad if total is None else total + grad
    re, im = split(total)
    keep[...] = jnp.where(flip, im, re)
    give[...] = jnp.where(flip, re, im)


def fold_kernel(keep, got, *outs):
    for i, ref in enumerate(outs):
        at = pl.ds(i * LANE, LANE)
        ref[...] = keep[at, :] + got[at, :]


def edge_kernel(recv, same, same_t, head_edge, sum0, sum1, sum2, sum3, send, token):
    n = LANE
    halves = unpack(recv, TILES2, 8, n)
    head_at = jnp.concatenate([head_edge[:, 0:1], head_edge[:, 1:2]], 0)
    query, tails = (
        jnp.concatenate(
            [jnp.concatenate(halves[i : i + 2], 1), jnp.concatenate(halves[i + 2 : i + 4], 1)], 0
        )
        for i in (0, 4)
    )
    met = pick(same[...], parts(tails, PIECES), NN)
    pos = jnp.sum(query * met, 1, keepdims=True)
    coef = jnp.where(head_at >= 0.0, -sigmoid(-pos), 0.0)
    to_head = coef * met
    to_tail = pick(same_t[...], parts(coef * query, PIECES), NN)
    neg = sum0[...] + sum1[...] + (sum2[...] + sum3[...])
    out = []
    for block in (to_head[:n], to_head[n:], to_tail[:n], to_tail[n:]):
        out += split(block)
    pack(send, TILES3, out + [neg])
    token[...] = neg[0:8, 0:128]


def place_kernel(rep, neg_rows, asks, token, *refs):
    n = LANE
    *sides, side, hot = refs
    for i, source in enumerate(sides):
        side[i * 2 * n : (i + 1) * 2 * n, :] = source[...]
    turned = asks[pl.ds(1, n, stride=TILES1), :].T
    sub = lax.broadcasted_iota(jnp.int32, (512, n), 0)
    for s in range(4):
        at = turned[72 + 2 * s : 73 + 2 * s, :]
        hot[:, s * n : (s + 1) * n] = jnp.where(sub.astype(f32) == at, 1.0, 0.0).astype(bf16)
    hot[:, 4 * n :] = jnp.where(sub == neg_rows[rep[0]], 1.0, 0.0).astype(bf16)


def scatter_kernel(recv, hot, side, out):
    n = LANE
    halves = unpack(recv, TILES3, 9, n)
    even = lax.broadcasted_iota(jnp.int32, (n, 256), 0) % 2 == 0
    halves = halves[:8] + [jnp.where(even, halves[8], 0.0), jnp.where(even, 0.0, halves[8])]
    blocks = [jnp.concatenate(halves[i : i + 2], 1) for i in range(0, 10, 2)]
    head = split(jnp.concatenate(blocks[0:2], 0) + side[0 : 2 * n, :])
    head = jnp.concatenate(cmul(head, conj(split(side[4 * n :, :]))), 1)
    tail = jnp.concatenate(blocks[2:4], 0) + side[2 * n : 4 * n, :]
    grad = jnp.concatenate([head, tail, blocks[4]], 0)
    total = pick(hot[...], parts(grad, PIECES), NN)
    for q in range(4):
        groups = []
        for g in range(4):
            start = q * n + g * GROUP
            groups += split(total[start : start + GROUP, :])
        pack(out, TILES2, groups, q * TILES2 * GROUP)


def update_kernel(rep, grads, table_t, state, out, sums):
    n = LANE
    rows = TILES2 * GROUP
    sums[...] = (
        grads[0:rows, :] + grads[rows : 2 * rows, :]
        + (grads[2 * rows : 3 * rows, :] + grads[3 * rows :, :])
    )
    halves = unpack(sums, TILES2, 8, GROUP)
    grad = jnp.concatenate(
        [jnp.concatenate(halves[i::2], 0).T[0:200, :] for i in range(2)], 0
    )
    start = pl.multiple_of(rep[0] * n, n)
    mean = jnp.sum(grad * grad, 0, keepdims=True) * (1.0 / 400.0)
    new = state[:, pl.ds(start, n)] + mean
    out[0:400, :] = table_t[:, pl.ds(start, n)] - learn_rate * grad / jnp.sqrt(new)
    out[400:408, :] = jnp.broadcast_to(new, (8, n))


def join_kernel(parts_in, table_new, state_new):
    for q in range(4):
        table_new[:, q * LANE : (q + 1) * LANE] = parts_in[q, 0:400, :]
        state_new[:, q * LANE : (q + 1) * LANE] = parts_in[q, 400:401, :]


def call(kernel, outs, args, scalars=(), name=None, scratch=(), whole=0):
    space = pl.BlockSpec(memory_space=pltpu.VMEM)
    return pl.pallas_call(
        kernel,
        out_shape=[
            (pltpu.VMEM if near else pltpu.HBM)(shape, kind)
            for shape, kind, near in outs
        ],
        in_specs=[pl.BlockSpec(memory_space=pltpu.SMEM)] * len(scalars)
        + [space] * (len(args) - whole)
        + [pl.BlockSpec(memory_space=pltpu.HBM)] * whole,
        out_specs=[space] * len(outs),
        scratch_shapes=list(scratch),
        compiler_params=pltpu.CompilerParams(vmem_limit_bytes=24 << 20),
        name=name,
    )(*scalars, *args)


def near(x):
    return pltpu.with_memory_space_constraint(x, pltpu.VMEM)


def far(x):
    return pltpu.with_memory_space_constraint(x, pltpu.HBM)


def exchange(x, axis, tiles):
    n = lax.axis_size(axis)
    x = x.reshape(n, 1, tiles * LANE)
    x = lax.all_to_all(x, axis, split_axis=0, concat_axis=0, tiled=True)
    return x.reshape(n * tiles, LANE)


def shift(x, by):
    n = lax.axis_size("rep")
    return lax.ppermute(x, "rep", [(i, (i + by) % n) for i in range(n)])


def swap_cores(x):
    return lax.ppermute(x, "ent", [(i, i ^ 1) for i in range(lax.axis_size("ent"))])


def on_device(
    entity_table,
    adagrad_state,
    head_owner,
    head_row,
    relation_ids,
    tail_owner,
    tail_row,
    neg_rows,
    relations,
):
    rep = lax.axis_index("rep").reshape(1).astype(jnp.int32)
    odd = (lax.axis_index("ent") & 1).reshape(1).astype(jnp.int32)
    table_t = entity_table.T
    neg_rows = far(neg_rows)
    n = LANE

    def line(x):
        return far(x.reshape(1, n))

    send1, head_edge, tail_edge = call(
        ask_kernel,
        [((n * TILES1, n), f32, False), ((n, n), f32, False), ((n, n), f32, False)],
        (
            line(head_owner),
            line(head_row),
            line(relation_ids),
            line(tail_owner),
            line(tail_row),
            far(table_t),
        ),
        (rep, neg_rows),
        "ask",
        (pltpu.VMEM((400, n), f32), pltpu.SemaphoreType.DMA),
        1,
    )
    recv1 = exchange(send1, "ent", TILES1)
    *pieces, same, same_t = call(
        ahead_kernel,
        [((4 * n, 512), bf16, True)] * PIECES
        + [((64, 512), bf16, True)] * PIECES
        + [((2 * n, 2 * n), bf16, False)] * 2,
        (table_t, relations, far(head_edge), far(tail_edge)),
        name="ahead",
    )
    rel_pieces = pieces[PIECES:]
    send2, rows = call(
        fetch_kernel,
        [((n * TILES2, n), f32, False), ((4 * n, 512), f32, True)],
        (near(recv1), *map(near, pieces)),
        name="fetch",
    )
    recv2 = exchange(send2, "ent", TILES2)
    mine = [recv1] + [shift(recv1, -j) for j in (1, 2, 3)]
    (mine,) = call(
        join_rows_kernel, [((4 * TILES1 * n, n), f32, True)], list(map(near, mine)), name="join_rows"
    )
    other = swap_cores(mine)
    query_side, tail_side, rels, keep, give = call(
        negatives_kernel,
        [((2 * n, 512), f32, False)] * 3 + [((4 * n, 256), f32, True)] * 2,
        (near(recv1), near(rows), *map(far, rel_pieces), near(mine), near(other)),
        (odd,),
        "negatives",
    )
    owned = call(
        fold_kernel,
        [((n, 256), f32, i > 0) for i in range(4)],
        (near(keep), near(swap_cores(give))),
        name="fold",
    )
    sums = [owned[0]] + [shift(owned[j], j) for j in (1, 2, 3)]
    send3, token = call(
        edge_kernel,
        [((n * TILES3, n), f32, False), ((8, n), f32, False)],
        (near(recv2), far(same), far(same_t), far(head_edge), far(sums[0]), *map(near, sums[1:])),
        name="edge",
    )
    recv3 = exchange(send3, "ent", TILES3)
    side, hot = call(
        place_kernel,
        [((6 * n, 512), f32, False), ((4 * n, 5 * n), bf16, True)],
        (recv1, far(token), far(query_side), far(tail_side), far(rels)),
        (rep, neg_rows),
        "place",
    )
    (grads,) = call(
        scatter_kernel,
        [((4 * TILES2 * GROUP, n), f32, False)],
        (near(recv3), near(hot), far(side)),
        name="scatter",
    )
    grads = lax.all_to_all(grads, "rep", split_axis=0, concat_axis=0, tiled=True)
    (fresh,) = call(
        update_kernel,
        [((408, n), f32, True)],
        (near(grads), table_t, adagrad_state.reshape(1, 512)),
        (rep,),
        "update",
        (pltpu.VMEM((TILES2 * GROUP, n), f32),),
    )
    fresh = lax.all_gather(fresh, "rep", axis=0, tiled=False)
    table_new, state_new = call(
        join_kernel, [((400, 512), f32, False), ((1, 512), f32, False)], (near(fresh),), name="join"
    )
    return (table_new.T, state_new.reshape(512))


def solution(mesh):
    placed = (
        P("ent", None),
        P("ent"),
        P(("ent", "rep"), None),
        P(("ent", "rep")),
        P(("ent", "rep")),
        P(("ent", "rep"), None),
        P(("ent", "rep")),
        P("ent"),
        P(),
    )
    return jax.shard_map(
        on_device, mesh=mesh, in_specs=placed, out_specs=(P("ent", None), P("ent")), check_vma=False
    )
```

```python
import math

import jax
import jax.numpy as jnp
from jax import lax
from jax.experimental import pallas as pl
from jax.experimental.pallas import tpu as pltpu
from jax.sharding import PartitionSpec as P

learn_rate = 0.1

LANE = 128
f32 = jnp.float32
bf16 = jnp.bfloat16
NN = (((1,), (0,)), ((), ()))
NT = (((1,), (1,)), ((), ()))
TN = (((0,), (0,)), ((), ()))
PIECES = 2
TILES1 = 2
TILES2 = 13
TILES3 = 15
GROUP = 32


def dot(a, b, dims):
    return lax.dot_general(a, b, dims, preferred_element_type=f32)


def parts(x, count):
    out = []
    for _ in range(count):
        head = x.astype(bf16)
        out.append(head)
        x = x - head.astype(f32)
    return out


def pick(onehot, pieces, dims):
    total = dot(onehot, pieces[0], dims)
    for piece in pieces[1:]:
        total = total + dot(onehot, piece, dims)
    return total


def dot3(a, b, dims):
    a0, a1 = parts(a, 2)
    b0, b1 = parts(b, 2)
    return dot(a0, b0, dims) + (dot(a0, b1, dims) + dot(a1, b0, dims))


def lanes(shape):
    return lax.broadcasted_iota(jnp.int32, shape, len(shape) - 1)


def cmul(a, b):
    return (a[0] * b[0] - a[1] * b[1], a[0] * b[1] + a[1] * b[0])


def conj(a):
    return (a[0], -a[1])


def sigmoid(x):
    return 1.0 / (1.0 + jnp.exp(-x))


def column(tile, lane):
    return jnp.sum(jnp.where(lanes(tile.shape) == lane, tile, 0.0), 1, keepdims=True)


def pack(ref, tiles, halves, base=0):
    n = halves[0].shape[0]
    at = lanes((n, LANE))
    tail = jnp.zeros((n, LANE), f32)
    for i, half in enumerate(halves):
        ref[pl.ds(base + i, n, stride=tiles), :] = half[:, :LANE]
        rest = half[:, LANE:]
        shift = (8 * i - 64) % LANE
        moved = pltpu.roll(rest, shift, 1) if shift else rest
        tail = jnp.where((at >= 8 * i) & (at < 8 * i + 8), moved, tail)
    for i in range(0, len(halves), 2):
        pair = halves[i][:, LANE:]
        if i + 1 < len(halves):
            pair = jnp.where(at < 64, pair, pltpu.roll(halves[i + 1][:, LANE:], 64, 1))
        ref[pl.ds(base + len(halves) + i // 2, n, stride=tiles), :] = pair
    ref[pl.ds(base + tiles - 1, n, stride=tiles), :] = tail


def unpack(ref, tiles, count, n):
    at = lanes((n, LANE))
    tail = ref[pl.ds(tiles - 1, n, stride=tiles), :]
    out = []
    for i in range(count):
        full = ref[pl.ds(i, n, stride=tiles), :]
        pair = ref[pl.ds(count + i // 2, n, stride=tiles), :]
        if i % 2:
            pair = pltpu.roll(pair, 64, 1)
        shift = (64 - 8 * i) % LANE
        moved = pltpu.roll(tail, shift, 1) if shift else tail
        rest = jnp.where(at < 64, pair, jnp.where(at < 72, moved, 0.0))
        out.append(jnp.concatenate([full, rest], 1))
    return out


def ask_kernel(
    rep, neg_rows, head_owner, head_row, rel, tail_owner, tail_row, table_t,
    send, head_edge, tail_edge, block, done,
):
    n = LANE
    neg_at = neg_rows[rep[0]]
    copy = pltpu.make_async_copy(
        table_t.at[:, pl.ds(pl.multiple_of(neg_at // n * n, n), n)], block, done
    )
    copy.start()
    sub = lax.broadcasted_iota(jnp.int32, (n, n), 0)
    lane = lanes((n, n))

    def wide(x):
        return jnp.broadcast_to(x, (n, x.shape[1]))

    head_owner, head_row, rel, tail_owner, tail_row = (
        wide(ref[...].astype(f32)) for ref in (head_owner, head_row, rel, tail_owner, tail_row)
    )
    owner_id = sub.astype(f32)
    columns = []

    def slots(owner, named):
        owner_c = owner.T
        rank = jnp.sum(jnp.where((owner == owner_c) & (sub < lane), 1.0, 0.0), 0, keepdims=True)
        edges = []
        for s in range(2):
            here = (owner == owner_id) & (wide(rank) == float(s))
            columns.append(jnp.sum(jnp.where(here, named + 1.0, 0.0), 1, keepdims=True) - 1.0)
            columns.append(jnp.sum(jnp.where(here, rel, 0.0), 1, keepdims=True))
            edges.append(
                jnp.sum(jnp.where(here, lane.astype(f32) + 1.0, 0.0), 1, keepdims=True) - 1.0
            )
        return jnp.where(lane == 0, edges[0], jnp.where(lane == 1, edges[1], -1.0))

    head_edge[...] = slots(head_owner, head_row)
    tail_edge[...] = slots(tail_owner, tail_row)

    copy.wait()
    pad = jnp.zeros((56, n), f32)
    line = []
    for i in range(2):
        half = jnp.concatenate([block[200 * i : 200 * i + 200, :], pad], 0).T
        picked = lax.broadcasted_iota(jnp.int32, (n, 256), 0) == neg_at % n
        line.append(jnp.sum(jnp.where(picked, half, 0.0), 0, keepdims=True))
    even = sub % 2 == 0
    send[pl.ds(0, n, stride=TILES1), :] = jnp.where(even, wide(line[0][:, :n]), wide(line[1][:, :n]))
    tile = jnp.where(even, wide(line[0][:, n:]), wide(line[1][:, n:]))
    for j, col in enumerate(columns):
        tile = jnp.where(lane == 72 + j, col, tile)
    send[pl.ds(1, n, stride=TILES1), :] = tile


def ahead_kernel(table_t, relations, head_edge, tail_edge, *outs):
    pad = jnp.zeros((56, 512), f32)
    whole = jnp.concatenate([table_t[0:200, :], pad, table_t[200:400, :], pad], 0).T
    for ref, piece in zip(outs[:PIECES], parts(whole, PIECES), strict=True):
        ref[...] = piece
    pad = jnp.zeros((64, 56), f32)
    whole = jnp.concatenate([relations[:, :200], pad, relations[:, 200:], pad], 1)
    for ref, piece in zip(outs[PIECES : 2 * PIECES], parts(whole, PIECES), strict=True):
        ref[...] = piece
    same, same_t = outs[2 * PIECES :]

    def stack(ref, by_rows):
        if by_rows:
            turned = ref[...].T
            return jnp.concatenate([turned[0:1, :], turned[1:2, :]], 1)
        return jnp.concatenate([ref[:, 0:1], ref[:, 1:2]], 0)

    for ref, one, other in ((same, head_edge, tail_edge), (same_t, tail_edge, head_edge)):
        col, row = stack(one, False), stack(other, True)
        ref[...] = jnp.where((col == row) & (col >= 0.0), 1.0, 0.0).astype(bf16)


def rel_vectors(tile, slots, pieces):
    ids = jnp.concatenate([column(tile, 72 + 2 * s + 1) for s in slots], 0)
    hot = jnp.where(lanes((ids.shape[0], 64)).astype(f32) == ids, 1.0, 0.0).astype(bf16)
    both = pick(hot, [p[...] for p in pieces], NN)
    return (both[:, :256], both[:, 256:])


def split(x):
    return (x[:, :256], x[:, 256:])


def fetch_kernel(recv, *refs):
    n = LANE
    table, rel = refs[:PIECES], refs[PIECES : 2 * PIECES]
    send, rows, negs = refs[2 * PIECES :]
    negs[...] = recv[...]
    tile = recv[pl.ds(1, n, stride=TILES1), :]
    halves = []
    for side in range(2):
        slots = (2 * side, 2 * side + 1)
        at = jnp.concatenate([column(tile, 72 + 2 * s) for s in slots], 0)
        hot = jnp.where(lanes((2 * n, 512)).astype(f32) == at, 1.0, 0.0).astype(bf16)
        vec = split(pick(hot, [p[...] for p in table], NN))
        if side == 0:
            vec = cmul(vec, rel_vectors(tile, slots, rel))
        for i in range(2):
            halves += [v[i * n : (i + 1) * n, :] for v in vec]
        for i in range(2):
            rows[2 * n * side : 2 * n * (side + 1), i * 256 : (i + 1) * 256] = vec[i]
    pack(send, TILES2, halves)


def negatives_kernel(odd, recv, rows, *refs):
    n = LANE
    rel = refs[:PIECES]
    mine, other, query_side, tail_side, rels, keep, give = refs[PIECES:]
    tile = recv[pl.ds(1, n, stride=TILES1), :]
    mask = lanes((n, LANE)) < 72

    def half(ref, base):
        low = ref[pl.ds(base, n, stride=TILES1), :]
        high = jnp.where(mask, ref[pl.ds(base + 1, n, stride=TILES1), :], 0.0)
        return jnp.concatenate([low, high], 1)

    flip = odd[0] > 0
    own, got = (
        jnp.concatenate([half(ref, TILES1 * n * j) for j in range(4)], 0) for ref in (mine, other)
    )
    negs = jnp.concatenate([jnp.where(flip, got, own), jnp.where(flip, own, got)], 1)
    weight = 1.0 / math.sqrt(512.0)
    total = None
    for side in range(2):
        slots = (2 * side, 2 * side + 1)
        x = rows[2 * n * side : 2 * n * (side + 1), :]
        rv = rel_vectors(tile, slots, rel)
        if side:
            x = jnp.concatenate(cmul(conj(rv), split(x)), 1)
        valid = jnp.concatenate([column(tile, 72 + 2 * s) for s in slots], 0)
        scores = dot3(x, negs, NT)
        coef = jnp.where(valid >= 0.0, sigmoid(scores) * weight, 0.0)
        back = dot3(coef, negs, NN)
        if side:
            tail_side[...] = jnp.concatenate(cmul(split(back), rv), 1)
        else:
            query_side[...] = back
            rels[...] = jnp.concatenate(rv, 1)
        grad = dot3(coef, x, TN)
        total = grad if total is None else total + grad
    re, im = split(total)
    keep[...] = jnp.where(flip, im, re)
    give[...] = jnp.where(flip, re, im)


def fold_kernel(rep, keep, got, *outs):
    for i, ref in enumerate(outs):
        at = pl.ds(pl.multiple_of((rep[0] + i) % 4 * LANE, LANE), LANE)
        ref[...] = keep[at, :] + got[at, :]


def edge_kernel(recv, same, same_t, head_edge, sum0, sum1, sum2, sum3, send, token):
    n = LANE
    halves = unpack(recv, TILES2, 8, n)
    head_at = jnp.concatenate([head_edge[:, 0:1], head_edge[:, 1:2]], 0)
    query, tails = (
        jnp.concatenate(
            [jnp.concatenate(halves[i : i + 2], 1), jnp.concatenate(halves[i + 2 : i + 4], 1)], 0
        )
        for i in (0, 4)
    )
    met = pick(same[...], parts(tails, PIECES), NN)
    pos = jnp.sum(query * met, 1, keepdims=True)
    coef = jnp.where(head_at >= 0.0, -sigmoid(-pos), 0.0)
    to_head = coef * met
    to_tail = pick(same_t[...], parts(coef * query, PIECES), NN)
    neg = sum0[...] + sum1[...] + (sum2[...] + sum3[...])
    out = []
    for block in (to_head[:n], to_head[n:], to_tail[:n], to_tail[n:]):
        out += split(block)
    pack(send, TILES3, out + [neg])
    token[...] = neg[0:8, 0:128]


def carry_kernel(token, *refs):
    *sides, side = refs
    for i, source in enumerate(sides):
        side[i * 2 * LANE : (i + 1) * 2 * LANE, :] = source[...]


def place_kernel(rep, neg_rows, asks, token, hot):
    n = LANE
    turned = asks[pl.ds(1, n, stride=TILES1), :].T
    sub = lax.broadcasted_iota(jnp.int32, (512, n), 0)
    for s in range(4):
        at = turned[72 + 2 * s : 73 + 2 * s, :]
        hot[:, s * n : (s + 1) * n] = jnp.where(sub.astype(f32) == at, 1.0, 0.0).astype(bf16)
    hot[:, 4 * n :] = jnp.where(sub == neg_rows[rep[0]], 1.0, 0.0).astype(bf16)


def scatter_kernel(recv, hot, side, out):
    n = LANE
    halves = unpack(recv, TILES3, 9, n)
    even = lax.broadcasted_iota(jnp.int32, (n, 256), 0) % 2 == 0
    halves = halves[:8] + [jnp.where(even, halves[8], 0.0), jnp.where(even, 0.0, halves[8])]
    blocks = [jnp.concatenate(halves[i : i + 2], 1) for i in range(0, 10, 2)]
    head = split(jnp.concatenate(blocks[0:2], 0) + side[0 : 2 * n, :])
    head = jnp.concatenate(cmul(head, conj(split(side[4 * n :, :]))), 1)
    tail = jnp.concatenate(blocks[2:4], 0) + side[2 * n : 4 * n, :]
    grad = jnp.concatenate([head, tail, blocks[4]], 0)
    total = pick(hot[...], parts(grad, PIECES), NN)
    for q in range(4):
        groups = []
        for g in range(4):
            start = q * n + g * GROUP
            groups += split(total[start : start + GROUP, :])
        pack(out, TILES2, groups, q * TILES2 * GROUP)


def update_kernel(rep, grads, state, table_t, out, sums, block, done):
    n = LANE
    start = pl.multiple_of(rep[0] * n, n)
    copy = pltpu.make_async_copy(table_t.at[:, pl.ds(start, n)], block, done)
    copy.start()
    rows = TILES2 * GROUP
    sums[...] = (
        grads[0:rows, :] + grads[rows : 2 * rows, :]
        + (grads[2 * rows : 3 * rows, :] + grads[3 * rows :, :])
    )
    halves = unpack(sums, TILES2, 8, GROUP)
    grad = jnp.concatenate(
        [jnp.concatenate(halves[i::2], 0).T[0:200, :] for i in range(2)], 0
    )
    mean = jnp.sum(grad * grad, 0, keepdims=True) * (1.0 / 400.0)
    new = state[:, pl.ds(start, n)] + mean
    copy.wait()
    out[0:400, :] = block[...] - learn_rate * grad / jnp.sqrt(new)
    out[400:408, :] = jnp.broadcast_to(new, (8, n))


def join_kernel(parts_in, table_new, state_new, done):
    copies = []
    for q in range(4):
        at = pl.ds(q * LANE, LANE)
        copies.append((parts_in.at[q, pl.ds(0, 400), :], table_new.at[:, at]))
    copies = [pltpu.make_async_copy(a, b, done.at[q]) for q, (a, b) in enumerate(copies)]
    for copy in copies:
        copy.start()
    for q in range(4):
        state_new[:, q * LANE : (q + 1) * LANE] = parts_in[q, 400:401, :]
    for copy in copies:
        copy.wait()


def call(kernel, outs, args, scalars=(), name=None, scratch=(), whole=0, direct=0):
    space = pl.BlockSpec(memory_space=pltpu.VMEM)
    return pl.pallas_call(
        kernel,
        out_shape=[
            (pltpu.VMEM if near else pltpu.HBM)(shape, kind)
            for shape, kind, near in outs
        ],
        in_specs=[pl.BlockSpec(memory_space=pltpu.SMEM)] * len(scalars)
        + [space] * (len(args) - whole)
        + [pl.BlockSpec(memory_space=pltpu.HBM)] * whole,
        out_specs=[pl.BlockSpec(memory_space=pltpu.HBM)] * direct + [space] * (len(outs) - direct),
        scratch_shapes=list(scratch),
        compiler_params=pltpu.CompilerParams(vmem_limit_bytes=24 << 20),
        name=name,
    )(*scalars, *args)


def near(x):
    return pltpu.with_memory_space_constraint(x, pltpu.VMEM)


def far(x):
    return pltpu.with_memory_space_constraint(x, pltpu.HBM)


def exchange(x, axis, tiles):
    n = lax.axis_size(axis)
    x = x.reshape(n, 1, tiles * LANE)
    x = lax.all_to_all(x, axis, split_axis=0, concat_axis=0, tiled=True)
    return x.reshape(n * tiles, LANE)


def shift(x, by):
    n = lax.axis_size("rep")
    return lax.ppermute(x, "rep", [(i, (i + by) % n) for i in range(n)])


def swap_cores(x):
    return lax.ppermute(x, "ent", [(i, i ^ 1) for i in range(lax.axis_size("ent"))])


def on_device(
    entity_table,
    adagrad_state,
    head_owner,
    head_row,
    relation_ids,
    tail_owner,
    tail_row,
    neg_rows,
    relations,
):
    rep = lax.axis_index("rep").reshape(1).astype(jnp.int32)
    odd = (lax.axis_index("ent") & 1).reshape(1).astype(jnp.int32)
    table_t = entity_table.T
    neg_rows = far(neg_rows)
    n = LANE

    def line(x):
        return far(x.reshape(1, n))

    send1, head_edge, tail_edge = call(
        ask_kernel,
        [((n * TILES1, n), f32, False), ((n, n), f32, False), ((n, n), f32, False)],
        (
            line(head_owner),
            line(head_row),
            line(relation_ids),
            line(tail_owner),
            line(tail_row),
            far(table_t),
        ),
        (rep, neg_rows),
        "ask",
        (pltpu.VMEM((400, n), f32), pltpu.SemaphoreType.DMA),
        1,
    )
    recv1 = exchange(send1, "ent", TILES1)
    *pieces, same, same_t = call(
        ahead_kernel,
        [((4 * n, 512), bf16, True)] * PIECES
        + [((64, 512), bf16, True)] * PIECES
        + [((2 * n, 2 * n), bf16, False)] * 2,
        (table_t, relations, far(head_edge), far(tail_edge)),
        name="ahead",
    )
    rel_pieces = pieces[PIECES:]
    send2, rows, own_negs = call(
        fetch_kernel,
        [
            ((n * TILES2, n), f32, False),
            ((4 * n, 512), f32, True),
            ((n * TILES1, n), f32, True),
        ],
        (near(recv1), *map(near, pieces)),
        name="fetch",
    )
    recv2 = exchange(send2, "ent", TILES2)
    mine = lax.all_gather(own_negs, "rep", axis=0, tiled=True)
    other = swap_cores(mine)
    query_side, tail_side, rels, keep, give = call(
        negatives_kernel,
        [((2 * n, 512), f32, False)] * 3 + [((4 * n, 256), f32, True)] * 2,
        (near(recv1), near(rows), *map(far, rel_pieces), near(mine), near(other)),
        (odd,),
        "negatives",
    )
    owned = call(
        fold_kernel,
        [((n, 256), f32, i > 0) for i in range(4)],
        (near(keep), near(swap_cores(give))),
        (rep,),
        "fold",
    )
    sums = [owned[0]] + [shift(owned[j], j) for j in (1, 2, 3)]
    send3, token = call(
        edge_kernel,
        [((n * TILES3, n), f32, False), ((8, n), f32, False)],
        (near(recv2), far(same), far(same_t), far(head_edge), far(sums[0]), *map(near, sums[1:])),
        name="edge",
    )
    recv3 = exchange(send3, "ent", TILES3)
    token = far(token)
    (side,) = call(
        carry_kernel,
        [((6 * n, 512), f32, True)],
        (token, far(query_side), far(tail_side), far(rels)),
        name="carry",
    )
    (hot,) = call(
        place_kernel, [((4 * n, 5 * n), bf16, True)], (recv1, token), (rep, neg_rows), "place"
    )
    (grads,) = call(
        scatter_kernel,
        [((4 * TILES2 * GROUP, n), f32, False)],
        (near(recv3), near(hot), near(side)),
        name="scatter",
    )
    grads = lax.all_to_all(grads, "rep", split_axis=0, concat_axis=0, tiled=True)
    (fresh,) = call(
        update_kernel,
        [((408, n), f32, True)],
        (near(grads), adagrad_state.reshape(1, 512), far(table_t)),
        (rep,),
        "update",
        (
            pltpu.VMEM((TILES2 * GROUP, n), f32),
            pltpu.VMEM((400, n), f32),
            pltpu.SemaphoreType.DMA,
        ),
        1,
    )
    fresh = lax.all_gather(fresh, "rep", axis=0, tiled=False)
    table_new, state_new = call(
        join_kernel, [((400, 512), f32, False), ((1, 512), f32, False)], (near(fresh),), name="join",
        scratch=(pltpu.SemaphoreType.DMA((4,)),), direct=1,
    )
    return (table_new.T, state_new.reshape(512))


def solution(mesh):
    placed = (
        P("ent", None),
        P("ent"),
        P(("ent", "rep"), None),
        P(("ent", "rep")),
        P(("ent", "rep")),
        P(("ent", "rep"), None),
        P(("ent", "rep")),
        P("ent"),
        P(),
    )
    return jax.shard_map(
        on_device, mesh=mesh, in_specs=placed, out_specs=(P("ent", None), P("ent")), check_vma=False
    )
```

```python
import math

import jax
import jax.numpy as jnp
from jax import lax
from jax.experimental import pallas as pl
from jax.experimental.pallas import tpu as pltpu
from jax.sharding import PartitionSpec as P

learn_rate = 0.1

LANE = 128
f32 = jnp.float32
bf16 = jnp.bfloat16
NN = (((1,), (0,)), ((), ()))
NT = (((1,), (1,)), ((), ()))
TN = (((0,), (0,)), ((), ()))
PIECES = 2
TILES1 = 2
TILES2 = 13
TILES3 = 15
GROUP = 32


def dot(a, b, dims):
    return lax.dot_general(a, b, dims, preferred_element_type=f32)


def parts(x, count):
    out = []
    for _ in range(count):
        head = x.astype(bf16)
        out.append(head)
        x = x - head.astype(f32)
    return out


def pick(onehot, pieces, dims):
    total = dot(onehot, pieces[0], dims)
    for piece in pieces[1:]:
        total = total + dot(onehot, piece, dims)
    return total


def dot3(a, b, dims):
    a0, a1 = parts(a, 2)
    b0, b1 = parts(b, 2)
    return dot(a0, b0, dims) + (dot(a0, b1, dims) + dot(a1, b0, dims))


def lanes(shape):
    return lax.broadcasted_iota(jnp.int32, shape, len(shape) - 1)


def cmul(a, b):
    return (a[0] * b[0] - a[1] * b[1], a[0] * b[1] + a[1] * b[0])


def conj(a):
    return (a[0], -a[1])


def sigmoid(x):
    return 1.0 / (1.0 + jnp.exp(-x))


def column(tile, lane):
    return jnp.sum(jnp.where(lanes(tile.shape) == lane, tile, 0.0), 1, keepdims=True)


def pack(ref, tiles, halves, base=0):
    n = halves[0].shape[0]
    at = lanes((n, LANE))
    tail = jnp.zeros((n, LANE), f32)
    for i, half in enumerate(halves):
        ref[pl.ds(base + i, n, stride=tiles), :] = half[:, :LANE]
        rest = half[:, LANE:]
        shift = (8 * i - 64) % LANE
        moved = pltpu.roll(rest, shift, 1) if shift else rest
        tail = jnp.where((at >= 8 * i) & (at < 8 * i + 8), moved, tail)
    for i in range(0, len(halves), 2):
        pair = halves[i][:, LANE:]
        if i + 1 < len(halves):
            pair = jnp.where(at < 64, pair, pltpu.roll(halves[i + 1][:, LANE:], 64, 1))
        ref[pl.ds(base + len(halves) + i // 2, n, stride=tiles), :] = pair
    ref[pl.ds(base + tiles - 1, n, stride=tiles), :] = tail


def unpack(ref, tiles, count, n):
    at = lanes((n, LANE))
    tail = ref[pl.ds(tiles - 1, n, stride=tiles), :]
    out = []
    for i in range(count):
        full = ref[pl.ds(i, n, stride=tiles), :]
        pair = ref[pl.ds(count + i // 2, n, stride=tiles), :]
        if i % 2:
            pair = pltpu.roll(pair, 64, 1)
        shift = (64 - 8 * i) % LANE
        moved = pltpu.roll(tail, shift, 1) if shift else tail
        rest = jnp.where(at < 64, pair, jnp.where(at < 72, moved, 0.0))
        out.append(jnp.concatenate([full, rest], 1))
    return out


def ask_kernel(
    rep, neg_rows, head_owner, head_row, rel, tail_owner, tail_row, table_t,
    send, head_edge, tail_edge, block, done,
):
    n = LANE
    neg_at = neg_rows[rep[0]]
    copy = pltpu.make_async_copy(
        table_t.at[:, pl.ds(pl.multiple_of(neg_at // n * n, n), n)], block, done
    )
    copy.start()
    sub = lax.broadcasted_iota(jnp.int32, (n, n), 0)
    lane = lanes((n, n))

    def wide(x):
        return jnp.broadcast_to(x, (n, x.shape[1]))

    head_owner, head_row, rel, tail_owner, tail_row = (
        wide(ref[...].astype(f32)) for ref in (head_owner, head_row, rel, tail_owner, tail_row)
    )
    owner_id = sub.astype(f32)
    columns = []

    def slots(owner, named):
        owner_c = owner.T
        rank = jnp.sum(jnp.where((owner == owner_c) & (sub < lane), 1.0, 0.0), 0, keepdims=True)
        edges = []
        for s in range(2):
            here = (owner == owner_id) & (wide(rank) == float(s))
            columns.append(jnp.sum(jnp.where(here, named + 1.0, 0.0), 1, keepdims=True) - 1.0)
            columns.append(jnp.sum(jnp.where(here, rel, 0.0), 1, keepdims=True))
            edges.append(
                jnp.sum(jnp.where(here, lane.astype(f32) + 1.0, 0.0), 1, keepdims=True) - 1.0
            )
        return jnp.where(lane == 0, edges[0], jnp.where(lane == 1, edges[1], -1.0))

    head_edge[...] = slots(head_owner, head_row)
    tail_edge[...] = slots(tail_owner, tail_row)

    copy.wait()
    pad = jnp.zeros((56, n), f32)
    line = []
    for i in range(2):
        half = jnp.concatenate([block[200 * i : 200 * i + 200, :], pad], 0).T
        picked = lax.broadcasted_iota(jnp.int32, (n, 256), 0) == neg_at % n
        line.append(jnp.sum(jnp.where(picked, half, 0.0), 0, keepdims=True))
    even = sub % 2 == 0
    send[pl.ds(0, n, stride=TILES1), :] = jnp.where(even, wide(line[0][:, :n]), wide(line[1][:, :n]))
    tile = jnp.where(even, wide(line[0][:, n:]), wide(line[1][:, n:]))
    for j, col in enumerate(columns):
        tile = jnp.where(lane == 72 + j, col, tile)
    send[pl.ds(1, n, stride=TILES1), :] = tile


def ahead_kernel(table_t, relations, *outs):
    pad = jnp.zeros((56, 512), f32)
    whole = jnp.concatenate([table_t[0:200, :], pad, table_t[200:400, :], pad], 0).T
    for ref, piece in zip(outs[:PIECES], parts(whole, PIECES), strict=True):
        ref[...] = piece
    pad = jnp.zeros((64, 56), f32)
    whole = jnp.concatenate([relations[:, :200], pad, relations[:, 200:], pad], 1)
    for ref, piece in zip(outs[PIECES : 2 * PIECES], parts(whole, PIECES), strict=True):
        ref[...] = piece


def pair_kernel(head_edge, tail_edge, same):
    n = 2 * LANE

    def stack(ref, by_rows):
        if by_rows:
            turned = ref[...].T
            return jnp.concatenate([turned[0:1, :], turned[1:2, :]], 1)
        return jnp.concatenate([ref[:, 0:1], ref[:, 1:2]], 0)

    for i, (one, other) in enumerate(((head_edge, tail_edge), (tail_edge, head_edge))):
        col, row = stack(one, False), stack(other, True)
        same[i * n : (i + 1) * n, :] = jnp.where(
            (col == row) & (col >= 0.0), 1.0, 0.0
        ).astype(bf16)


def rel_vectors(tile, slots, pieces):
    ids = jnp.concatenate([column(tile, 72 + 2 * s + 1) for s in slots], 0)
    hot = jnp.where(lanes((ids.shape[0], 64)).astype(f32) == ids, 1.0, 0.0).astype(bf16)
    both = pick(hot, [p[...] for p in pieces], NN)
    return (both[:, :256], both[:, 256:])


def split(x):
    return (x[:, :256], x[:, 256:])


def fetch_kernel(recv, *refs):
    n = LANE
    table, rel = refs[:PIECES], refs[PIECES : 2 * PIECES]
    send, rows, negs = refs[2 * PIECES :]
    negs[...] = recv[...]
    tile = recv[pl.ds(1, n, stride=TILES1), :]
    halves = []
    for side in range(2):
        slots = (2 * side, 2 * side + 1)
        at = jnp.concatenate([column(tile, 72 + 2 * s) for s in slots], 0)
        hot = jnp.where(lanes((2 * n, 512)).astype(f32) == at, 1.0, 0.0).astype(bf16)
        vec = split(pick(hot, [p[...] for p in table], NN))
        if side == 0:
            vec = cmul(vec, rel_vectors(tile, slots, rel))
        for i in range(2):
            halves += [v[i * n : (i + 1) * n, :] for v in vec]
        for i in range(2):
            rows[2 * n * side : 2 * n * (side + 1), i * 256 : (i + 1) * 256] = vec[i]
    pack(send, TILES2, halves)


def negatives_kernel(odd, recv, rows, *refs):
    n = LANE
    rel = refs[:PIECES]
    mine, other, back, keep, give = refs[PIECES:]
    tile = recv[pl.ds(1, n, stride=TILES1), :]
    mask = lanes((n, LANE)) < 72

    def half(ref, base):
        low = ref[pl.ds(base, n, stride=TILES1), :]
        high = jnp.where(mask, ref[pl.ds(base + 1, n, stride=TILES1), :], 0.0)
        return jnp.concatenate([low, high], 1)

    flip = odd[0] > 0
    own, got = (
        jnp.concatenate([half(ref, TILES1 * n * j) for j in range(4)], 0) for ref in (mine, other)
    )
    negs = jnp.concatenate([jnp.where(flip, got, own), jnp.where(flip, own, got)], 1)
    probe = cmul(conj(rel_vectors(tile, (2, 3), rel)), split(rows[2 * n :, :]))
    x = jnp.concatenate([rows[0 : 2 * n, :], jnp.concatenate(probe, 1)], 0)
    valid = jnp.concatenate([column(tile, 72 + 2 * s) for s in range(4)], 0)
    coef = sigmoid(dot3(x, negs, NT)) * (1.0 / math.sqrt(512.0))
    coef = jnp.where(valid >= 0.0, coef, 0.0)
    back[...] = dot3(coef, negs, NN)
    total = dot3(coef, x, TN)
    re, im = split(total)
    keep[...] = jnp.where(flip, im, re)
    give[...] = jnp.where(flip, re, im)


def fold_kernel(rep, keep, got, *outs):
    for i, ref in enumerate(outs):
        at = pl.ds(pl.multiple_of((rep[0] + i) % 4 * LANE, LANE), LANE)
        ref[...] = keep[at, :] + got[at, :]


def edge_kernel(recv, same, sum0, sum1, sum2, sum3, send, token):
    n = LANE
    halves = unpack(recv, TILES2, 8, n)
    query, tails = (
        jnp.concatenate(
            [jnp.concatenate(halves[i : i + 2], 1), jnp.concatenate(halves[i + 2 : i + 4], 1)], 0
        )
        for i in (0, 4)
    )
    met = pick(same[0 : 2 * n, :], parts(tails, PIECES), NN)
    pos = jnp.sum(query * met, 1, keepdims=True)
    coef = -sigmoid(-pos)
    to_head = coef * met
    to_tail = pick(same[2 * n :, :], parts(coef * query, PIECES), NN)
    neg = sum0[...] + sum1[...] + (sum2[...] + sum3[...])
    out = []
    for block in (to_head[:n], to_head[n:], to_tail[:n], to_tail[n:]):
        out += split(block)
    pack(send, TILES3, out + [neg])
    token[...] = neg[0:8, 0:128]


def carry_kernel(token, asks, back, *refs):
    n = 2 * LANE
    *rel, side = refs
    tile = asks[pl.ds(1, LANE, stride=TILES1), :]
    side[0:n, :] = back[0:n, :]
    turned = cmul(split(back[n:, :]), rel_vectors(tile, (2, 3), rel))
    side[n : 2 * n, :] = jnp.concatenate(turned, 1)
    side[2 * n :, :] = jnp.concatenate(rel_vectors(tile, (0, 1), rel), 1)


def place_kernel(rep, neg_rows, asks, token, hot):
    n = LANE
    turned = asks[pl.ds(1, n, stride=TILES1), :].T
    sub = lax.broadcasted_iota(jnp.int32, (512, n), 0)
    for s in range(4):
        at = turned[72 + 2 * s : 73 + 2 * s, :]
        hot[:, s * n : (s + 1) * n] = jnp.where(sub.astype(f32) == at, 1.0, 0.0).astype(bf16)
    hot[:, 4 * n :] = jnp.where(sub == neg_rows[rep[0]], 1.0, 0.0).astype(bf16)


def scatter_kernel(recv, hot, side, out):
    n = LANE
    halves = unpack(recv, TILES3, 9, n)
    even = lax.broadcasted_iota(jnp.int32, (n, 256), 0) % 2 == 0
    halves = halves[:8] + [jnp.where(even, halves[8], 0.0), jnp.where(even, 0.0, halves[8])]
    blocks = [jnp.concatenate(halves[i : i + 2], 1) for i in range(0, 10, 2)]
    head = split(jnp.concatenate(blocks[0:2], 0) + side[0 : 2 * n, :])
    head = jnp.concatenate(cmul(head, conj(split(side[4 * n :, :]))), 1)
    tail = jnp.concatenate(blocks[2:4], 0) + side[2 * n : 4 * n, :]
    grad = jnp.concatenate([head, tail, blocks[4]], 0)
    total = pick(hot[...], parts(grad, PIECES), NN)
    for q in range(4):
        groups = []
        for g in range(4):
            start = q * n + g * GROUP
            groups += split(total[start : start + GROUP, :])
        pack(out, TILES2, groups, q * TILES2 * GROUP)


def update_kernel(rep, grads, block, state, out, sums):
    n = LANE
    rows = TILES2 * GROUP
    sums[...] = (
        grads[0:rows, :] + grads[rows : 2 * rows, :]
        + (grads[2 * rows : 3 * rows, :] + grads[3 * rows :, :])
    )
    halves = unpack(sums, TILES2, 8, GROUP)
    grad = jnp.concatenate(
        [jnp.concatenate(halves[i::2], 0).T[0:200, :] for i in range(2)], 0
    )
    start = pl.multiple_of(rep[0] * n, n)
    mean = jnp.sum(grad * grad, 0, keepdims=True) * (1.0 / 400.0)
    new = state[:, pl.ds(start, n)] + mean
    out[0:400, :] = block[...] - learn_rate * grad / jnp.sqrt(new)
    out[400:408, :] = jnp.broadcast_to(new, (8, n))


def cut_kernel(rep, token, table_t, block, done):
    start = pl.multiple_of(rep[0] * LANE, LANE)
    copy = pltpu.make_async_copy(table_t.at[:, pl.ds(start, LANE)], block, done)
    copy.start()
    copy.wait()


def join_kernel(parts_in, table_new, state_new):
    for q in range(4):
        table_new[:, q * LANE : (q + 1) * LANE] = parts_in[q, 0:400, :]
        state_new[:, q * LANE : (q + 1) * LANE] = parts_in[q, 400:401, :]


def call(kernel, outs, args, scalars=(), name=None, scratch=(), whole=0):
    space = pl.BlockSpec(memory_space=pltpu.VMEM)
    return pl.pallas_call(
        kernel,
        out_shape=[
            (pltpu.VMEM if near else pltpu.HBM)(shape, kind)
            for shape, kind, near in outs
        ],
        in_specs=[pl.BlockSpec(memory_space=pltpu.SMEM)] * len(scalars)
        + [space] * (len(args) - whole)
        + [pl.BlockSpec(memory_space=pltpu.HBM)] * whole,
        out_specs=[space] * len(outs),
        scratch_shapes=list(scratch),
        compiler_params=pltpu.CompilerParams(vmem_limit_bytes=24 << 20),
        name=name,
    )(*scalars, *args)


def near(x):
    return pltpu.with_memory_space_constraint(x, pltpu.VMEM)


def far(x):
    return pltpu.with_memory_space_constraint(x, pltpu.HBM)


def exchange(x, axis, tiles):
    n = lax.axis_size(axis)
    x = x.reshape(n, 1, tiles * LANE)
    x = lax.all_to_all(x, axis, split_axis=0, concat_axis=0, tiled=True)
    return x.reshape(n * tiles, LANE)


def shift(x, by):
    n = lax.axis_size("rep")
    return lax.ppermute(x, "rep", [(i, (i + by) % n) for i in range(n)])


def swap_cores(x):
    return lax.ppermute(x, "ent", [(i, i ^ 1) for i in range(lax.axis_size("ent"))])


def on_device(
    entity_table,
    adagrad_state,
    head_owner,
    head_row,
    relation_ids,
    tail_owner,
    tail_row,
    neg_rows,
    relations,
):
    rep = lax.axis_index("rep").reshape(1).astype(jnp.int32)
    odd = (lax.axis_index("ent") & 1).reshape(1).astype(jnp.int32)
    table_t = entity_table.T
    neg_rows = far(neg_rows)
    n = LANE

    def line(x):
        return far(x.reshape(1, n))

    send1, head_edge, tail_edge = call(
        ask_kernel,
        [((n * TILES1, n), f32, False), ((n, n), f32, False), ((n, n), f32, False)],
        (
            line(head_owner),
            line(head_row),
            line(relation_ids),
            line(tail_owner),
            line(tail_row),
            far(table_t),
        ),
        (rep, neg_rows),
        "ask",
        (pltpu.VMEM((400, n), f32), pltpu.SemaphoreType.DMA),
        1,
    )
    recv1 = exchange(send1, "ent", TILES1)
    pieces = call(
        ahead_kernel,
        [((4 * n, 512), bf16, True)] * PIECES + [((64, 512), bf16, True)] * PIECES,
        (table_t, relations),
        name="ahead",
    )
    (same,) = call(
        pair_kernel,
        [((4 * n, 2 * n), bf16, True)],
        (far(head_edge), far(tail_edge)),
        name="pair",
    )
    rel_pieces = pieces[PIECES:]
    send2, rows, own_negs = call(
        fetch_kernel,
        [
            ((n * TILES2, n), f32, False),
            ((4 * n, 512), f32, True),
            ((n * TILES1, n), f32, True),
        ],
        (near(recv1), *map(near, pieces)),
        name="fetch",
    )
    recv2 = exchange(send2, "ent", TILES2)
    mine = lax.all_gather(own_negs, "rep", axis=0, tiled=True)
    other = swap_cores(mine)
    back, keep, give = call(
        negatives_kernel,
        [((4 * n, 512), f32, True)] + [((4 * n, 256), f32, True)] * 2,
        (near(recv1), near(rows), *map(far, rel_pieces), near(mine), near(other)),
        (odd,),
        "negatives",
    )
    owned = call(
        fold_kernel,
        [((n, 256), f32, True)] * 4,
        (near(keep), near(swap_cores(give))),
        (rep,),
        "fold",
    )
    sums = [owned[0]] + [shift(owned[j], j) for j in (1, 2, 3)]
    send3, token = call(
        edge_kernel,
        [((n * TILES3, n), f32, False), ((8, n), f32, False)],
        (near(recv2), near(same), far(sums[0]), *map(near, sums[1:])),
        name="edge",
    )
    recv3 = exchange(send3, "ent", TILES3)
    token = far(token)
    (side,) = call(
        carry_kernel,
        [((6 * n, 512), f32, True)],
        (token, recv1, far(back), *map(far, rel_pieces)),
        name="carry",
    )
    (hot,) = call(
        place_kernel, [((4 * n, 5 * n), bf16, True)], (recv1, token), (rep, neg_rows), "place"
    )
    (block,) = call(
        cut_kernel,
        [((400, n), f32, True)],
        (token, far(table_t)),
        (rep,),
        "cut",
        (pltpu.SemaphoreType.DMA,),
        1,
    )
    (grads,) = call(
        scatter_kernel,
        [((4 * TILES2 * GROUP, n), f32, False)],
        (near(recv3), near(hot), near(side)),
        name="scatter",
    )
    grads = lax.all_to_all(grads, "rep", split_axis=0, concat_axis=0, tiled=True)
    (fresh,) = call(
        update_kernel,
        [((408, n), f32, True)],
        (near(grads), near(block), adagrad_state.reshape(1, 512)),
        (rep,),
        "update",
        (pltpu.VMEM((TILES2 * GROUP, n), f32),),
    )
    fresh = lax.all_gather(fresh, "rep", axis=0, tiled=False)
    table_new, state_new = call(
        join_kernel, [((400, 512), f32, False), ((1, 512), f32, False)], (near(fresh),), name="join"
    )
    return (table_new.T, state_new.reshape(512))


def solution(mesh):
    placed = (
        P("ent", None),
        P("ent"),
        P(("ent", "rep"), None),
        P(("ent", "rep")),
        P(("ent", "rep")),
        P(("ent", "rep"), None),
        P(("ent", "rep")),
        P("ent"),
        P(),
    )
    return jax.shard_map(
        on_device, mesh=mesh, in_specs=placed, out_specs=(P("ent", None), P("ent")), check_vma=False
    )
```

```python
import math

import jax
import jax.numpy as jnp
from jax import lax
from jax.experimental import pallas as pl
from jax.experimental.pallas import tpu as pltpu
from jax.sharding import PartitionSpec as P

learn_rate = 0.1

LANE = 128
f32 = jnp.float32
bf16 = jnp.bfloat16
NN = (((1,), (0,)), ((), ()))
NT = (((1,), (1,)), ((), ()))
TN = (((0,), (0,)), ((), ()))
PIECES = 2
TILES1 = 2
TILES2 = 13
TILES3 = 4
STARTS = (0, 56, 104, 152)
SIZES = (56, 48, 48, 48)


def dot(a, b, dims):
    return lax.dot_general(a, b, dims, preferred_element_type=f32)


def parts(x, count):
    out = []
    for _ in range(count):
        head = x.astype(bf16)
        out.append(head)
        x = x - head.astype(f32)
    return out


def pick(onehot, pieces, dims):
    total = dot(onehot, pieces[0], dims)
    for piece in pieces[1:]:
        total = total + dot(onehot, piece, dims)
    return total


def dot3(a, b, dims):
    a0, a1 = parts(a, 2)
    b0, b1 = parts(b, 2)
    return dot(a0, b0, dims) + (dot(a0, b1, dims) + dot(a1, b0, dims))


def lanes(shape):
    return lax.broadcasted_iota(jnp.int32, shape, len(shape) - 1)


def cmul(a, b):
    return (a[0] * b[0] - a[1] * b[1], a[0] * b[1] + a[1] * b[0])


def conj(a):
    return (a[0], -a[1])


def sigmoid(x):
    return 1.0 / (1.0 + jnp.exp(-x))


def column(tile, lane):
    return jnp.sum(jnp.where(lanes(tile.shape) == lane, tile, 0.0), 1, keepdims=True)


def pack(ref, tiles, halves):
    n = halves[0].shape[0]
    at = lanes((n, LANE))
    tail = jnp.zeros((n, LANE), f32)
    for i, half in enumerate(halves):
        ref[pl.ds(i, n, stride=tiles), :] = half[:, :LANE]
        rest = half[:, LANE:]
        shift = (8 * i - 64) % LANE
        moved = pltpu.roll(rest, shift, 1) if shift else rest
        tail = jnp.where((at >= 8 * i) & (at < 8 * i + 8), moved, tail)
    for i in range(0, len(halves), 2):
        pair = halves[i][:, LANE:]
        if i + 1 < len(halves):
            pair = jnp.where(at < 64, pair, pltpu.roll(halves[i + 1][:, LANE:], 64, 1))
        ref[pl.ds(len(halves) + i // 2, n, stride=tiles), :] = pair
    ref[pl.ds(tiles - 1, n, stride=tiles), :] = tail


def unpack(ref, tiles, count, n):
    at = lanes((n, LANE))
    tail = ref[pl.ds(tiles - 1, n, stride=tiles), :]
    out = []
    for i in range(count):
        full = ref[pl.ds(i, n, stride=tiles), :]
        pair = ref[pl.ds(count + i // 2, n, stride=tiles), :]
        if i % 2:
            pair = pltpu.roll(pair, 64, 1)
        shift = (64 - 8 * i) % LANE
        moved = pltpu.roll(tail, shift, 1) if shift else tail
        rest = jnp.where(at < 64, pair, jnp.where(at < 72, moved, 0.0))
        out.append(jnp.concatenate([full, rest], 1))
    return out


def window(into, low, high, start, size, dest):
    at = lanes(into.shape)
    for src, first in ((low, 0), (high, LANE)):
        begin, end = max(start, first), min(start + size, first + LANE)
        if begin < end:
            goal = dest + begin - start
            shift = (goal - (begin - first)) % LANE
            moved = pltpu.roll(src, shift, 1) if shift else src
            into = jnp.where((at >= goal) & (at < goal + end - begin), moved, into)
    return into


def quarter(wide, q):
    out = jnp.zeros((wide.shape[0], LANE), f32)
    for i in range(2):
        low, high = (wide[:, (2 * i + j) * LANE : (2 * i + j + 1) * LANE] for j in range(2))
        out = window(out, low, high, STARTS[q], SIZES[q], 64 * i)
    return out


def ask_kernel(
    rep, neg_rows, head_owner, head_row, rel, tail_owner, tail_row, table_t,
    send, head_edge, tail_edge, block, done,
):
    n = LANE
    neg_at = neg_rows[rep[0]]
    copy = pltpu.make_async_copy(
        table_t.at[:, pl.ds(pl.multiple_of(neg_at // n * n, n), n)], block, done
    )
    copy.start()
    sub = lax.broadcasted_iota(jnp.int32, (n, n), 0)
    lane = lanes((n, n))

    def wide(x):
        return jnp.broadcast_to(x, (n, x.shape[1]))

    head_owner, head_row, rel, tail_owner, tail_row = (
        wide(ref[...].astype(f32)) for ref in (head_owner, head_row, rel, tail_owner, tail_row)
    )
    owner_id = sub.astype(f32)
    columns = []

    def slots(owner, named):
        owner_c = owner.T
        rank = jnp.sum(jnp.where((owner == owner_c) & (sub < lane), 1.0, 0.0), 0, keepdims=True)
        edges = []
        for s in range(2):
            here = (owner == owner_id) & (wide(rank) == float(s))
            columns.append(jnp.sum(jnp.where(here, named + 1.0, 0.0), 1, keepdims=True) - 1.0)
            columns.append(jnp.sum(jnp.where(here, rel, 0.0), 1, keepdims=True))
            edges.append(
                jnp.sum(jnp.where(here, lane.astype(f32) + 1.0, 0.0), 1, keepdims=True) - 1.0
            )
        return jnp.where(lane == 0, edges[0], jnp.where(lane == 1, edges[1], -1.0))

    head_edge[...] = slots(head_owner, head_row)
    tail_edge[...] = slots(tail_owner, tail_row)

    copy.wait()
    pad = jnp.zeros((56, n), f32)
    line = []
    for i in range(2):
        half = jnp.concatenate([block[200 * i : 200 * i + 200, :], pad], 0).T
        picked = lax.broadcasted_iota(jnp.int32, (n, 256), 0) == neg_at % n
        line.append(jnp.sum(jnp.where(picked, half, 0.0), 0, keepdims=True))
    even = sub % 2 == 0
    send[pl.ds(0, n, stride=TILES1), :] = jnp.where(even, wide(line[0][:, :n]), wide(line[1][:, :n]))
    tile = jnp.where(even, wide(line[0][:, n:]), wide(line[1][:, n:]))
    for j, col in enumerate(columns):
        tile = jnp.where(lane == 72 + j, col, tile)
    send[pl.ds(1, n, stride=TILES1), :] = tile


def ahead_kernel(table_t, relations, *outs):
    pad = jnp.zeros((56, 512), f32)
    whole = jnp.concatenate([table_t[0:200, :], pad, table_t[200:400, :], pad], 0).T
    for ref, piece in zip(outs[:PIECES], parts(whole, PIECES), strict=True):
        ref[...] = piece
    pad = jnp.zeros((64, 56), f32)
    whole = jnp.concatenate([relations[:, :200], pad, relations[:, 200:], pad], 1)
    for ref, piece in zip(outs[PIECES : 2 * PIECES], parts(whole, PIECES), strict=True):
        ref[...] = piece


def pair_kernel(head_edge, tail_edge, same):
    n = 2 * LANE

    def stack(ref, by_rows):
        if by_rows:
            turned = ref[...].T
            return jnp.concatenate([turned[0:1, :], turned[1:2, :]], 1)
        return jnp.concatenate([ref[:, 0:1], ref[:, 1:2]], 0)

    for i, (one, other) in enumerate(((head_edge, tail_edge), (tail_edge, head_edge))):
        col, row = stack(one, False), stack(other, True)
        same[i * n : (i + 1) * n, :] = jnp.where(
            (col == row) & (col >= 0.0), 1.0, 0.0
        ).astype(bf16)


def rel_vectors(tile, slots, pieces):
    ids = jnp.concatenate([column(tile, 72 + 2 * s + 1) for s in slots], 0)
    hot = jnp.where(lanes((ids.shape[0], 64)).astype(f32) == ids, 1.0, 0.0).astype(bf16)
    both = pick(hot, [p[...] for p in pieces], NN)
    return (both[:, :256], both[:, 256:])


def split(x):
    return (x[:, :256], x[:, 256:])


def fetch_kernel(recv, *refs):
    n = LANE
    table, rel = refs[:PIECES], refs[PIECES : 2 * PIECES]
    send, rows, negs = refs[2 * PIECES :]
    negs[...] = recv[...]
    tile = recv[pl.ds(1, n, stride=TILES1), :]
    halves = []
    for side in range(2):
        slots = (2 * side, 2 * side + 1)
        at = jnp.concatenate([column(tile, 72 + 2 * s) for s in slots], 0)
        hot = jnp.where(lanes((2 * n, 512)).astype(f32) == at, 1.0, 0.0).astype(bf16)
        vec = split(pick(hot, [p[...] for p in table], NN))
        if side == 0:
            vec = cmul(vec, rel_vectors(tile, slots, rel))
        for i in range(2):
            halves += [v[i * n : (i + 1) * n, :] for v in vec]
        for i in range(2):
            rows[2 * n * side : 2 * n * (side + 1), i * 256 : (i + 1) * 256] = vec[i]
    pack(send, TILES2, halves)


def negatives_kernel(odd, recv, rows, *refs):
    n = LANE
    rel = refs[:PIECES]
    mine, other, back, keep, give = refs[PIECES:]
    tile = recv[pl.ds(1, n, stride=TILES1), :]
    mask = lanes((n, LANE)) < 72

    def half(ref, base):
        low = ref[pl.ds(base, n, stride=TILES1), :]
        high = jnp.where(mask, ref[pl.ds(base + 1, n, stride=TILES1), :], 0.0)
        return jnp.concatenate([low, high], 1)

    flip = odd[0] > 0
    own, got = (
        jnp.concatenate([half(ref, TILES1 * n * j) for j in range(4)], 0) for ref in (mine, other)
    )
    negs = jnp.concatenate([jnp.where(flip, got, own), jnp.where(flip, own, got)], 1)
    probe = cmul(conj(rel_vectors(tile, (2, 3), rel)), split(rows[2 * n :, :]))
    x = jnp.concatenate([rows[0 : 2 * n, :], jnp.concatenate(probe, 1)], 0)
    valid = jnp.concatenate([column(tile, 72 + 2 * s) for s in range(4)], 0)
    coef = sigmoid(dot3(x, negs, NT)) * (1.0 / math.sqrt(512.0))
    coef = jnp.where(valid >= 0.0, coef, 0.0)
    back[...] = dot3(coef, negs, NN)
    total = dot3(coef, x, TN)
    re, im = split(total)
    keep[...] = jnp.where(flip, im, re)
    give[...] = jnp.where(flip, re, im)


def fold_kernel(rep, keep, got, *outs):
    for i, ref in enumerate(outs):
        at = pl.ds(pl.multiple_of((rep[0] + i) % 4 * LANE, LANE), LANE)
        ref[...] = keep[at, :] + got[at, :]


def edge_kernel(recv, same, sum0, sum1, sum2, sum3, send, token):
    n = LANE
    halves = unpack(recv, TILES2, 8, n)
    query, tails = (
        jnp.concatenate(
            [jnp.concatenate(halves[i : i + 2], 1), jnp.concatenate(halves[i + 2 : i + 4], 1)], 0
        )
        for i in (0, 4)
    )
    met = pick(same[0 : 2 * n, :], parts(tails, PIECES), NN)
    pos = jnp.sum(query * met, 1, keepdims=True)
    coef = -sigmoid(-pos)
    to_head = coef * met
    to_tail = pick(same[2 * n :, :], parts(coef * query, PIECES), NN)
    neg = sum0[...] + sum1[...] + (sum2[...] + sum3[...])
    low, high = neg[:, :LANE], neg[:, LANE:]
    for s, block in enumerate((to_head[:n], to_head[n:], to_tail[:n], to_tail[n:])):
        for q in range(4):
            tile = quarter(block, q)
            for i in range(2):
                word = 16 * s + 8 * i
                if word < 56:
                    tile = window(tile, low, high, STARTS[q] + word, 8, 56 + 64 * i)
            send[pl.ds(4 * q + s, n, stride=4 * TILES3), :] = tile
    token[...] = neg[0:8, 0:128]


def local_kernel(rep, token, asks, back, *refs):
    n = 2 * LANE
    *rel, out0, out1, out2, out3, quarters = refs
    tile = asks[pl.ds(1, LANE, stride=TILES1), :]
    turned = tile.T
    sub = lax.broadcasted_iota(jnp.int32, (512, LANE), 0).astype(f32)
    hot = jnp.concatenate(
        [
            jnp.where(sub == turned[72 + 2 * s : 73 + 2 * s, :], 1.0, 0.0).astype(bf16)
            for s in range(4)
        ],
        1,
    )
    head = cmul(split(back[0:n, :]), conj(rel_vectors(tile, (0, 1), rel)))
    tail = cmul(split(back[n:, :]), rel_vectors(tile, (2, 3), rel))
    grad = jnp.concatenate([jnp.concatenate(head, 1), jnp.concatenate(tail, 1)], 0)
    total = pick(hot, parts(grad, PIECES), NN)
    for q in range(4):
        quarters[q] = quarter(total, q)
    for i, ref in enumerate((out0, out1, out2, out3)):
        ref[...] = quarters[(rep[0] + i) % 4]


def gather_local_kernel(part0, part1, part2, part3, out):
    out[...] = part0[...] + part1[...] + (part2[...] + part3[...])


def rels_kernel(rep, token, asks, relations, out):
    pad = jnp.zeros((64, 56), f32)
    wide = jnp.concatenate([relations[:, :200], pad, relations[:, 200:], pad], 1)
    mine = jnp.zeros((64, LANE), f32)
    for q in range(4):
        mine = jnp.where(rep[0] == q, quarter(wide, q), mine)
    pieces = parts(mine, PIECES)
    for x in range(4):
        tile = asks[pl.ds(x * TILES1 * LANE + 1, LANE, stride=TILES1), :]
        ids = jnp.concatenate([column(tile, 73), column(tile, 75)], 0)
        hot = jnp.where(lanes((2 * LANE, 64)).astype(f32) == ids, 1.0, 0.0).astype(bf16)
        out[2 * x * LANE : 2 * (x + 1) * LANE, :] = pick(hot, pieces, NN)


def place_kernel(neg_rows, asks, token, hot):
    n = LANE
    sub = lax.broadcasted_iota(jnp.int32, (512, n), 0).astype(f32)
    for x in range(4):
        turned = asks[pl.ds(x * TILES1 * n + 1, n, stride=TILES1), :].T
        for s in range(4):
            at = turned[72 + 2 * s : 73 + 2 * s, :]
            b = 4 * x + s
            hot[:, b * n : (b + 1) * n] = jnp.where(sub == at, 1.0, 0.0).astype(bf16)
    at = jnp.full((1, n), -1.0, f32)
    for x in range(4):
        at = jnp.where(lanes((1, n)) == x, neg_rows[x].astype(f32), at)
    hot[:, 16 * n :] = jnp.where(sub == at, 1.0, 0.0).astype(bf16)


def scatter_kernel(recv, hot, rels, local, out):
    n = LANE
    at = lanes((n, n))
    even = lax.broadcasted_iota(jnp.int32, (n, n), 0) % 2 == 0
    which = lax.broadcasted_iota(jnp.int32, (8, n), 0)
    sums = [[jnp.zeros((8, n), f32) for _ in range(2)] for _ in range(4)]
    blocks = []
    for x in range(4):
        for s in range(4):
            tile = recv[pl.ds(4 * x + s, n, stride=4 * TILES3), :]
            reals = jnp.sum(jnp.where(even, tile, 0.0), 0, keepdims=True)
            imags = jnp.sum(jnp.where(even, 0.0, tile), 0, keepdims=True)
            sums[s] = [
                jnp.where(which == x, new, old) for old, new in zip(sums[s], (reals, imags))
            ]
            if s < 2:
                rel = rels[(2 * x + s) * n : (2 * x + s + 1) * n, :]
                other = pltpu.roll(rel, 64, 1)
                tile = tile * jnp.where(at < 64, rel, other) + pltpu.roll(
                    tile, 64, 1
                ) * jnp.where(at < 64, other, -rel)
            blocks.append(tile)
    neg = jnp.zeros((8, n), f32)
    lane = lanes((8, n))
    for s in range(4):
        for i in range(2):
            word = 16 * s + 8 * i
            if word < 56:
                for side in range(2):
                    goal = 64 * side + word
                    shift = (goal - (56 + 64 * i)) % n
                    moved = pltpu.roll(sums[s][side], shift, 1) if shift else sums[s][side]
                    neg = jnp.where((lane >= goal) & (lane < goal + 8), moved, neg)
    blocks += [neg, jnp.zeros((n - 8, n), f32)]
    both = jnp.concatenate(parts(jnp.concatenate(blocks, 0), 2), 1)
    total = dot(hot[...], both, NN)
    turned = (total[:, :n] + total[:, n:] + local[...]).T
    out[0:56, :] = turned[0:56, :]
    out[56:112, :] = turned[64:120, :]


def finish_kernel(grads, table_t, state, table_new, state_new):
    spans = [
        (q * 112 + i * 56, i * 200 + STARTS[q], SIZES[q]) for q in range(4) for i in range(2)
    ]
    total = jnp.zeros((1, 512), f32)
    for at, _, size in spans:
        grad = grads[at : at + size, :]
        total = total + jnp.sum(grad * grad, 0, keepdims=True)
    new = state[...] + total * (1.0 / 400.0)
    state_new[...] = new
    step = learn_rate / jnp.sqrt(new)
    for at, to, size in spans:
        table_new[to : to + size, :] = table_t[to : to + size, :] - grads[at : at + size, :] * step


def call(kernel, outs, args, scalars=(), name=None, scratch=(), whole=0):
    space = pl.BlockSpec(memory_space=pltpu.VMEM)
    return pl.pallas_call(
        kernel,
        out_shape=[
            (pltpu.VMEM if near else pltpu.HBM)(shape, kind)
            for shape, kind, near in outs
        ],
        in_specs=[pl.BlockSpec(memory_space=pltpu.SMEM)] * len(scalars)
        + [space] * (len(args) - whole)
        + [pl.BlockSpec(memory_space=pltpu.HBM)] * whole,
        out_specs=[space] * len(outs),
        scratch_shapes=list(scratch),
        compiler_params=pltpu.CompilerParams(vmem_limit_bytes=24 << 20),
        name=name,
    )(*scalars, *args)


def near(x):
    return pltpu.with_memory_space_constraint(x, pltpu.VMEM)


def far(x):
    return pltpu.with_memory_space_constraint(x, pltpu.HBM)


def exchange(x, axis, tiles):
    n = x.shape[0] // tiles
    x = x.reshape(n, 1, tiles * LANE)
    x = lax.all_to_all(x, axis, split_axis=0, concat_axis=0, tiled=True)
    return x.reshape(n * tiles, LANE)


def shift(x, by):
    n = lax.axis_size("rep")
    return lax.ppermute(x, "rep", [(i, (i + by) % n) for i in range(n)])


def swap_cores(x):
    return lax.ppermute(x, "ent", [(i, i ^ 1) for i in range(lax.axis_size("ent"))])


def on_device(
    entity_table,
    adagrad_state,
    head_owner,
    head_row,
    relation_ids,
    tail_owner,
    tail_row,
    neg_rows,
    relations,
):
    rep = lax.axis_index("rep").reshape(1).astype(jnp.int32)
    odd = (lax.axis_index("ent") & 1).reshape(1).astype(jnp.int32)
    table_t = entity_table.T
    neg_rows = far(neg_rows)
    n = LANE

    def line(x):
        return far(x.reshape(1, n))

    send1, head_edge, tail_edge = call(
        ask_kernel,
        [((n * TILES1, n), f32, False), ((n, n), f32, False), ((n, n), f32, False)],
        (
            line(head_owner),
            line(head_row),
            line(relation_ids),
            line(tail_owner),
            line(tail_row),
            far(table_t),
        ),
        (rep, neg_rows),
        "ask",
        (pltpu.VMEM((400, n), f32), pltpu.SemaphoreType.DMA),
        1,
    )
    recv1 = exchange(send1, "ent", TILES1)
    pieces = call(
        ahead_kernel,
        [((4 * n, 512), bf16, True)] * PIECES + [((64, 512), bf16, True)] * PIECES,
        (table_t, relations),
        name="ahead",
    )
    (same,) = call(
        pair_kernel,
        [((4 * n, 2 * n), bf16, True)],
        (far(head_edge), far(tail_edge)),
        name="pair",
    )
    rel_pieces = pieces[PIECES:]
    send2, rows, own_negs = call(
        fetch_kernel,
        [
            ((n * TILES2, n), f32, False),
            ((4 * n, 512), f32, True),
            ((n * TILES1, n), f32, True),
        ],
        (near(recv1), *map(near, pieces)),
        name="fetch",
    )
    recv2 = exchange(send2, "ent", TILES2)
    mine = lax.all_gather(own_negs, "rep", axis=0, tiled=True)
    other = swap_cores(mine)
    back, keep, give = call(
        negatives_kernel,
        [((4 * n, 512), f32, True)] + [((4 * n, 256), f32, True)] * 2,
        (near(recv1), near(rows), *map(far, rel_pieces), near(mine), near(other)),
        (odd,),
        "negatives",
    )
    owned = call(
        fold_kernel,
        [((n, 256), f32, True)] * 4,
        (near(keep), near(swap_cores(give))),
        (rep,),
        "fold",
    )
    sums = [owned[0]] + [shift(owned[j], j) for j in (1, 2, 3)]
    send3, token = call(
        edge_kernel,
        [((4 * n * TILES3, n), f32, False), ((8, n), f32, False)],
        (near(recv2), near(same), far(sums[0]), *map(near, sums[1:])),
        name="edge",
    )
    recv3 = exchange(send3, ("ent", "rep"), TILES3)
    token = far(token)
    local = call(
        local_kernel,
        [((4 * n, n), f32, True)] * 4,
        (token, recv1, far(back), *map(far, rel_pieces)),
        (rep,),
        "local",
        (pltpu.VMEM((4, 4 * n, n), f32),),
    )
    (local,) = call(
        gather_local_kernel,
        [((4 * n, n), f32, True)],
        [far(local[0])] + [far(shift(local[j], j)) for j in (1, 2, 3)],
        name="gather_local",
    )
    (hot,) = call(
        place_kernel, [((4 * n, 17 * n), bf16, True)], (far(mine), token), (neg_rows,), "place"
    )
    (rels,) = call(
        rels_kernel, [((8 * n, n), f32, True)], (near(local), far(mine), relations), (rep,), "rels"
    )
    (grads,) = call(
        scatter_kernel,
        [((112, 512), f32, True)],
        (near(recv3), near(hot), near(rels), near(local)),
        name="scatter",
    )
    grads = lax.all_gather(grads, "rep", axis=0, tiled=True)
    table_new, state_new = call(
        finish_kernel,
        [((400, 512), f32, False), ((1, 512), f32, False)],
        (near(grads), table_t, adagrad_state.reshape(1, 512)),
        name="finish",
    )
    return (table_new.T, state_new.reshape(512))


def solution(mesh):
    placed = (
        P("ent", None),
        P("ent"),
        P(("ent", "rep"), None),
        P(("ent", "rep")),
        P(("ent", "rep")),
        P(("ent", "rep"), None),
        P(("ent", "rep")),
        P("ent"),
        P(),
    )
    return jax.shard_map(
        on_device, mesh=mesh, in_specs=placed, out_specs=(P("ent", None), P("ent")), check_vma=False
    )
```

```python
import math

import jax
import jax.numpy as jnp
from jax import lax
from jax.experimental import pallas as pl
from jax.experimental.pallas import tpu as pltpu
from jax.sharding import PartitionSpec as P

learn_rate = 0.1

LANE = 128
f32 = jnp.float32
bf16 = jnp.bfloat16
NN = (((1,), (0,)), ((), ()))
NT = (((1,), (1,)), ((), ()))
TN = (((0,), (0,)), ((), ()))
PIECES = 2
TILES1 = 2
TILES2 = 13
TILES3 = 4
ASKS = 112
STARTS = (0, 56, 104, 152)
SIZES = (56, 48, 48, 48)


def dot(a, b, dims):
    return lax.dot_general(a, b, dims, preferred_element_type=f32)


def parts(x, count):
    out = []
    for _ in range(count):
        head = x.astype(bf16)
        out.append(head)
        x = x - head.astype(f32)
    return out


def pick(onehot, pieces, dims):
    total = dot(onehot, pieces[0], dims)
    for piece in pieces[1:]:
        total = total + dot(onehot, piece, dims)
    return total


def dot3(a, b, dims):
    a0, a1 = parts(a, 2)
    b0, b1 = parts(b, 2)
    return dot(a0, b0, dims) + (dot(a0, b1, dims) + dot(a1, b0, dims))


def lanes(shape):
    return lax.broadcasted_iota(jnp.int32, shape, len(shape) - 1)


def tile_of(x, q):
    return x[:, q * LANE : (q + 1) * LANE]


def turn(x):
    return jnp.concatenate([pltpu.roll(tile_of(x, q), 64, 1) for q in range(4)], 1)


def cmul(a, b, conj=False):
    low = lanes(b.shape) % LANE < 64
    other = turn(b)
    second = jnp.where(low, other, -b) if conj else jnp.where(low, -other, b)
    return a * jnp.where(low, b, other) + turn(a) * second


def sigmoid(x):
    return 1.0 / (1.0 + jnp.exp(-x))


def column(tile, lane):
    return jnp.sum(jnp.where(lanes(tile.shape) == lane, tile, 0.0), 1, keepdims=True)


def pack(ref, slots):
    n = slots[0].shape[0]
    at = lanes((n, LANE)) % 64
    tail = jnp.zeros((n, LANE), f32)
    for s, slot in enumerate(slots):
        first = tile_of(slot, 0)
        for j in range(1, 4):
            moved = pltpu.roll(first, 64 - 16 * j, 1)
            ref[pl.ds(3 * s + j - 1, n, stride=TILES2), :] = jnp.where(
                at < 48, tile_of(slot, j), moved
            )
        moved = pltpu.roll(first, (8 * s - 48) % LANE, 1)
        tail = jnp.where((at >= 8 * s) & (at < 8 * s + 8), moved, tail)
    ref[pl.ds(12, n, stride=TILES2), :] = tail


def unpack(ref, n):
    at = lanes((n, LANE)) % 64
    tail = ref[pl.ds(12, n, stride=TILES2), :]
    out = []
    for s in range(4):
        first = jnp.where(at < 56, pltpu.roll(tail, 48 - 8 * s, 1), 0.0)
        others = []
        for j in range(3, 0, -1):
            dense = ref[pl.ds(3 * s + j - 1, n, stride=TILES2), :]
            first = jnp.where(at < 16 * j, pltpu.roll(dense, 64 + 16 * j, 1), first)
            others.append(jnp.where(at < 48, dense, 0.0))
        out.append(jnp.concatenate([first] + others[::-1], 1))
    return out


def window(into, low, high, start, size, dest):
    at = lanes(into.shape)
    for src, first in ((low, 0), (high, LANE)):
        begin, end = max(start, first), min(start + size, first + LANE)
        if begin < end:
            goal = dest + begin - start
            shift = (goal - (begin - first)) % LANE
            moved = pltpu.roll(src, shift, 1) if shift else src
            into = jnp.where((at >= goal) & (at < goal + end - begin), moved, into)
    return into


def quarter(wide, q):
    out = jnp.zeros((wide.shape[0], LANE), f32)
    for i in range(2):
        low, high = (wide[:, (2 * i + j) * LANE : (2 * i + j + 1) * LANE] for j in range(2))
        out = window(out, low, high, STARTS[q], SIZES[q], 64 * i)
    return out


def spread(rows, sides):
    out = []
    for q in range(4):
        for i in sides:
            at = 200 * i + STARTS[q]
            out.append(rows[at : at + SIZES[q], :])
            out.append(jnp.zeros((64 - SIZES[q], rows.shape[1]), f32))
    return jnp.concatenate(out, 0)


def ask_kernel(
    rep, neg_rows, head_owner, head_row, rel, tail_owner, tail_row, table_t,
    send, head_edge, tail_edge, block, done,
):
    n = LANE
    neg_at = neg_rows[rep[0]]
    copy = pltpu.make_async_copy(
        table_t.at[:, pl.ds(pl.multiple_of(neg_at // n * n, n), n)], block, done
    )
    copy.start()
    sub = lax.broadcasted_iota(jnp.int32, (n, n), 0)
    lane = lanes((n, n))

    def wide(x):
        return jnp.broadcast_to(x, (n, x.shape[1]))

    head_owner, head_row, rel, tail_owner, tail_row = (
        wide(ref[...].astype(f32)) for ref in (head_owner, head_row, rel, tail_owner, tail_row)
    )
    owner_id = sub.astype(f32)
    columns = []

    def slots(owner, named):
        owner_c = owner.T
        rank = jnp.sum(jnp.where((owner == owner_c) & (sub < lane), 1.0, 0.0), 0, keepdims=True)
        edges = []
        for s in range(2):
            here = (owner == owner_id) & (wide(rank) == float(s))
            columns.append(jnp.sum(jnp.where(here, named + 1.0, 0.0), 1, keepdims=True) - 1.0)
            columns.append(jnp.sum(jnp.where(here, rel, 0.0), 1, keepdims=True))
            edges.append(
                jnp.sum(jnp.where(here, lane.astype(f32) + 1.0, 0.0), 1, keepdims=True) - 1.0
            )
        return jnp.where(lane == 0, edges[0], jnp.where(lane == 1, edges[1], -1.0))

    edges = slots(head_owner, head_row)
    edges = jnp.where(lane == 2, columns[1], jnp.where(lane == 3, columns[3], edges))
    head_edge[...] = edges
    tail_edge[...] = slots(tail_owner, tail_row)

    copy.wait()
    line = []
    for i in range(2):
        half = spread(block, (i,)).T
        picked = lax.broadcasted_iota(jnp.int32, (n, 256), 0) == neg_at % n
        line.append(jnp.sum(jnp.where(picked, half, 0.0), 0, keepdims=True))
    even = sub % 2 == 0
    send[pl.ds(0, n, stride=TILES1), :] = jnp.where(even, wide(line[0][:, :n]), wide(line[1][:, :n]))
    tile = jnp.where(even, wide(line[0][:, n:]), wide(line[1][:, n:]))
    for j, col in enumerate(columns):
        tile = jnp.where(lane == ASKS + j, col, tile)
    send[pl.ds(1, n, stride=TILES1), :] = tile


def ahead_kernel(table_t, relations, head_edge, *outs):
    whole = spread(table_t[...], (0, 1)).T
    for ref, piece in zip(outs[:PIECES], parts(whole, PIECES), strict=True):
        ref[...] = piece
    pad = jnp.zeros((64, 56), f32)
    whole = jnp.concatenate([relations[:, :200], pad, relations[:, 200:], pad], 1)
    whole = jnp.concatenate([quarter(whole, q) for q in range(4)], 1)
    pieces = parts(whole, PIECES)
    for ref, piece in zip(outs[PIECES:-1], pieces, strict=True):
        ref[...] = piece
    ids = jnp.concatenate([head_edge[:, 2:3], head_edge[:, 3:4]], 0)
    hot = jnp.where(lanes((2 * LANE, 64)).astype(f32) == ids, 1.0, 0.0).astype(bf16)
    outs[-1][...] = pick(hot, pieces, NN)


def pair_kernel(head_edge, tail_edge, same):
    n = 2 * LANE

    def stack(ref, by_rows):
        if by_rows:
            turned = ref[...].T
            return jnp.concatenate([turned[0:1, :], turned[1:2, :]], 1)
        return jnp.concatenate([ref[:, 0:1], ref[:, 1:2]], 0)

    for i, (one, other) in enumerate(((head_edge, tail_edge), (tail_edge, head_edge))):
        col, row = stack(one, False), stack(other, True)
        same[i * n : (i + 1) * n, :] = jnp.where(
            (col == row) & (col >= 0.0), 1.0, 0.0
        ).astype(bf16)


def rel_vectors(tile, slots, pieces):
    ids = jnp.concatenate([column(tile, ASKS + 2 * s + 1) for s in slots], 0)
    hot = jnp.where(lanes((ids.shape[0], 64)).astype(f32) == ids, 1.0, 0.0).astype(bf16)
    return pick(hot, [p[...] for p in pieces], NN)


def fetch_kernel(recv, *refs):
    n = LANE
    table, rel = refs[:PIECES], refs[PIECES : 2 * PIECES]
    send, rows, negs = refs[2 * PIECES :]
    negs[...] = recv[...]
    tile = recv[pl.ds(1, n, stride=TILES1), :]
    packed = []
    for side in range(2):
        slots = (2 * side, 2 * side + 1)
        at = jnp.concatenate([column(tile, ASKS + 2 * s) for s in slots], 0)
        hot = jnp.where(lanes((2 * n, 512)).astype(f32) == at, 1.0, 0.0).astype(bf16)
        vec = pick(hot, [p[...] for p in table], NN)
        if side == 0:
            vec = cmul(vec, rel_vectors(tile, slots, rel))
        packed += [vec[:n, :], vec[n:, :]]
        rows[2 * n * side : 2 * n * (side + 1), :] = vec
    pack(send, packed)


def negatives_kernel(odd, recv, rows, *refs):
    n = LANE
    rel = refs[:PIECES]
    mine, other, back, keep, give = refs[PIECES:]
    tile = recv[pl.ds(1, n, stride=TILES1), :]
    at = lanes((n, LANE))
    low = lanes((4 * n, LANE)) < 64

    def half(ref):
        first = [ref[pl.ds(TILES1 * n * j, n, stride=TILES1), :] for j in range(4)]
        second = [ref[pl.ds(TILES1 * n * j + 1, n, stride=TILES1), :] for j in range(4)]
        second = [jnp.where(at < ASKS, x, 0.0) for x in second]
        return jnp.concatenate(first, 0), jnp.concatenate(second, 0)

    flip = odd[0] > 0
    negs = []
    for own, got in zip(half(mine), half(other)):
        re, im = jnp.where(flip, got, own), jnp.where(flip, own, got)
        negs.append(jnp.where(low, re, pltpu.roll(im, 64, 1)))
        negs.append(jnp.where(low, pltpu.roll(re, 64, 1), im))
    negs = jnp.concatenate(negs, 1)
    probe = cmul(rows[2 * n :, :], rel_vectors(tile, (2, 3), rel), True)
    x = jnp.concatenate([rows[0 : 2 * n, :], probe], 0)
    valid = jnp.concatenate([column(tile, ASKS + 2 * s) for s in range(4)], 0)
    coef = sigmoid(dot3(x, negs, NT)) * (1.0 / math.sqrt(512.0))
    coef = jnp.where(valid >= 0.0, coef, 0.0)
    back[...] = dot3(coef, negs, NN)
    total = dot3(coef, x, TN)
    for i in range(2):
        first, second = tile_of(total, 2 * i), tile_of(total, 2 * i + 1)
        re = jnp.where(low, first, pltpu.roll(second, 64, 1))
        im = jnp.where(low, pltpu.roll(first, 64, 1), second)
        keep[:, i * n : (i + 1) * n] = jnp.where(flip, im, re)
        give[:, i * n : (i + 1) * n] = jnp.where(flip, re, im)


def fold_kernel(rep, keep, got, *outs):
    for i, ref in enumerate(outs):
        at = pl.ds(pl.multiple_of((rep[0] + i) % 4 * LANE, LANE), LANE)
        ref[...] = keep[at, :] + got[at, :]


def edge_kernel(recv, same, rels, sum0, sum1, sum2, sum3, send, token):
    n = LANE
    slots = unpack(recv, n)
    query, tails = jnp.concatenate(slots[:2], 0), jnp.concatenate(slots[2:], 0)
    met = pick(same[0 : 2 * n, :], parts(tails, PIECES), NN)
    pos = jnp.sum(query * met, 1, keepdims=True)
    coef = -sigmoid(-pos)
    to_head = cmul(coef * met, rels[...], True)
    to_tail = pick(same[2 * n :, :], parts(coef * query, PIECES), NN)
    neg = sum0[...] + sum1[...] + (sum2[...] + sum3[...])
    at = lanes((n, LANE))
    for q in range(4):
        words = tile_of(neg, q // 2)
        if q % 2:
            words = pltpu.roll(words, 64, 1)
        words = jnp.where(at < 64, words, pltpu.roll(words, 32, 1))
        for s, block in enumerate((to_head[:n], to_head[n:], to_tail[:n], to_tail[n:])):
            moved = pltpu.roll(words, 56 - 8 * s, 1)
            send[pl.ds(4 * q + s, n, stride=4 * TILES3), :] = jnp.where(
                at % 64 < 56, tile_of(block, q), moved
            )
    token[...] = neg[0:8, 0:128]


def local_kernel(rep, token, asks, back, *refs):
    n = 2 * LANE
    *rel, out0, out1, out2, out3, quarters = refs
    tile = asks[pl.ds(1, LANE, stride=TILES1), :]
    turned = tile.T
    sub = lax.broadcasted_iota(jnp.int32, (512, LANE), 0).astype(f32)
    hot = jnp.concatenate(
        [
            jnp.where(sub == turned[ASKS + 2 * s : ASKS + 2 * s + 1, :], 1.0, 0.0).astype(bf16)
            for s in range(4)
        ],
        1,
    )
    head = cmul(back[0:n, :], rel_vectors(tile, (0, 1), rel), True)
    tail = cmul(back[n:, :], rel_vectors(tile, (2, 3), rel))
    grad = jnp.concatenate([head, tail], 0)
    total = pick(hot, parts(grad, PIECES), NN)
    for q in range(4):
        quarters[q] = tile_of(total, q)
    for i, ref in enumerate((out0, out1, out2, out3)):
        ref[...] = quarters[(rep[0] + i) % 4]


def gather_local_kernel(part0, part1, part2, part3, out):
    out[...] = part0[...] + part1[...] + (part2[...] + part3[...])


def place_kernel(neg_rows, asks, token, hot):
    n = LANE
    sub = lax.broadcasted_iota(jnp.int32, (512, n), 0).astype(f32)
    for x in range(4):
        turned = asks[pl.ds(x * TILES1 * n + 1, n, stride=TILES1), :].T
        for s in range(4):
            at = turned[ASKS + 2 * s : ASKS + 2 * s + 1, :]
            b = 4 * x + s
            hot[:, b * n : (b + 1) * n] = jnp.where(sub == at, 1.0, 0.0).astype(bf16)
    at = jnp.full((1, n), -1.0, f32)
    for x in range(4):
        at = jnp.where(lanes((1, n)) == x, neg_rows[x].astype(f32), at)
    hot[:, 16 * n :] = jnp.where(sub == at, 1.0, 0.0).astype(bf16)


def scatter_kernel(recv, hot, local, out):
    n = LANE
    even = lax.broadcasted_iota(jnp.int32, (n, n), 0) % 2 == 0
    which = lax.broadcasted_iota(jnp.int32, (8, n), 0)
    sums = [[jnp.zeros((8, n), f32) for _ in range(2)] for _ in range(4)]
    blocks = []
    for x in range(4):
        for s in range(4):
            tile = recv[pl.ds(4 * x + s, n, stride=4 * TILES3), :]
            reals = jnp.sum(jnp.where(even, tile, 0.0), 0, keepdims=True)
            imags = jnp.sum(jnp.where(even, 0.0, tile), 0, keepdims=True)
            sums[s] = [
                jnp.where(which == x, new, old) for old, new in zip(sums[s], (reals, imags))
            ]
            blocks.append(tile)
    neg = jnp.zeros((8, n), f32)
    lane = lanes((8, n))
    for s in range(4):
        for i in range(2):
            word = 32 * i + 8 * s
            if word < 56:
                for side in range(2):
                    goal = 64 * side + word
                    shift = (goal - (56 + 64 * i)) % n
                    moved = pltpu.roll(sums[s][side], shift, 1) if shift else sums[s][side]
                    neg = jnp.where((lane >= goal) & (lane < goal + 8), moved, neg)
    blocks += [neg, jnp.zeros((n - 8, n), f32)]
    both = jnp.concatenate(parts(jnp.concatenate(blocks, 0), 2), 1)
    total = dot(hot[...], both, NN)
    turned = (total[:, :n] + total[:, n:] + local[...]).T
    out[0:56, :] = turned[0:56, :]
    out[56:112, :] = turned[64:120, :]


def finish_kernel(grads, table_t, state, table_new, state_new):
    spans = [
        (q * 112 + i * 56, i * 200 + STARTS[q], SIZES[q]) for q in range(4) for i in range(2)
    ]
    total = jnp.zeros((1, 512), f32)
    for at, _, size in spans:
        grad = grads[at : at + size, :]
        total = total + jnp.sum(grad * grad, 0, keepdims=True)
    new = state[...] + total * (1.0 / 400.0)
    state_new[...] = new
    step = learn_rate / jnp.sqrt(new)
    for at, to, size in spans:
        table_new[to : to + size, :] = table_t[to : to + size, :] - grads[at : at + size, :] * step


def call(kernel, outs, args, scalars=(), name=None, scratch=(), whole=0):
    space = pl.BlockSpec(memory_space=pltpu.VMEM)
    return pl.pallas_call(
        kernel,
        out_shape=[
            (pltpu.VMEM if near else pltpu.HBM)(shape, kind)
            for shape, kind, near in outs
        ],
        in_specs=[pl.BlockSpec(memory_space=pltpu.SMEM)] * len(scalars)
        + [space] * (len(args) - whole)
        + [pl.BlockSpec(memory_space=pltpu.HBM)] * whole,
        out_specs=[space] * len(outs),
        scratch_shapes=list(scratch),
        compiler_params=pltpu.CompilerParams(vmem_limit_bytes=24 << 20),
        name=name,
    )(*scalars, *args)


def near(x):
    return pltpu.with_memory_space_constraint(x, pltpu.VMEM)


def far(x):
    return pltpu.with_memory_space_constraint(x, pltpu.HBM)


def exchange(x, axis, tiles):
    n = x.shape[0] // tiles
    x = x.reshape(n, 1, tiles * LANE)
    x = lax.all_to_all(x, axis, split_axis=0, concat_axis=0, tiled=True)
    return x.reshape(n * tiles, LANE)


def shift(x, by):
    n = lax.axis_size("rep")
    return lax.ppermute(x, "rep", [(i, (i + by) % n) for i in range(n)])


def swap_cores(x):
    return lax.ppermute(x, "ent", [(i, i ^ 1) for i in range(lax.axis_size("ent"))])


def on_device(
    entity_table,
    adagrad_state,
    head_owner,
    head_row,
    relation_ids,
    tail_owner,
    tail_row,
    neg_rows,
    relations,
):
    rep = lax.axis_index("rep").reshape(1).astype(jnp.int32)
    odd = (lax.axis_index("ent") & 1).reshape(1).astype(jnp.int32)
    table_t = entity_table.T
    neg_rows = far(neg_rows)
    n = LANE

    def line(x):
        return far(x.reshape(1, n))

    send1, head_edge, tail_edge = call(
        ask_kernel,
        [((n * TILES1, n), f32, False), ((n, n), f32, False), ((n, n), f32, False)],
        (
            line(head_owner),
            line(head_row),
            line(relation_ids),
            line(tail_owner),
            line(tail_row),
            far(table_t),
        ),
        (rep, neg_rows),
        "ask",
        (pltpu.VMEM((400, n), f32), pltpu.SemaphoreType.DMA),
        1,
    )
    recv1 = exchange(send1, "ent", TILES1)
    *pieces, edge_rels = call(
        ahead_kernel,
        [((4 * n, 512), bf16, True)] * PIECES
        + [((64, 512), bf16, True)] * PIECES
        + [((2 * n, 512), f32, True)],
        (table_t, relations, far(head_edge)),
        name="ahead",
    )
    (same,) = call(
        pair_kernel,
        [((4 * n, 2 * n), bf16, True)],
        (far(head_edge), far(tail_edge)),
        name="pair",
    )
    rel_pieces = pieces[PIECES:]
    send2, rows, own_negs = call(
        fetch_kernel,
        [
            ((n * TILES2, n), f32, False),
            ((4 * n, 512), f32, True),
            ((n * TILES1, n), f32, True),
        ],
        (near(recv1), *map(near, pieces)),
        name="fetch",
    )
    recv2 = exchange(send2, "ent", TILES2)
    mine = lax.all_gather(own_negs, "rep", axis=0, tiled=True)
    other = swap_cores(mine)
    back, keep, give = call(
        negatives_kernel,
        [((4 * n, 512), f32, True)] + [((4 * n, 256), f32, True)] * 2,
        (near(recv1), near(rows), *map(far, rel_pieces), near(mine), near(other)),
        (odd,),
        "negatives",
    )
    owned = call(
        fold_kernel,
        [((n, 256), f32, True)] * 4,
        (near(keep), near(swap_cores(give))),
        (rep,),
        "fold",
    )
    sums = [owned[0]] + [shift(owned[j], j) for j in (1, 2, 3)]
    send3, token = call(
        edge_kernel,
        [((4 * n * TILES3, n), f32, False), ((8, n), f32, False)],
        (near(recv2), near(same), far(edge_rels), far(sums[0]), *map(near, sums[1:])),
        name="edge",
    )
    recv3 = exchange(send3, ("ent", "rep"), TILES3)
    token = far(token)
    local = call(
        local_kernel,
        [((4 * n, n), f32, True)] * 4,
        (token, recv1, far(back), *map(far, rel_pieces)),
        (rep,),
        "local",
        (pltpu.VMEM((4, 4 * n, n), f32),),
    )
    (local,) = call(
        gather_local_kernel,
        [((4 * n, n), f32, True)],
        [far(local[0])] + [far(shift(local[j], j)) for j in (1, 2, 3)],
        name="gather_local",
    )
    (hot,) = call(
        place_kernel, [((4 * n, 17 * n), bf16, True)], (far(mine), token), (neg_rows,), "place"
    )
    (grads,) = call(
        scatter_kernel,
        [((112, 512), f32, True)],
        (near(recv3), near(hot), near(local)),
        name="scatter",
    )
    grads = lax.all_gather(grads, "rep", axis=0, tiled=True)
    table_new, state_new = call(
        finish_kernel,
        [((400, 512), f32, False), ((1, 512), f32, False)],
        (near(grads), table_t, adagrad_state.reshape(1, 512)),
        name="finish",
    )
    return (table_new.T, state_new.reshape(512))


def solution(mesh):
    placed = (
        P("ent", None),
        P("ent"),
        P(("ent", "rep"), None),
        P(("ent", "rep")),
        P(("ent", "rep")),
        P(("ent", "rep"), None),
        P(("ent", "rep")),
        P("ent"),
        P(),
    )
    return jax.shard_map(
        on_device, mesh=mesh, in_specs=placed, out_specs=(P("ent", None), P("ent")), check_vma=False
    )
```

```python
import math

import jax
import jax.numpy as jnp
from jax import lax
from jax.experimental import pallas as pl
from jax.experimental.pallas import tpu as pltpu
from jax.sharding import PartitionSpec as P

learn_rate = 0.1

LANE = 128
f32 = jnp.float32
bf16 = jnp.bfloat16
NN = (((1,), (0,)), ((), ()))
NT = (((1,), (1,)), ((), ()))
TN = (((0,), (0,)), ((), ()))
PIECES = 2
TILES1 = 2
TILES2 = 13
TILES3 = 4
ASKS = 112
STARTS = (0, 56, 104, 152)
SIZES = (56, 48, 48, 48)


def dot(a, b, dims):
    return lax.dot_general(a, b, dims, preferred_element_type=f32)


def parts(x, count):
    out = []
    for _ in range(count):
        head = x.astype(bf16)
        out.append(head)
        x = x - head.astype(f32)
    return out


def pick(onehot, pieces, dims):
    total = dot(onehot, pieces[0], dims)
    for piece in pieces[1:]:
        total = total + dot(onehot, piece, dims)
    return total


def dot3(a, b, dims):
    a0, a1 = parts(a, 2)
    b0, b1 = parts(b, 2)
    return dot(a0, b0, dims) + (dot(a0, b1, dims) + dot(a1, b0, dims))


def lanes(shape):
    return lax.broadcasted_iota(jnp.int32, shape, len(shape) - 1)


def tile_of(x, q):
    return x[:, q * LANE : (q + 1) * LANE]


def turn(x):
    return jnp.concatenate([pltpu.roll(tile_of(x, q), 64, 1) for q in range(4)], 1)


def factors(b, conj=False):
    low = lanes(b.shape) % LANE < 64
    other = turn(b)
    second = jnp.where(low, other, -b) if conj else jnp.where(low, -other, b)
    return jnp.where(low, b, other), second


def cmul(a, b, conj=False):
    first, second = factors(b, conj)
    return a * first + turn(a) * second


def in_parts(write, rows, stage, out, done):
    copies = []
    for c in range(4):
        write(c)
        at = pl.ds(c * rows, rows)
        copies.append(pltpu.make_async_copy(stage.at[at, :], out.at[at, :], done.at[c]))
        copies[-1].start()
    for copy in copies:
        copy.wait()


def sigmoid(x):
    return 1.0 / (1.0 + jnp.exp(-x))


def column(tile, lane):
    return jnp.sum(jnp.where(lanes(tile.shape) == lane, tile, 0.0), 1, keepdims=True)


def pack(ref, slots, base):
    n = slots[0].shape[0]
    at = lanes((n, LANE)) % 64
    tail = jnp.zeros((n, LANE), f32)
    for s, slot in enumerate(slots):
        first = tile_of(slot, 0)
        for j in range(1, 4):
            moved = pltpu.roll(first, 64 - 16 * j, 1)
            ref[pl.ds(base + 3 * s + j - 1, n, stride=TILES2), :] = jnp.where(
                at < 48, tile_of(slot, j), moved
            )
        moved = pltpu.roll(first, (8 * s - 48) % LANE, 1)
        tail = jnp.where((at >= 8 * s) & (at < 8 * s + 8), moved, tail)
    ref[pl.ds(base + 12, n, stride=TILES2), :] = tail


def unpack(ref, n):
    at = lanes((n, LANE)) % 64
    tail = ref[pl.ds(12, n, stride=TILES2), :]
    out = []
    for s in range(4):
        first = jnp.where(at < 56, pltpu.roll(tail, 48 - 8 * s, 1), 0.0)
        others = []
        for j in range(3, 0, -1):
            dense = ref[pl.ds(3 * s + j - 1, n, stride=TILES2), :]
            first = jnp.where(at < 16 * j, pltpu.roll(dense, 64 + 16 * j, 1), first)
            others.append(jnp.where(at < 48, dense, 0.0))
        out.append(jnp.concatenate([first] + others[::-1], 1))
    return out


def window(into, low, high, start, size, dest):
    at = lanes(into.shape)
    for src, first in ((low, 0), (high, LANE)):
        begin, end = max(start, first), min(start + size, first + LANE)
        if begin < end:
            goal = dest + begin - start
            shift = (goal - (begin - first)) % LANE
            moved = pltpu.roll(src, shift, 1) if shift else src
            into = jnp.where((at >= goal) & (at < goal + end - begin), moved, into)
    return into


def quarter(wide, q):
    out = jnp.zeros((wide.shape[0], LANE), f32)
    for i in range(2):
        low, high = (wide[:, (2 * i + j) * LANE : (2 * i + j + 1) * LANE] for j in range(2))
        out = window(out, low, high, STARTS[q], SIZES[q], 64 * i)
    return out


def spread(rows, sides):
    out = []
    for q in range(4):
        for i in sides:
            at = 200 * i + STARTS[q]
            out.append(rows[at : at + SIZES[q], :])
            out.append(jnp.zeros((64 - SIZES[q], rows.shape[1]), f32))
    return jnp.concatenate(out, 0)


def ask_kernel(
    rep, neg_rows, head_owner, head_row, rel, tail_owner, tail_row, table_t,
    send, head_edge, tail_edge, block, done,
):
    n = LANE
    neg_at = neg_rows[rep[0]]
    copy = pltpu.make_async_copy(
        table_t.at[:, pl.ds(pl.multiple_of(neg_at // n * n, n), n)], block, done
    )
    copy.start()
    sub = lax.broadcasted_iota(jnp.int32, (n, n), 0)
    lane = lanes((n, n))

    def wide(x):
        return jnp.broadcast_to(x, (n, x.shape[1]))

    head_owner, head_row, rel, tail_owner, tail_row = (
        wide(ref[...].astype(f32)) for ref in (head_owner, head_row, rel, tail_owner, tail_row)
    )
    owner_id = sub.astype(f32)
    columns = []

    def slots(owner, named):
        owner_c = owner.T
        rank = jnp.sum(jnp.where((owner == owner_c) & (sub < lane), 1.0, 0.0), 0, keepdims=True)
        edges = []
        for s in range(2):
            here = (owner == owner_id) & (wide(rank) == float(s))
            columns.append(jnp.sum(jnp.where(here, named + 1.0, 0.0), 1, keepdims=True) - 1.0)
            columns.append(jnp.sum(jnp.where(here, rel, 0.0), 1, keepdims=True))
            edges.append(
                jnp.sum(jnp.where(here, lane.astype(f32) + 1.0, 0.0), 1, keepdims=True) - 1.0
            )
        return jnp.where(lane == 0, edges[0], jnp.where(lane == 1, edges[1], -1.0))

    edges = slots(head_owner, head_row)
    edges = jnp.where(lane == 2, columns[1], jnp.where(lane == 3, columns[3], edges))
    head_edge[...] = edges
    tail_edge[...] = slots(tail_owner, tail_row)

    copy.wait()
    line = []
    for i in range(2):
        half = spread(block, (i,)).T
        picked = lax.broadcasted_iota(jnp.int32, (n, 256), 0) == neg_at % n
        line.append(jnp.sum(jnp.where(picked, half, 0.0), 0, keepdims=True))
    even = sub % 2 == 0
    send[pl.ds(0, n, stride=TILES1), :] = jnp.where(even, wide(line[0][:, :n]), wide(line[1][:, :n]))
    tile = jnp.where(even, wide(line[0][:, n:]), wide(line[1][:, n:]))
    for j, col in enumerate(columns):
        tile = jnp.where(lane == ASKS + j, col, tile)
    send[pl.ds(1, n, stride=TILES1), :] = tile


def ahead_kernel(table_t, relations, head_edge, *outs):
    whole = spread(table_t[...], (0, 1)).T
    for ref, piece in zip(outs[:PIECES], parts(whole, PIECES), strict=True):
        ref[...] = piece
    pad = jnp.zeros((64, 56), f32)
    whole = jnp.concatenate([relations[:, :200], pad, relations[:, 200:], pad], 1)
    whole = jnp.concatenate([quarter(whole, q) for q in range(4)], 1)
    pieces = parts(whole, PIECES)
    for ref, piece in zip(outs[PIECES:-1], pieces, strict=True):
        ref[...] = piece
    ids = jnp.concatenate([head_edge[:, 2:3], head_edge[:, 3:4]], 0)
    hot = jnp.where(lanes((2 * LANE, 64)).astype(f32) == ids, 1.0, 0.0).astype(bf16)
    outs[-1][...] = pick(hot, pieces, NN)


def pair_kernel(head_edge, tail_edge, rels, out):
    n = 2 * LANE
    out[0:n, :], out[n : 2 * n, :] = factors(rels[...], True)

    def stack(ref, by_rows):
        if by_rows:
            turned = ref[...].T
            return jnp.concatenate([turned[0:1, :], turned[1:2, :]], 1)
        return jnp.concatenate([ref[:, 0:1], ref[:, 1:2]], 0)

    for i, (one, other) in enumerate(((head_edge, tail_edge), (tail_edge, head_edge))):
        col, row = stack(one, False), stack(other, True)
        out[2 * n :, i * n : (i + 1) * n] = jnp.where((col == row) & (col >= 0.0), 1.0, 0.0)


def rel_vectors(tile, slots, pieces):
    ids = jnp.concatenate([column(tile, ASKS + 2 * s + 1) for s in slots], 0)
    hot = jnp.where(lanes((ids.shape[0], 64)).astype(f32) == ids, 1.0, 0.0).astype(bf16)
    return pick(hot, [p[...] for p in pieces], NN)


def fetch_kernel(recv, *refs):
    n = LANE
    table, rel = refs[:PIECES], refs[PIECES : 2 * PIECES]
    send, rows, negs, stage, done = refs[2 * PIECES :]
    negs[...] = recv[...]
    tile = recv[pl.ds(1, n, stride=TILES1), :]
    packed = []
    for side in range(2):
        slots = (2 * side, 2 * side + 1)
        at = jnp.concatenate([column(tile, ASKS + 2 * s) for s in slots], 0)
        hot = jnp.where(lanes((2 * n, 512)).astype(f32) == at, 1.0, 0.0).astype(bf16)
        vec = pick(hot, [p[...] for p in table], NN)
        if side == 0:
            vec = cmul(vec, rel_vectors(tile, slots, rel))
        packed += [vec[:n, :], vec[n:, :]]
        rows[2 * n * side : 2 * n * (side + 1), :] = vec

    def write(c):
        part = n // 4
        pack(stage, [x[c * part : (c + 1) * part, :] for x in packed], c * part * TILES2)

    in_parts(write, n // 4 * TILES2, stage, send, done)


def negatives_kernel(odd, recv, rows, *refs):
    n = LANE
    rel = refs[:PIECES]
    mine, other, back, keep, give = refs[PIECES:]
    tile = recv[pl.ds(1, n, stride=TILES1), :]
    at = lanes((n, LANE))
    low = lanes((4 * n, LANE)) < 64

    def half(ref):
        first = [ref[pl.ds(TILES1 * n * j, n, stride=TILES1), :] for j in range(4)]
        second = [ref[pl.ds(TILES1 * n * j + 1, n, stride=TILES1), :] for j in range(4)]
        second = [jnp.where(at < ASKS, x, 0.0) for x in second]
        return jnp.concatenate(first, 0), jnp.concatenate(second, 0)

    flip = odd[0] > 0
    negs = []
    for own, got in zip(half(mine), half(other)):
        re, im = jnp.where(flip, got, own), jnp.where(flip, own, got)
        negs.append(jnp.where(low, re, pltpu.roll(im, 64, 1)))
        negs.append(jnp.where(low, pltpu.roll(re, 64, 1), im))
    negs = jnp.concatenate(negs, 1)
    probe = cmul(rows[2 * n :, :], rel_vectors(tile, (2, 3), rel), True)
    x = jnp.concatenate([rows[0 : 2 * n, :], probe], 0)
    valid = jnp.concatenate([column(tile, ASKS + 2 * s) for s in range(4)], 0)
    coef = sigmoid(dot3(x, negs, NT)) * (1.0 / math.sqrt(512.0))
    coef = jnp.where(valid >= 0.0, coef, 0.0)
    back[...] = dot3(coef, negs, NN)
    total = dot3(coef, x, TN)
    for i in range(2):
        first, second = tile_of(total, 2 * i), tile_of(total, 2 * i + 1)
        re = jnp.where(low, first, pltpu.roll(second, 64, 1))
        im = jnp.where(low, pltpu.roll(first, 64, 1), second)
        keep[:, i * n : (i + 1) * n] = jnp.where(flip, im, re)
        give[:, i * n : (i + 1) * n] = jnp.where(flip, re, im)


def fold_kernel(rep, keep, got, *outs):
    for i, ref in enumerate(outs):
        at = pl.ds(pl.multiple_of((rep[0] + i) % 4 * LANE, LANE), LANE)
        ref[...] = keep[at, :] + got[at, :]


def edge_kernel(recv, aids, sum0, sum1, sum2, sum3, send, token, stage, done):
    n = LANE
    slots = unpack(recv, n)
    query, tails = jnp.concatenate(slots[:2], 0), jnp.concatenate(slots[2:], 0)
    met = pick(aids[4 * n :, 0 : 2 * n].astype(bf16), parts(tails, PIECES), NN)
    pos = jnp.sum(query * met, 1, keepdims=True)
    coef = -sigmoid(-pos)
    met = coef * met
    to_head = met * aids[0 : 2 * n, :] + turn(met) * aids[2 * n : 4 * n, :]
    to_tail = pick(aids[4 * n :, 2 * n :].astype(bf16), parts(coef * query, PIECES), NN)
    neg = sum0[...] + sum1[...] + (sum2[...] + sum3[...])
    token[...] = neg[0:8, 0:128]
    part = n // 4
    at = lanes((part, LANE))

    def write(c):
        rows = slice(c * part, (c + 1) * part)
        for q in range(4):
            words = tile_of(neg[rows, :], q // 2)
            if q % 2:
                words = pltpu.roll(words, 64, 1)
            words = jnp.where(at < 64, words, pltpu.roll(words, 32, 1))
            for s, block in enumerate((to_head[:n], to_head[n:], to_tail[:n], to_tail[n:])):
                moved = pltpu.roll(words, 56 - 8 * s, 1)
                first = c * part * 4 * TILES3 + 4 * q + s
                stage[pl.ds(first, part, stride=4 * TILES3), :] = jnp.where(
                    at % 64 < 56, tile_of(block[rows, :], q), moved
                )

    in_parts(write, part * 4 * TILES3, stage, send, done)


def local_kernel(rep, token, asks, back, *refs):
    n = 2 * LANE
    *rel, out0, out1, out2, out3, quarters = refs
    tile = asks[pl.ds(1, LANE, stride=TILES1), :]
    turned = tile.T
    sub = lax.broadcasted_iota(jnp.int32, (512, LANE), 0).astype(f32)
    hot = jnp.concatenate(
        [
            jnp.where(sub == turned[ASKS + 2 * s : ASKS + 2 * s + 1, :], 1.0, 0.0).astype(bf16)
            for s in range(4)
        ],
        1,
    )
    head = cmul(back[0:n, :], rel_vectors(tile, (0, 1), rel), True)
    tail = cmul(back[n:, :], rel_vectors(tile, (2, 3), rel))
    grad = jnp.concatenate([head, tail], 0)
    total = pick(hot, parts(grad, PIECES), NN)
    for q in range(4):
        quarters[q] = tile_of(total, q)
    for i, ref in enumerate((out0, out1, out2, out3)):
        ref[...] = quarters[(rep[0] + i) % 4]


def gather_local_kernel(part0, part1, part2, part3, out):
    out[...] = part0[...] + part1[...] + (part2[...] + part3[...])


def place_kernel(neg_rows, asks, token, hot):
    n = LANE
    sub = lax.broadcasted_iota(jnp.int32, (512, n), 0).astype(f32)
    for x in range(4):
        turned = asks[pl.ds(x * TILES1 * n + 1, n, stride=TILES1), :].T
        for s in range(4):
            at = turned[ASKS + 2 * s : ASKS + 2 * s + 1, :]
            b = 4 * x + s
            hot[:, b * n : (b + 1) * n] = jnp.where(sub == at, 1.0, 0.0).astype(bf16)
    at = jnp.full((1, n), -1.0, f32)
    for x in range(4):
        at = jnp.where(lanes((1, n)) == x, neg_rows[x].astype(f32), at)
    hot[:, 16 * n :] = jnp.where(sub == at, 1.0, 0.0).astype(bf16)


def scatter_kernel(recv, hot, local, out):
    n = LANE
    even = lax.broadcasted_iota(jnp.int32, (n, n), 0) % 2 == 0
    which = lax.broadcasted_iota(jnp.int32, (8, n), 0)
    sums = [[jnp.zeros((8, n), f32) for _ in range(2)] for _ in range(4)]
    blocks = []
    for x in range(4):
        for s in range(4):
            tile = recv[pl.ds(4 * x + s, n, stride=4 * TILES3), :]
            reals = jnp.sum(jnp.where(even, tile, 0.0), 0, keepdims=True)
            imags = jnp.sum(jnp.where(even, 0.0, tile), 0, keepdims=True)
            sums[s] = [
                jnp.where(which == x, new, old) for old, new in zip(sums[s], (reals, imags))
            ]
            blocks.append(tile)
    neg = jnp.zeros((8, n), f32)
    lane = lanes((8, n))
    for s in range(4):
        for i in range(2):
            word = 32 * i + 8 * s
            if word < 56:
                for side in range(2):
                    goal = 64 * side + word
                    shift = (goal - (56 + 64 * i)) % n
                    moved = pltpu.roll(sums[s][side], shift, 1) if shift else sums[s][side]
                    neg = jnp.where((lane >= goal) & (lane < goal + 8), moved, neg)
    blocks += [neg, jnp.zeros((n - 8, n), f32)]
    both = jnp.concatenate(parts(jnp.concatenate(blocks, 0), 2), 1)
    total = dot(hot[...], both, NN)
    turned = (total[:, :n] + total[:, n:] + local[...]).T
    out[0:56, :] = turned[0:56, :]
    out[56:112, :] = turned[64:120, :]


def finish_kernel(grads, table_t, state, table_new, state_new):
    spans = [
        (q * 112 + i * 56, i * 200 + STARTS[q], SIZES[q]) for q in range(4) for i in range(2)
    ]
    total = jnp.zeros((1, 512), f32)
    for at, _, size in spans:
        grad = grads[at : at + size, :]
        total = total + jnp.sum(grad * grad, 0, keepdims=True)
    new = state[...] + total * (1.0 / 400.0)
    state_new[...] = new
    step = learn_rate / jnp.sqrt(new)
    for at, to, size in spans:
        table_new[to : to + size, :] = table_t[to : to + size, :] - grads[at : at + size, :] * step


def call(kernel, outs, args, scalars=(), name=None, scratch=(), whole=0, direct=0):
    space = pl.BlockSpec(memory_space=pltpu.VMEM)
    return pl.pallas_call(
        kernel,
        out_shape=[
            (pltpu.VMEM if near else pltpu.HBM)(shape, kind)
            for shape, kind, near in outs
        ],
        in_specs=[pl.BlockSpec(memory_space=pltpu.SMEM)] * len(scalars)
        + [space] * (len(args) - whole)
        + [pl.BlockSpec(memory_space=pltpu.HBM)] * whole,
        out_specs=[pl.BlockSpec(memory_space=pltpu.HBM)] * direct + [space] * (len(outs) - direct),
        scratch_shapes=list(scratch),
        compiler_params=pltpu.CompilerParams(vmem_limit_bytes=24 << 20),
        name=name,
    )(*scalars, *args)


def near(x):
    return pltpu.with_memory_space_constraint(x, pltpu.VMEM)


def far(x):
    return pltpu.with_memory_space_constraint(x, pltpu.HBM)


def exchange(x, axis, tiles):
    n = x.shape[0] // tiles
    x = x.reshape(n, 1, tiles * LANE)
    x = lax.all_to_all(x, axis, split_axis=0, concat_axis=0, tiled=True)
    return x.reshape(n * tiles, LANE)


def shift(x, by):
    n = lax.axis_size("rep")
    return lax.ppermute(x, "rep", [(i, (i + by) % n) for i in range(n)])


def swap_cores(x):
    return lax.ppermute(x, "ent", [(i, i ^ 1) for i in range(lax.axis_size("ent"))])


def on_device(
    entity_table,
    adagrad_state,
    head_owner,
    head_row,
    relation_ids,
    tail_owner,
    tail_row,
    neg_rows,
    relations,
):
    rep = lax.axis_index("rep").reshape(1).astype(jnp.int32)
    odd = (lax.axis_index("ent") & 1).reshape(1).astype(jnp.int32)
    table_t = entity_table.T
    neg_rows = far(neg_rows)
    n = LANE

    def line(x):
        return far(x.reshape(1, n))

    send1, head_edge, tail_edge = call(
        ask_kernel,
        [((n * TILES1, n), f32, False), ((n, n), f32, False), ((n, n), f32, False)],
        (
            line(head_owner),
            line(head_row),
            line(relation_ids),
            line(tail_owner),
            line(tail_row),
            far(table_t),
        ),
        (rep, neg_rows),
        "ask",
        (pltpu.VMEM((400, n), f32), pltpu.SemaphoreType.DMA),
        1,
    )
    recv1 = exchange(send1, "ent", TILES1)
    *pieces, edge_rels = call(
        ahead_kernel,
        [((4 * n, 512), bf16, True)] * PIECES
        + [((64, 512), bf16, True)] * PIECES
        + [((2 * n, 512), f32, True)],
        (table_t, relations, far(head_edge)),
        name="ahead",
    )
    (aids,) = call(
        pair_kernel,
        [((6 * n, 512), f32, True)],
        (far(head_edge), far(tail_edge), far(edge_rels)),
        name="pair",
    )
    rel_pieces = pieces[PIECES:]
    send2, rows, own_negs = call(
        fetch_kernel,
        [
            ((n * TILES2, n), f32, False),
            ((4 * n, 512), f32, True),
            ((n * TILES1, n), f32, True),
        ],
        (near(recv1), *map(near, pieces)),
        name="fetch",
        scratch=(pltpu.VMEM((n * TILES2, n), f32), pltpu.SemaphoreType.DMA((4,))),
        direct=1,
    )
    recv2 = exchange(send2, "ent", TILES2)
    mine = lax.all_gather(own_negs, "rep", axis=0, tiled=True)
    other = swap_cores(mine)
    back, keep, give = call(
        negatives_kernel,
        [((4 * n, 512), f32, True)] + [((4 * n, 256), f32, True)] * 2,
        (near(recv1), near(rows), *map(far, rel_pieces), near(mine), near(other)),
        (odd,),
        "negatives",
    )
    owned = call(
        fold_kernel,
        [((n, 256), f32, True)] * 4,
        (near(keep), near(swap_cores(give))),
        (rep,),
        "fold",
    )
    sums = [owned[0]] + [shift(owned[j], j) for j in (1, 2, 3)]
    send3, token = call(
        edge_kernel,
        [((4 * n * TILES3, n), f32, False), ((8, n), f32, False)],
        (near(recv2), near(aids), far(sums[0]), *map(near, sums[1:])),
        name="edge",
        scratch=(pltpu.VMEM((4 * n * TILES3, n), f32), pltpu.SemaphoreType.DMA((4,))),
        direct=1,
    )
    recv3 = exchange(send3, ("ent", "rep"), TILES3)
    token = far(token)
    local = call(
        local_kernel,
        [((4 * n, n), f32, True)] * 4,
        (token, recv1, far(back), *map(far, rel_pieces)),
        (rep,),
        "local",
        (pltpu.VMEM((4, 4 * n, n), f32),),
    )
    (local,) = call(
        gather_local_kernel,
        [((4 * n, n), f32, True)],
        [far(local[0])] + [far(shift(local[j], j)) for j in (1, 2, 3)],
        name="gather_local",
    )
    (hot,) = call(
        place_kernel, [((4 * n, 17 * n), bf16, True)], (far(mine), token), (neg_rows,), "place"
    )
    (grads,) = call(
        scatter_kernel,
        [((112, 512), f32, True)],
        (near(recv3), near(hot), near(local)),
        name="scatter",
    )
    grads = lax.all_gather(grads, "rep", axis=0, tiled=True)
    table_new, state_new = call(
        finish_kernel,
        [((400, 512), f32, False), ((1, 512), f32, False)],
        (near(grads), table_t, adagrad_state.reshape(1, 512)),
        name="finish",
    )
    return (table_new.T, state_new.reshape(512))


def solution(mesh):
    placed = (
        P("ent", None),
        P("ent"),
        P(("ent", "rep"), None),
        P(("ent", "rep")),
        P(("ent", "rep")),
        P(("ent", "rep"), None),
        P(("ent", "rep")),
        P("ent"),
        P(),
    )
    return jax.shard_map(
        on_device, mesh=mesh, in_specs=placed, out_specs=(P("ent", None), P("ent")), check_vma=False
    )
```

```python
import math

import jax
import jax.numpy as jnp
from jax import lax
from jax.experimental import pallas as pl
from jax.experimental.pallas import tpu as pltpu
from jax.sharding import PartitionSpec as P

learn_rate = 0.1

LANE = 128
f32 = jnp.float32
bf16 = jnp.bfloat16
NN = (((1,), (0,)), ((), ()))
NT = (((1,), (1,)), ((), ()))
TN = (((0,), (0,)), ((), ()))
PIECES = 2
TILES1 = 2
TILES2 = 13
TILES3 = 4
ASKS = 112
STARTS = (0, 56, 104, 152)
SIZES = (56, 48, 48, 48)


def dot(a, b, dims):
    return lax.dot_general(a, b, dims, preferred_element_type=f32)


def parts(x, count):
    out = []
    for _ in range(count):
        head = x.astype(bf16)
        out.append(head)
        x = x - head.astype(f32)
    return out


def pick(onehot, pieces, dims):
    total = dot(onehot, pieces[0], dims)
    for piece in pieces[1:]:
        total = total + dot(onehot, piece, dims)
    return total


def dot3(a, b, dims):
    a0, a1 = parts(a, 2)
    b0, b1 = parts(b, 2)
    return dot(a0, b0, dims) + (dot(a0, b1, dims) + dot(a1, b0, dims))


def lanes(shape):
    return lax.broadcasted_iota(jnp.int32, shape, len(shape) - 1)


def tile_of(x, q):
    return x[:, q * LANE : (q + 1) * LANE]


def turn(x):
    return jnp.concatenate([pltpu.roll(tile_of(x, q), 64, 1) for q in range(4)], 1)


def factors(b, conj=False):
    low = lanes(b.shape) % LANE < 64
    other = turn(b)
    second = jnp.where(low, other, -b) if conj else jnp.where(low, -other, b)
    return jnp.where(low, b, other), second


def cmul(a, b, conj=False):
    first, second = factors(b, conj)
    return a * first + turn(a) * second


def sigmoid(x):
    return 1.0 / (1.0 + jnp.exp(-x))


def column(tile, lane):
    return jnp.sum(jnp.where(lanes(tile.shape) == lane, tile, 0.0), 1, keepdims=True)


def pack(ref, slots):
    n = slots[0].shape[0]
    at = lanes((n, LANE)) % 64
    tail = jnp.zeros((n, LANE), f32)
    for s, slot in enumerate(slots):
        first = tile_of(slot, 0)
        for j in range(1, 4):
            moved = pltpu.roll(first, 64 - 16 * j, 1)
            ref[pl.ds(3 * s + j - 1, n, stride=TILES2), :] = jnp.where(
                at < 48, tile_of(slot, j), moved
            )
        moved = pltpu.roll(first, (8 * s - 48) % LANE, 1)
        tail = jnp.where((at >= 8 * s) & (at < 8 * s + 8), moved, tail)
    ref[pl.ds(12, n, stride=TILES2), :] = tail


def unpack(ref, n):
    at = lanes((n, LANE)) % 64
    tail = ref[pl.ds(12, n, stride=TILES2), :]
    out = []
    for s in range(4):
        first = jnp.where(at < 56, pltpu.roll(tail, 48 - 8 * s, 1), 0.0)
        others = []
        for j in range(3, 0, -1):
            dense = ref[pl.ds(3 * s + j - 1, n, stride=TILES2), :]
            first = jnp.where(at < 16 * j, pltpu.roll(dense, 64 + 16 * j, 1), first)
            others.append(jnp.where(at < 48, dense, 0.0))
        out.append(jnp.concatenate([first] + others[::-1], 1))
    return out


def window(into, low, high, start, size, dest):
    at = lanes(into.shape)
    for src, first in ((low, 0), (high, LANE)):
        begin, end = max(start, first), min(start + size, first + LANE)
        if begin < end:
            goal = dest + begin - start
            shift = (goal - (begin - first)) % LANE
            moved = pltpu.roll(src, shift, 1) if shift else src
            into = jnp.where((at >= goal) & (at < goal + end - begin), moved, into)
    return into


def quarter(wide, q):
    out = jnp.zeros((wide.shape[0], LANE), f32)
    for i in range(2):
        low, high = (wide[:, (2 * i + j) * LANE : (2 * i + j + 1) * LANE] for j in range(2))
        out = window(out, low, high, STARTS[q], SIZES[q], 64 * i)
    return out


def spread(rows, sides):
    out = []
    for q in range(4):
        for i in sides:
            at = 200 * i + STARTS[q]
            out.append(rows[at : at + SIZES[q], :])
            out.append(jnp.zeros((64 - SIZES[q], rows.shape[1]), f32))
    return jnp.concatenate(out, 0)


def ask_kernel(
    rep, neg_rows, head_owner, head_row, rel, tail_owner, tail_row, table_t,
    send, head_edge, tail_edge, block, done,
):
    n = LANE
    neg_at = neg_rows[rep[0]]
    copy = pltpu.make_async_copy(
        table_t.at[:, pl.ds(pl.multiple_of(neg_at // n * n, n), n)], block, done
    )
    copy.start()
    sub = lax.broadcasted_iota(jnp.int32, (n, n), 0)
    lane = lanes((n, n))

    def wide(x):
        return jnp.broadcast_to(x, (n, x.shape[1]))

    head_owner, head_row, rel, tail_owner, tail_row = (
        wide(ref[...].astype(f32)) for ref in (head_owner, head_row, rel, tail_owner, tail_row)
    )
    owner_id = sub.astype(f32)
    columns = []

    def slots(owner, named):
        owner_c = owner.T
        rank = jnp.sum(jnp.where((owner == owner_c) & (sub < lane), 1.0, 0.0), 0, keepdims=True)
        edges = []
        for s in range(2):
            here = (owner == owner_id) & (wide(rank) == float(s))
            columns.append(jnp.sum(jnp.where(here, named + 1.0, 0.0), 1, keepdims=True) - 1.0)
            columns.append(jnp.sum(jnp.where(here, rel, 0.0), 1, keepdims=True))
            edges.append(
                jnp.sum(jnp.where(here, lane.astype(f32) + 1.0, 0.0), 1, keepdims=True) - 1.0
            )
        return jnp.where(lane == 0, edges[0], jnp.where(lane == 1, edges[1], -1.0))

    edges = slots(head_owner, head_row)
    edges = jnp.where(lane == 2, columns[1], jnp.where(lane == 3, columns[3], edges))
    head_edge[...] = edges
    tail_edge[...] = slots(tail_owner, tail_row)

    copy.wait()
    line = []
    for i in range(2):
        half = spread(block, (i,)).T
        picked = lax.broadcasted_iota(jnp.int32, (n, 256), 0) == neg_at % n
        line.append(jnp.sum(jnp.where(picked, half, 0.0), 0, keepdims=True))
    even = sub % 2 == 0
    send[pl.ds(0, n, stride=TILES1), :] = jnp.where(even, wide(line[0][:, :n]), wide(line[1][:, :n]))
    tile = jnp.where(even, wide(line[0][:, n:]), wide(line[1][:, n:]))
    for j, col in enumerate(columns):
        tile = jnp.where(lane == ASKS + j, col, tile)
    send[pl.ds(1, n, stride=TILES1), :] = tile


def ahead_kernel(table_t, relations, head_edge, *outs):
    whole = spread(table_t[...], (0, 1)).T
    for ref, piece in zip(outs[:PIECES], parts(whole, PIECES), strict=True):
        ref[...] = piece
    pad = jnp.zeros((64, 56), f32)
    whole = jnp.concatenate([relations[:, :200], pad, relations[:, 200:], pad], 1)
    whole = jnp.concatenate([quarter(whole, q) for q in range(4)], 1)
    pieces = parts(whole, PIECES)
    for ref, piece in zip(outs[PIECES:-1], pieces, strict=True):
        ref[...] = piece
    ids = jnp.concatenate([head_edge[:, 2:3], head_edge[:, 3:4]], 0)
    hot = jnp.where(lanes((2 * LANE, 64)).astype(f32) == ids, 1.0, 0.0).astype(bf16)
    outs[-1][...] = pick(hot, pieces, NN)


def pair_kernel(head_edge, tail_edge, rels, neg, out):
    n = 2 * LANE
    out[0:n, :], out[n : 2 * n, :] = factors(rels[...], True)

    def stack(ref, by_rows):
        if by_rows:
            turned = ref[...].T
            return jnp.concatenate([turned[0:1, :], turned[1:2, :]], 1)
        return jnp.concatenate([ref[:, 0:1], ref[:, 1:2]], 0)

    for i, (one, other) in enumerate(((head_edge, tail_edge), (tail_edge, head_edge))):
        col, row = stack(one, False), stack(other, True)
        out[2 * n : 3 * n, i * n : (i + 1) * n] = jnp.where(
            (col == row) & (col >= 0.0), 1.0, 0.0
        )
    out[3 * n :, 0:n] = neg[...]
    out[3 * n :, n:] = jnp.zeros((LANE, n), f32)


def rel_vectors(tile, slots, pieces):
    ids = jnp.concatenate([column(tile, ASKS + 2 * s + 1) for s in slots], 0)
    hot = jnp.where(lanes((ids.shape[0], 64)).astype(f32) == ids, 1.0, 0.0).astype(bf16)
    return pick(hot, [p[...] for p in pieces], NN)


def fetch_kernel(recv, *refs):
    n = LANE
    table, rel = refs[:PIECES], refs[PIECES : 2 * PIECES]
    send, rows, negs = refs[2 * PIECES :]
    negs[...] = recv[...]
    tile = recv[pl.ds(1, n, stride=TILES1), :]
    packed = []
    for side in range(2):
        slots = (2 * side, 2 * side + 1)
        at = jnp.concatenate([column(tile, ASKS + 2 * s) for s in slots], 0)
        hot = jnp.where(lanes((2 * n, 512)).astype(f32) == at, 1.0, 0.0).astype(bf16)
        vec = pick(hot, [p[...] for p in table], NN)
        if side == 0:
            vec = cmul(vec, rel_vectors(tile, slots, rel))
        packed += [vec[:n, :], vec[n:, :]]
        rows[2 * n * side : 2 * n * (side + 1), :] = vec
    pack(send, packed)


def negatives_kernel(odd, recv, rows, *refs):
    n = LANE
    rel = refs[:PIECES]
    mine, other, back, keep, give = refs[PIECES:]
    tile = recv[pl.ds(1, n, stride=TILES1), :]
    at = lanes((n, LANE))
    low = lanes((4 * n, LANE)) < 64

    def half(ref):
        first = [ref[pl.ds(TILES1 * n * j, n, stride=TILES1), :] for j in range(4)]
        second = [ref[pl.ds(TILES1 * n * j + 1, n, stride=TILES1), :] for j in range(4)]
        second = [jnp.where(at < ASKS, x, 0.0) for x in second]
        return jnp.concatenate(first, 0), jnp.concatenate(second, 0)

    flip = odd[0] > 0
    negs = []
    for own, got in zip(half(mine), half(other)):
        re, im = jnp.where(flip, got, own), jnp.where(flip, own, got)
        negs.append(jnp.where(low, re, pltpu.roll(im, 64, 1)))
        negs.append(jnp.where(low, pltpu.roll(re, 64, 1), im))
    negs = jnp.concatenate(negs, 1)
    probe = cmul(rows[2 * n :, :], rel_vectors(tile, (2, 3), rel), True)
    x = jnp.concatenate([rows[0 : 2 * n, :], probe], 0)
    valid = jnp.concatenate([column(tile, ASKS + 2 * s) for s in range(4)], 0)
    coef = sigmoid(dot3(x, negs, NT)) * (1.0 / math.sqrt(512.0))
    coef = jnp.where(valid >= 0.0, coef, 0.0)
    back[...] = dot3(coef, negs, NN)
    total = dot3(coef, x, TN)
    for i in range(2):
        first, second = tile_of(total, 2 * i), tile_of(total, 2 * i + 1)
        re = jnp.where(low, first, pltpu.roll(second, 64, 1))
        im = jnp.where(low, pltpu.roll(first, 64, 1), second)
        keep[:, i * n : (i + 1) * n] = jnp.where(flip, im, re)
        give[:, i * n : (i + 1) * n] = jnp.where(flip, re, im)


def fold_kernel(rep, keep, got, *outs):
    for i, ref in enumerate(outs):
        at = pl.ds(pl.multiple_of((rep[0] + i) % 4 * LANE, LANE), LANE)
        ref[...] = keep[at, :] + got[at, :]


def edge_kernel(recv, aids, sum1, sum2, sum3, send, token):
    n = LANE
    slots = unpack(recv, n)
    query, tails = jnp.concatenate(slots[:2], 0), jnp.concatenate(slots[2:], 0)
    met = pick(aids[4 * n : 6 * n, 0 : 2 * n].astype(bf16), parts(tails, PIECES), NN)
    pos = jnp.sum(query * met, 1, keepdims=True)
    coef = -sigmoid(-pos)
    met = coef * met
    to_head = met * aids[0 : 2 * n, :] + turn(met) * aids[2 * n : 4 * n, :]
    to_tail = pick(aids[4 * n : 6 * n, 2 * n :].astype(bf16), parts(coef * query, PIECES), NN)
    neg = aids[6 * n :, 0 : 2 * n] + sum1[...] + (sum2[...] + sum3[...])
    at = lanes((n, LANE))
    for q in range(4):
        words = tile_of(neg, q // 2)
        if q % 2:
            words = pltpu.roll(words, 64, 1)
        words = jnp.where(at < 64, words, pltpu.roll(words, 32, 1))
        for s, block in enumerate((to_head[:n], to_head[n:], to_tail[:n], to_tail[n:])):
            moved = pltpu.roll(words, 56 - 8 * s, 1)
            send[pl.ds(4 * q + s, n, stride=4 * TILES3), :] = jnp.where(
                at % 64 < 56, tile_of(block, q), moved
            )
    token[...] = neg[0:8, 0:128]


def local_kernel(rep, token, asks, back, *refs):
    n = 2 * LANE
    *rel, out0, out1, out2, out3, quarters = refs
    tile = asks[pl.ds(1, LANE, stride=TILES1), :]
    turned = tile.T
    sub = lax.broadcasted_iota(jnp.int32, (512, LANE), 0).astype(f32)
    hot = jnp.concatenate(
        [
            jnp.where(sub == turned[ASKS + 2 * s : ASKS + 2 * s + 1, :], 1.0, 0.0).astype(bf16)
            for s in range(4)
        ],
        1,
    )
    head = cmul(back[0:n, :], rel_vectors(tile, (0, 1), rel), True)
    tail = cmul(back[n:, :], rel_vectors(tile, (2, 3), rel))
    grad = jnp.concatenate([head, tail], 0)
    total = pick(hot, parts(grad, PIECES), NN)
    for q in range(4):
        quarters[q] = tile_of(total, q)
    for i, ref in enumerate((out0, out1, out2, out3)):
        ref[...] = quarters[(rep[0] + i) % 4]


def gather_local_kernel(part0, part1, part2, part3, out):
    out[...] = part0[...] + part1[...] + (part2[...] + part3[...])


def place_kernel(neg_rows, asks, token, hot):
    n = LANE
    sub = lax.broadcasted_iota(jnp.int32, (512, n), 0).astype(f32)
    for x in range(4):
        turned = asks[pl.ds(x * TILES1 * n + 1, n, stride=TILES1), :].T
        for s in range(4):
            at = turned[ASKS + 2 * s : ASKS + 2 * s + 1, :]
            b = 4 * x + s
            hot[:, b * n : (b + 1) * n] = jnp.where(sub == at, 1.0, 0.0).astype(bf16)
    at = jnp.full((1, n), -1.0, f32)
    for x in range(4):
        at = jnp.where(lanes((1, n)) == x, neg_rows[x].astype(f32), at)
    hot[:, 16 * n :] = jnp.where(sub == at, 1.0, 0.0).astype(bf16)


def scatter_kernel(recv, hot, local, out):
    n = LANE
    even = lax.broadcasted_iota(jnp.int32, (n, n), 0) % 2 == 0
    which = lax.broadcasted_iota(jnp.int32, (8, n), 0)
    sums = [[jnp.zeros((8, n), f32) for _ in range(2)] for _ in range(4)]
    blocks = []
    for x in range(4):
        for s in range(4):
            tile = recv[pl.ds(4 * x + s, n, stride=4 * TILES3), :]
            reals = jnp.sum(jnp.where(even, tile, 0.0), 0, keepdims=True)
            imags = jnp.sum(jnp.where(even, 0.0, tile), 0, keepdims=True)
            sums[s] = [
                jnp.where(which == x, new, old) for old, new in zip(sums[s], (reals, imags))
            ]
            blocks.append(tile)
    neg = jnp.zeros((8, n), f32)
    lane = lanes((8, n))
    for s in range(4):
        for i in range(2):
            word = 32 * i + 8 * s
            if word < 56:
                for side in range(2):
                    goal = 64 * side + word
                    shift = (goal - (56 + 64 * i)) % n
                    moved = pltpu.roll(sums[s][side], shift, 1) if shift else sums[s][side]
                    neg = jnp.where((lane >= goal) & (lane < goal + 8), moved, neg)
    blocks += [neg, jnp.zeros((n - 8, n), f32)]
    both = jnp.concatenate(parts(jnp.concatenate(blocks, 0), 2), 1)
    total = dot(hot[...], both, NN)
    turned = (total[:, :n] + total[:, n:] + local[...]).T
    out[0:56, :] = turned[0:56, :]
    out[56:112, :] = turned[64:120, :]


def finish_kernel(grads, table_t, state, table_new, state_new):
    spans = [
        (q * 112 + i * 56, i * 200 + STARTS[q], SIZES[q]) for q in range(4) for i in range(2)
    ]
    total = jnp.zeros((1, 512), f32)
    for at, _, size in spans:
        grad = grads[at : at + size, :]
        total = total + jnp.sum(grad * grad, 0, keepdims=True)
    new = state[...] + total * (1.0 / 400.0)
    state_new[...] = new
    step = learn_rate / jnp.sqrt(new)
    for at, to, size in spans:
        table_new[to : to + size, :] = table_t[to : to + size, :] - grads[at : at + size, :] * step


def call(kernel, outs, args, scalars=(), name=None, scratch=(), whole=0):
    space = pl.BlockSpec(memory_space=pltpu.VMEM)
    return pl.pallas_call(
        kernel,
        out_shape=[
            (pltpu.VMEM if near else pltpu.HBM)(shape, kind)
            for shape, kind, near in outs
        ],
        in_specs=[pl.BlockSpec(memory_space=pltpu.SMEM)] * len(scalars)
        + [space] * (len(args) - whole)
        + [pl.BlockSpec(memory_space=pltpu.HBM)] * whole,
        out_specs=[space] * len(outs),
        scratch_shapes=list(scratch),
        compiler_params=pltpu.CompilerParams(vmem_limit_bytes=24 << 20),
        name=name,
    )(*scalars, *args)


def near(x):
    return pltpu.with_memory_space_constraint(x, pltpu.VMEM)


def far(x):
    return pltpu.with_memory_space_constraint(x, pltpu.HBM)


def exchange(x, axis, tiles):
    n = x.shape[0] // tiles
    x = x.reshape(n, 1, tiles * LANE)
    x = lax.all_to_all(x, axis, split_axis=0, concat_axis=0, tiled=True)
    return x.reshape(n * tiles, LANE)


def shift(x, by):
    n = lax.axis_size("rep")
    return lax.ppermute(x, "rep", [(i, (i + by) % n) for i in range(n)])


def swap_cores(x):
    return lax.ppermute(x, "ent", [(i, i ^ 1) for i in range(lax.axis_size("ent"))])


def on_device(
    entity_table,
    adagrad_state,
    head_owner,
    head_row,
    relation_ids,
    tail_owner,
    tail_row,
    neg_rows,
    relations,
):
    rep = lax.axis_index("rep").reshape(1).astype(jnp.int32)
    odd = (lax.axis_index("ent") & 1).reshape(1).astype(jnp.int32)
    table_t = entity_table.T
    neg_rows = far(neg_rows)
    n = LANE

    def line(x):
        return far(x.reshape(1, n))

    send1, head_edge, tail_edge = call(
        ask_kernel,
        [((n * TILES1, n), f32, False), ((n, n), f32, False), ((n, n), f32, False)],
        (
            line(head_owner),
            line(head_row),
            line(relation_ids),
            line(tail_owner),
            line(tail_row),
            far(table_t),
        ),
        (rep, neg_rows),
        "ask",
        (pltpu.VMEM((400, n), f32), pltpu.SemaphoreType.DMA),
        1,
    )
    recv1 = exchange(send1, "ent", TILES1)
    *pieces, edge_rels = call(
        ahead_kernel,
        [((4 * n, 512), bf16, True)] * PIECES
        + [((64, 512), bf16, True)] * PIECES
        + [((2 * n, 512), f32, True)],
        (table_t, relations, far(head_edge)),
        name="ahead",
    )
    rel_pieces = pieces[PIECES:]
    send2, rows, own_negs = call(
        fetch_kernel,
        [
            ((n * TILES2, n), f32, False),
            ((4 * n, 512), f32, True),
            ((n * TILES1, n), f32, True),
        ],
        (near(recv1), *map(near, pieces)),
        name="fetch",
    )
    recv2 = exchange(send2, "ent", TILES2)
    mine = lax.all_gather(own_negs, "rep", axis=0, tiled=True)
    other = swap_cores(mine)
    back, keep, give = call(
        negatives_kernel,
        [((4 * n, 512), f32, True)] + [((4 * n, 256), f32, True)] * 2,
        (near(recv1), near(rows), *map(far, rel_pieces), near(mine), near(other)),
        (odd,),
        "negatives",
    )
    owned = call(
        fold_kernel,
        [((n, 256), f32, True)] * 4,
        (near(keep), near(swap_cores(give))),
        (rep,),
        "fold",
    )
    sums = [shift(owned[j], j) for j in (1, 2, 3)]
    (aids,) = call(
        pair_kernel,
        [((7 * n, 512), f32, True)],
        (far(head_edge), far(tail_edge), far(edge_rels), near(owned[0])),
        name="pair",
    )
    send3, token = call(
        edge_kernel,
        [((4 * n * TILES3, n), f32, False), ((8, n), f32, False)],
        (near(recv2), near(aids), *map(near, sums)),
        name="edge",
    )
    recv3 = exchange(send3, ("ent", "rep"), TILES3)
    token = far(token)
    local = call(
        local_kernel,
        [((4 * n, n), f32, True)] * 4,
        (token, recv1, far(back), *map(far, rel_pieces)),
        (rep,),
        "local",
        (pltpu.VMEM((4, 4 * n, n), f32),),
    )
    (local,) = call(
        gather_local_kernel,
        [((4 * n, n), f32, True)],
        [far(local[0])] + [far(shift(local[j], j)) for j in (1, 2, 3)],
        name="gather_local",
    )
    (hot,) = call(
        place_kernel, [((4 * n, 17 * n), bf16, True)], (far(mine), token), (neg_rows,), "place"
    )
    (grads,) = call(
        scatter_kernel,
        [((112, 512), f32, True)],
        (near(recv3), near(hot), near(local)),
        name="scatter",
    )
    grads = lax.all_gather(grads, "rep", axis=0, tiled=True)
    table_new, state_new = call(
        finish_kernel,
        [((400, 512), f32, False), ((1, 512), f32, False)],
        (near(grads), table_t, adagrad_state.reshape(1, 512)),
        name="finish",
    )
    return (table_new.T, state_new.reshape(512))


def solution(mesh):
    placed = (
        P("ent", None),
        P("ent"),
        P(("ent", "rep"), None),
        P(("ent", "rep")),
        P(("ent", "rep")),
        P(("ent", "rep"), None),
        P(("ent", "rep")),
        P("ent"),
        P(),
    )
    return jax.shard_map(
        on_device, mesh=mesh, in_specs=placed, out_specs=(P("ent", None), P("ent")), check_vma=False
    )
```

```python
import math

import jax
import jax.numpy as jnp
from jax import lax
from jax.experimental import pallas as pl
from jax.experimental.pallas import tpu as pltpu
from jax.sharding import PartitionSpec as P

learn_rate = 0.1

LANE = 128
f32 = jnp.float32
bf16 = jnp.bfloat16
NN = (((1,), (0,)), ((), ()))
NT = (((1,), (1,)), ((), ()))
TN = (((0,), (0,)), ((), ()))
PIECES = 2
TILES1 = 2
TILES2 = 13
TILES3 = 4
ASKS = 112
STARTS = (0, 56, 104, 152)
SIZES = (56, 48, 48, 48)


def dot(a, b, dims):
    return lax.dot_general(a, b, dims, preferred_element_type=f32)


def parts(x, count):
    out = []
    for _ in range(count):
        head = x.astype(bf16)
        out.append(head)
        x = x - head.astype(f32)
    return out


def pick(onehot, pieces, dims):
    total = dot(onehot, pieces[0], dims)
    for piece in pieces[1:]:
        total = total + dot(onehot, piece, dims)
    return total


def dot3(a, b, dims):
    a0, a1 = parts(a, 2)
    b0, b1 = parts(b, 2)
    return dot(a0, b0, dims) + (dot(a0, b1, dims) + dot(a1, b0, dims))


def lanes(shape):
    return lax.broadcasted_iota(jnp.int32, shape, len(shape) - 1)


def tile_of(x, q):
    return x[:, q * LANE : (q + 1) * LANE]


def turn(x):
    return jnp.concatenate([pltpu.roll(tile_of(x, q), 64, 1) for q in range(4)], 1)


def factors(b, conj=False):
    low = lanes(b.shape) % LANE < 64
    other = turn(b)
    second = jnp.where(low, other, -b) if conj else jnp.where(low, -other, b)
    return jnp.where(low, b, other), second


def cmul(a, b, conj=False):
    first, second = factors(b, conj)
    return a * first + turn(a) * second


def sigmoid(x):
    return 1.0 / (1.0 + jnp.exp(-x))


def column(tile, lane):
    return jnp.sum(jnp.where(lanes(tile.shape) == lane, tile, 0.0), 1, keepdims=True)


def pack(ref, slots):
    n = slots[0].shape[0]
    at = lanes((n, LANE)) % 64
    tail = jnp.zeros((n, LANE), f32)
    for s, slot in enumerate(slots):
        first = tile_of(slot, 0)
        for j in range(1, 4):
            moved = pltpu.roll(first, 64 - 16 * j, 1)
            ref[pl.ds(3 * s + j - 1, n, stride=TILES2), :] = jnp.where(
                at < 48, tile_of(slot, j), moved
            )
        moved = pltpu.roll(first, (8 * s - 48) % LANE, 1)
        tail = jnp.where((at >= 8 * s) & (at < 8 * s + 8), moved, tail)
    ref[pl.ds(12, n, stride=TILES2), :] = tail


def unpack(ref, n):
    at = lanes((n, LANE)) % 64
    tail = ref[pl.ds(12, n, stride=TILES2), :]
    out = []
    for s in range(4):
        first = jnp.where(at < 56, pltpu.roll(tail, 48 - 8 * s, 1), 0.0)
        others = []
        for j in range(3, 0, -1):
            dense = ref[pl.ds(3 * s + j - 1, n, stride=TILES2), :]
            first = jnp.where(at < 16 * j, pltpu.roll(dense, 64 + 16 * j, 1), first)
            others.append(jnp.where(at < 48, dense, 0.0))
        out.append(jnp.concatenate([first] + others[::-1], 1))
    return out


def window(into, low, high, start, size, dest):
    at = lanes(into.shape)
    for src, first in ((low, 0), (high, LANE)):
        begin, end = max(start, first), min(start + size, first + LANE)
        if begin < end:
            goal = dest + begin - start
            shift = (goal - (begin - first)) % LANE
            moved = pltpu.roll(src, shift, 1) if shift else src
            into = jnp.where((at >= goal) & (at < goal + end - begin), moved, into)
    return into


def quarter(wide, q):
    out = jnp.zeros((wide.shape[0], LANE), f32)
    for i in range(2):
        low, high = (wide[:, (2 * i + j) * LANE : (2 * i + j + 1) * LANE] for j in range(2))
        out = window(out, low, high, STARTS[q], SIZES[q], 64 * i)
    return out


def spread(rows, sides):
    out = []
    for q in range(4):
        for i in sides:
            at = 200 * i + STARTS[q]
            out.append(rows[at : at + SIZES[q], :])
            out.append(jnp.zeros((64 - SIZES[q], rows.shape[1]), f32))
    return jnp.concatenate(out, 0)


def ask_kernel(
    rep, neg_rows, head_owner, head_row, rel, tail_owner, tail_row, table_t,
    send, head_edge, tail_edge, block, done,
):
    n = LANE
    neg_at = neg_rows[rep[0]]
    copy = pltpu.make_async_copy(
        table_t.at[:, pl.ds(pl.multiple_of(neg_at // n * n, n), n)], block, done
    )
    copy.start()
    sub = lax.broadcasted_iota(jnp.int32, (n, n), 0)
    lane = lanes((n, n))

    def wide(x):
        return jnp.broadcast_to(x, (n, x.shape[1]))

    head_owner, head_row, rel, tail_owner, tail_row = (
        wide(ref[...].astype(f32)) for ref in (head_owner, head_row, rel, tail_owner, tail_row)
    )
    owner_id = sub.astype(f32)
    columns = []

    def slots(owner, named):
        owner_c = owner.T
        rank = jnp.sum(jnp.where((owner == owner_c) & (sub < lane), 1.0, 0.0), 0, keepdims=True)
        edges = []
        for s in range(2):
            here = (owner == owner_id) & (wide(rank) == float(s))
            columns.append(jnp.sum(jnp.where(here, named + 1.0, 0.0), 1, keepdims=True) - 1.0)
            columns.append(jnp.sum(jnp.where(here, rel, 0.0), 1, keepdims=True))
            edges.append(
                jnp.sum(jnp.where(here, lane.astype(f32) + 1.0, 0.0), 1, keepdims=True) - 1.0
            )
        return jnp.where(lane == 0, edges[0], jnp.where(lane == 1, edges[1], -1.0))

    edges = slots(head_owner, head_row)
    edges = jnp.where(lane == 2, columns[1], jnp.where(lane == 3, columns[3], edges))
    head_edge[...] = edges
    tail_edge[...] = slots(tail_owner, tail_row)

    copy.wait()
    line = []
    for i in range(2):
        half = spread(block, (i,)).T
        picked = lax.broadcasted_iota(jnp.int32, (n, 256), 0) == neg_at % n
        line.append(jnp.sum(jnp.where(picked, half, 0.0), 0, keepdims=True))
    even = sub % 2 == 0
    send[pl.ds(0, n, stride=TILES1), :] = jnp.where(even, wide(line[0][:, :n]), wide(line[1][:, :n]))
    tile = jnp.where(even, wide(line[0][:, n:]), wide(line[1][:, n:]))
    for j, col in enumerate(columns):
        tile = jnp.where(lane == ASKS + j, col, tile)
    send[pl.ds(1, n, stride=TILES1), :] = tile


def ahead_kernel(table_t, relations, head_edge, *outs):
    whole = spread(table_t[...], (0, 1)).T
    for ref, piece in zip(outs[:PIECES], parts(whole, PIECES), strict=True):
        ref[...] = piece
    pad = jnp.zeros((64, 56), f32)
    whole = jnp.concatenate([relations[:, :200], pad, relations[:, 200:], pad], 1)
    whole = jnp.concatenate([quarter(whole, q) for q in range(4)], 1)
    pieces = parts(whole, PIECES)
    for ref, piece in zip(outs[PIECES:-1], pieces, strict=True):
        ref[...] = piece
    ids = jnp.concatenate([head_edge[:, 2:3], head_edge[:, 3:4]], 0)
    hot = jnp.where(lanes((2 * LANE, 64)).astype(f32) == ids, 1.0, 0.0).astype(bf16)
    outs[-1][...] = pick(hot, pieces, NN)


def pair_kernel(head_edge, tail_edge, rels, neg, out):
    n = 2 * LANE
    out[0:n, :] = rels[...]

    def stack(ref, by_rows):
        if by_rows:
            turned = ref[...].T
            return jnp.concatenate([turned[0:1, :], turned[1:2, :]], 1)
        return jnp.concatenate([ref[:, 0:1], ref[:, 1:2]], 0)

    for i, (one, other) in enumerate(((head_edge, tail_edge), (tail_edge, head_edge))):
        col, row = stack(one, False), stack(other, True)
        out[n : 2 * n, i * n : (i + 1) * n] = jnp.where(
            (col == row) & (col >= 0.0), 1.0, 0.0
        )
    out[2 * n :, 0:n] = neg[...]
    out[2 * n :, n:] = jnp.zeros((LANE, n), f32)


def rel_vectors(tile, slots, pieces):
    ids = jnp.concatenate([column(tile, ASKS + 2 * s + 1) for s in slots], 0)
    hot = jnp.where(lanes((ids.shape[0], 64)).astype(f32) == ids, 1.0, 0.0).astype(bf16)
    return pick(hot, [p[...] for p in pieces], NN)


def fetch_kernel(recv, *refs):
    n = LANE
    table, rel = refs[:PIECES], refs[PIECES : 2 * PIECES]
    send, rows, negs = refs[2 * PIECES :]
    negs[...] = recv[...]
    tile = recv[pl.ds(1, n, stride=TILES1), :]
    packed = []
    for side in range(2):
        slots = (2 * side, 2 * side + 1)
        at = jnp.concatenate([column(tile, ASKS + 2 * s) for s in slots], 0)
        hot = jnp.where(lanes((2 * n, 512)).astype(f32) == at, 1.0, 0.0).astype(bf16)
        vec = pick(hot, [p[...] for p in table], NN)
        if side == 0:
            vec = cmul(vec, rel_vectors(tile, slots, rel))
        packed += [vec[:n, :], vec[n:, :]]
        rows[2 * n * side : 2 * n * (side + 1), :] = vec
    pack(send, packed)


def negatives_kernel(odd, recv, rows, *refs):
    n = LANE
    rel = refs[:PIECES]
    mine, other, back, keep, give = refs[PIECES:]
    tile = recv[pl.ds(1, n, stride=TILES1), :]
    at = lanes((n, LANE))
    low = lanes((4 * n, LANE)) < 64

    def half(ref):
        first = [ref[pl.ds(TILES1 * n * j, n, stride=TILES1), :] for j in range(4)]
        second = [ref[pl.ds(TILES1 * n * j + 1, n, stride=TILES1), :] for j in range(4)]
        second = [jnp.where(at < ASKS, x, 0.0) for x in second]
        return jnp.concatenate(first, 0), jnp.concatenate(second, 0)

    flip = odd[0] > 0
    negs = []
    for own, got in zip(half(mine), half(other)):
        re, im = jnp.where(flip, got, own), jnp.where(flip, own, got)
        negs.append(jnp.where(low, re, pltpu.roll(im, 64, 1)))
        negs.append(jnp.where(low, pltpu.roll(re, 64, 1), im))
    negs = jnp.concatenate(negs, 1)
    probe = cmul(rows[2 * n :, :], rel_vectors(tile, (2, 3), rel), True)
    x = jnp.concatenate([rows[0 : 2 * n, :], probe], 0)
    valid = jnp.concatenate([column(tile, ASKS + 2 * s) for s in range(4)], 0)
    coef = sigmoid(dot3(x, negs, NT)) * (1.0 / math.sqrt(512.0))
    coef = jnp.where(valid >= 0.0, coef, 0.0)
    back[...] = dot3(coef, negs, NN)
    total = dot3(coef, x, TN)
    for i in range(2):
        first, second = tile_of(total, 2 * i), tile_of(total, 2 * i + 1)
        re = jnp.where(low, first, pltpu.roll(second, 64, 1))
        im = jnp.where(low, pltpu.roll(first, 64, 1), second)
        keep[:, i * n : (i + 1) * n] = jnp.where(flip, im, re)
        give[:, i * n : (i + 1) * n] = jnp.where(flip, re, im)


def fold_kernel(rep, keep, got, *outs):
    for i, ref in enumerate(outs):
        at = pl.ds(pl.multiple_of((rep[0] + i) % 4 * LANE, LANE), LANE)
        ref[...] = keep[at, :] + got[at, :]


def edge_kernel(recv, aids, sum1, sum2, sum3, send, token):
    n = LANE
    slots = unpack(recv, n)
    query, tails = jnp.concatenate(slots[:2], 0), jnp.concatenate(slots[2:], 0)
    met = pick(aids[2 * n : 4 * n, 0 : 2 * n].astype(bf16), parts(tails, PIECES), NN)
    pos = jnp.sum(query * met, 1, keepdims=True)
    coef = -sigmoid(-pos)
    to_head = cmul(coef * met, aids[0 : 2 * n, :], True)
    to_tail = pick(aids[2 * n : 4 * n, 2 * n :].astype(bf16), parts(coef * query, PIECES), NN)
    neg = aids[4 * n :, 0 : 2 * n] + sum1[...] + (sum2[...] + sum3[...])
    at = lanes((n, LANE))
    for q in range(4):
        words = tile_of(neg, q // 2)
        if q % 2:
            words = pltpu.roll(words, 64, 1)
        words = jnp.where(at < 64, words, pltpu.roll(words, 32, 1))
        for s, block in enumerate((to_head[:n], to_head[n:], to_tail[:n], to_tail[n:])):
            moved = pltpu.roll(words, 56 - 8 * s, 1)
            send[pl.ds(4 * q + s, n, stride=4 * TILES3), :] = jnp.where(
                at % 64 < 56, tile_of(block, q), moved
            )
    token[...] = neg[0:8, 0:128]


def local_kernel(rep, token, asks, back, *refs):
    n = 2 * LANE
    *rel, out0, out1, out2, out3, quarters = refs
    tile = asks[pl.ds(1, LANE, stride=TILES1), :]
    turned = tile.T
    sub = lax.broadcasted_iota(jnp.int32, (512, LANE), 0).astype(f32)
    hot = jnp.concatenate(
        [
            jnp.where(sub == turned[ASKS + 2 * s : ASKS + 2 * s + 1, :], 1.0, 0.0).astype(bf16)
            for s in range(4)
        ],
        1,
    )
    head = cmul(back[0:n, :], rel_vectors(tile, (0, 1), rel), True)
    tail = cmul(back[n:, :], rel_vectors(tile, (2, 3), rel))
    grad = jnp.concatenate([head, tail], 0)
    total = pick(hot, parts(grad, PIECES), NN)
    for q in range(4):
        quarters[q] = tile_of(total, q)
    for i, ref in enumerate((out0, out1, out2, out3)):
        ref[...] = quarters[(rep[0] + i) % 4]


def gather_local_kernel(part0, part1, part2, part3, out):
    out[...] = part0[...] + part1[...] + (part2[...] + part3[...])


def place_kernel(neg_rows, asks, token, hot):
    n = LANE
    sub = lax.broadcasted_iota(jnp.int32, (512, n), 0).astype(f32)
    for x in range(4):
        turned = asks[pl.ds(x * TILES1 * n + 1, n, stride=TILES1), :].T
        for s in range(4):
            at = turned[ASKS + 2 * s : ASKS + 2 * s + 1, :]
            b = 4 * x + s
            hot[:, b * n : (b + 1) * n] = jnp.where(sub == at, 1.0, 0.0).astype(bf16)
    at = jnp.full((1, n), -1.0, f32)
    for x in range(4):
        at = jnp.where(lanes((1, n)) == x, neg_rows[x].astype(f32), at)
    hot[:, 16 * n :] = jnp.where(sub == at, 1.0, 0.0).astype(bf16)


def scatter_kernel(recv, hot, local, out):
    n = LANE
    even = lax.broadcasted_iota(jnp.int32, (n, n), 0) % 2 == 0
    which = lax.broadcasted_iota(jnp.int32, (8, n), 0)
    sums = [[jnp.zeros((8, n), f32) for _ in range(2)] for _ in range(4)]
    blocks = []
    for x in range(4):
        for s in range(4):
            tile = recv[pl.ds(4 * x + s, n, stride=4 * TILES3), :]
            reals = jnp.sum(jnp.where(even, tile, 0.0), 0, keepdims=True)
            imags = jnp.sum(jnp.where(even, 0.0, tile), 0, keepdims=True)
            sums[s] = [
                jnp.where(which == x, new, old) for old, new in zip(sums[s], (reals, imags))
            ]
            blocks.append(tile)
    neg = jnp.zeros((8, n), f32)
    lane = lanes((8, n))
    for s in range(4):
        for i in range(2):
            word = 32 * i + 8 * s
            if word < 56:
                for side in range(2):
                    goal = 64 * side + word
                    shift = (goal - (56 + 64 * i)) % n
                    moved = pltpu.roll(sums[s][side], shift, 1) if shift else sums[s][side]
                    neg = jnp.where((lane >= goal) & (lane < goal + 8), moved, neg)
    blocks += [neg, jnp.zeros((n - 8, n), f32)]
    both = jnp.concatenate(parts(jnp.concatenate(blocks, 0), 2), 1)
    total = dot(hot[...], both, NN)
    turned = (total[:, :n] + total[:, n:] + local[...]).T
    out[0:56, :] = turned[0:56, :]
    out[56:112, :] = turned[64:120, :]


def finish_kernel(grads, table_t, state, table_new, state_new):
    spans = [
        (q * 112 + i * 56, i * 200 + STARTS[q], SIZES[q]) for q in range(4) for i in range(2)
    ]
    total = jnp.zeros((1, 512), f32)
    for at, _, size in spans:
        grad = grads[at : at + size, :]
        total = total + jnp.sum(grad * grad, 0, keepdims=True)
    new = state[...] + total * (1.0 / 400.0)
    state_new[...] = new
    step = learn_rate / jnp.sqrt(new)
    for at, to, size in spans:
        table_new[to : to + size, :] = table_t[to : to + size, :] - grads[at : at + size, :] * step


def call(kernel, outs, args, scalars=(), name=None, scratch=(), whole=0):
    space = pl.BlockSpec(memory_space=pltpu.VMEM)
    return pl.pallas_call(
        kernel,
        out_shape=[
            (pltpu.VMEM if near else pltpu.HBM)(shape, kind)
            for shape, kind, near in outs
        ],
        in_specs=[pl.BlockSpec(memory_space=pltpu.SMEM)] * len(scalars)
        + [space] * (len(args) - whole)
        + [pl.BlockSpec(memory_space=pltpu.HBM)] * whole,
        out_specs=[space] * len(outs),
        scratch_shapes=list(scratch),
        compiler_params=pltpu.CompilerParams(vmem_limit_bytes=24 << 20),
        name=name,
    )(*scalars, *args)


def near(x):
    return pltpu.with_memory_space_constraint(x, pltpu.VMEM)


def far(x):
    return pltpu.with_memory_space_constraint(x, pltpu.HBM)


def exchange(x, axis, tiles):
    n = x.shape[0] // tiles
    x = x.reshape(n, 1, tiles * LANE)
    x = lax.all_to_all(x, axis, split_axis=0, concat_axis=0, tiled=True)
    return x.reshape(n * tiles, LANE)


def shift(x, by):
    n = lax.axis_size("rep")
    return lax.ppermute(x, "rep", [(i, (i + by) % n) for i in range(n)])


def swap_cores(x):
    return lax.ppermute(x, "ent", [(i, i ^ 1) for i in range(lax.axis_size("ent"))])


def on_device(
    entity_table,
    adagrad_state,
    head_owner,
    head_row,
    relation_ids,
    tail_owner,
    tail_row,
    neg_rows,
    relations,
):
    rep = lax.axis_index("rep").reshape(1).astype(jnp.int32)
    odd = (lax.axis_index("ent") & 1).reshape(1).astype(jnp.int32)
    table_t = entity_table.T
    neg_rows = far(neg_rows)
    n = LANE

    def line(x):
        return far(x.reshape(1, n))

    send1, head_edge, tail_edge = call(
        ask_kernel,
        [((n * TILES1, n), f32, False), ((n, n), f32, False), ((n, n), f32, False)],
        (
            line(head_owner),
            line(head_row),
            line(relation_ids),
            line(tail_owner),
            line(tail_row),
            far(table_t),
        ),
        (rep, neg_rows),
        "ask",
        (pltpu.VMEM((400, n), f32), pltpu.SemaphoreType.DMA),
        1,
    )
    recv1 = exchange(send1, "ent", TILES1)
    *pieces, edge_rels = call(
        ahead_kernel,
        [((4 * n, 512), bf16, True)] * PIECES
        + [((64, 512), bf16, True)] * PIECES
        + [((2 * n, 512), f32, True)],
        (table_t, relations, far(head_edge)),
        name="ahead",
    )
    rel_pieces = pieces[PIECES:]
    send2, rows, own_negs = call(
        fetch_kernel,
        [
            ((n * TILES2, n), f32, False),
            ((4 * n, 512), f32, True),
            ((n * TILES1, n), f32, True),
        ],
        (near(recv1), *map(near, pieces)),
        name="fetch",
    )
    recv2 = exchange(send2, "ent", TILES2)
    mine = lax.all_gather(own_negs, "rep", axis=0, tiled=True)
    other = swap_cores(mine)
    back, keep, give = call(
        negatives_kernel,
        [((4 * n, 512), f32, True)] + [((4 * n, 256), f32, True)] * 2,
        (near(recv1), near(rows), *map(far, rel_pieces), near(mine), near(other)),
        (odd,),
        "negatives",
    )
    owned = call(
        fold_kernel,
        [((n, 256), f32, True)] * 4,
        (near(keep), near(swap_cores(give))),
        (rep,),
        "fold",
    )
    sums = [shift(owned[j], j) for j in (1, 2, 3)]
    (aids,) = call(
        pair_kernel,
        [((5 * n, 512), f32, True)],
        (far(head_edge), far(tail_edge), far(edge_rels), near(owned[0])),
        name="pair",
    )
    send3, token = call(
        edge_kernel,
        [((4 * n * TILES3, n), f32, False), ((8, n), f32, False)],
        (near(recv2), near(aids), *map(near, sums)),
        name="edge",
    )
    recv3 = exchange(send3, ("ent", "rep"), TILES3)
    token = far(token)
    local = call(
        local_kernel,
        [((4 * n, n), f32, True)] * 4,
        (token, recv1, far(back), *map(far, rel_pieces)),
        (rep,),
        "local",
        (pltpu.VMEM((4, 4 * n, n), f32),),
    )
    (local,) = call(
        gather_local_kernel,
        [((4 * n, n), f32, True)],
        [far(local[0])] + [far(shift(local[j], j)) for j in (1, 2, 3)],
        name="gather_local",
    )
    (hot,) = call(
        place_kernel, [((4 * n, 17 * n), bf16, True)], (far(mine), token), (neg_rows,), "place"
    )
    (grads,) = call(
        scatter_kernel,
        [((112, 512), f32, True)],
        (near(recv3), near(hot), near(local)),
        name="scatter",
    )
    grads = lax.all_gather(grads, "rep", axis=0, tiled=True)
    table_new, state_new = call(
        finish_kernel,
        [((400, 512), f32, False), ((1, 512), f32, False)],
        (near(grads), table_t, adagrad_state.reshape(1, 512)),
        name="finish",
    )
    return (table_new.T, state_new.reshape(512))


def solution(mesh):
    placed = (
        P("ent", None),
        P("ent"),
        P(("ent", "rep"), None),
        P(("ent", "rep")),
        P(("ent", "rep")),
        P(("ent", "rep"), None),
        P(("ent", "rep")),
        P("ent"),
        P(),
    )
    return jax.shard_map(
        on_device, mesh=mesh, in_specs=placed, out_specs=(P("ent", None), P("ent")), check_vma=False
    )
```

```python
import math

import jax
import jax.numpy as jnp
from jax import lax
from jax.experimental import pallas as pl
from jax.experimental.pallas import tpu as pltpu
from jax.sharding import PartitionSpec as P

learn_rate = 0.1

LANE = 128
f32 = jnp.float32
bf16 = jnp.bfloat16
NN = (((1,), (0,)), ((), ()))
NT = (((1,), (1,)), ((), ()))
TN = (((0,), (0,)), ((), ()))
PIECES = 2
TILES1 = 2
TILES2 = 13
TILES3 = 4
ASKS = 112
STARTS = (0, 56, 104, 152)
SIZES = (56, 48, 48, 48)


def dot(a, b, dims):
    return lax.dot_general(a, b, dims, preferred_element_type=f32)


def parts(x, count):
    out = []
    for _ in range(count):
        head = x.astype(bf16)
        out.append(head)
        x = x - head.astype(f32)
    return out


def pick(onehot, pieces, dims):
    total = dot(onehot, pieces[0], dims)
    for piece in pieces[1:]:
        total = total + dot(onehot, piece, dims)
    return total


def dot3(a, b, dims):
    a0, a1 = parts(a, 2)
    b0, b1 = parts(b, 2)
    return dot(a0, b0, dims) + (dot(a0, b1, dims) + dot(a1, b0, dims))


def lanes(shape):
    return lax.broadcasted_iota(jnp.int32, shape, len(shape) - 1)


def tile_of(x, q):
    return x[:, q * LANE : (q + 1) * LANE]


def turn(x):
    return jnp.concatenate([pltpu.roll(tile_of(x, q), 64, 1) for q in range(4)], 1)


def factors(b, conj=False):
    low = lanes(b.shape) % LANE < 64
    other = turn(b)
    second = jnp.where(low, other, -b) if conj else jnp.where(low, -other, b)
    return jnp.where(low, b, other), second


def cmul(a, b, conj=False):
    first, second = factors(b, conj)
    return a * first + turn(a) * second


def sigmoid(x):
    return 1.0 / (1.0 + jnp.exp(-x))


def column(tile, lane):
    return jnp.sum(jnp.where(lanes(tile.shape) == lane, tile, 0.0), 1, keepdims=True)


def pack(ref, slots):
    n = slots[0].shape[0]
    at = lanes((n, LANE)) % 64
    tail = jnp.zeros((n, LANE), f32)
    for s, slot in enumerate(slots):
        first = tile_of(slot, 0)
        for j in range(1, 4):
            moved = pltpu.roll(first, 64 - 16 * j, 1)
            ref[pl.ds(3 * s + j - 1, n, stride=TILES2), :] = jnp.where(
                at < 48, tile_of(slot, j), moved
            )
        moved = pltpu.roll(first, (8 * s - 48) % LANE, 1)
        tail = jnp.where((at >= 8 * s) & (at < 8 * s + 8), moved, tail)
    ref[pl.ds(12, n, stride=TILES2), :] = tail


def unpack(ref, n):
    at = lanes((n, LANE)) % 64
    tail = ref[pl.ds(12, n, stride=TILES2), :]
    out = []
    for s in range(4):
        first = jnp.where(at < 56, pltpu.roll(tail, 48 - 8 * s, 1), 0.0)
        others = []
        for j in range(3, 0, -1):
            dense = ref[pl.ds(3 * s + j - 1, n, stride=TILES2), :]
            first = jnp.where(at < 16 * j, pltpu.roll(dense, 64 + 16 * j, 1), first)
            others.append(jnp.where(at < 48, dense, 0.0))
        out.append(jnp.concatenate([first] + others[::-1], 1))
    return out


def window(into, low, high, start, size, dest):
    at = lanes(into.shape)
    for src, first in ((low, 0), (high, LANE)):
        begin, end = max(start, first), min(start + size, first + LANE)
        if begin < end:
            goal = dest + begin - start
            shift = (goal - (begin - first)) % LANE
            moved = pltpu.roll(src, shift, 1) if shift else src
            into = jnp.where((at >= goal) & (at < goal + end - begin), moved, into)
    return into


def quarter(wide, q):
    out = jnp.zeros((wide.shape[0], LANE), f32)
    for i in range(2):
        low, high = (wide[:, (2 * i + j) * LANE : (2 * i + j + 1) * LANE] for j in range(2))
        out = window(out, low, high, STARTS[q], SIZES[q], 64 * i)
    return out


def spread(rows, sides):
    out = []
    for q in range(4):
        for i in sides:
            at = 200 * i + STARTS[q]
            out.append(rows[at : at + SIZES[q], :])
            out.append(jnp.zeros((64 - SIZES[q], rows.shape[1]), f32))
    return jnp.concatenate(out, 0)


def ask_kernel(
    rep, neg_rows, head_owner, head_row, rel, tail_owner, tail_row, table_t,
    send, head_edge, tail_edge, block, done,
):
    n = LANE
    neg_at = neg_rows[rep[0]]
    copy = pltpu.make_async_copy(
        table_t.at[:, pl.ds(pl.multiple_of(neg_at // n * n, n), n)], block, done
    )
    copy.start()
    sub = lax.broadcasted_iota(jnp.int32, (n, n), 0)
    lane = lanes((n, n))

    def wide(x):
        return jnp.broadcast_to(x, (n, x.shape[1]))

    head_owner, head_row, rel, tail_owner, tail_row = (
        wide(ref[...].astype(f32)) for ref in (head_owner, head_row, rel, tail_owner, tail_row)
    )
    owner_id = sub.astype(f32)
    columns = []

    def slots(owner, named):
        owner_c = owner.T
        rank = jnp.sum(jnp.where((owner == owner_c) & (sub < lane), 1.0, 0.0), 0, keepdims=True)
        edges = []
        for s in range(2):
            here = (owner == owner_id) & (wide(rank) == float(s))
            columns.append(jnp.sum(jnp.where(here, named + 1.0, 0.0), 1, keepdims=True) - 1.0)
            columns.append(jnp.sum(jnp.where(here, rel, 0.0), 1, keepdims=True))
            edges.append(
                jnp.sum(jnp.where(here, lane.astype(f32) + 1.0, 0.0), 1, keepdims=True) - 1.0
            )
        return jnp.where(lane == 0, edges[0], jnp.where(lane == 1, edges[1], -1.0))

    edges = slots(head_owner, head_row)
    edges = jnp.where(lane == 2, columns[1], jnp.where(lane == 3, columns[3], edges))
    head_edge[...] = edges
    tail_edge[...] = slots(tail_owner, tail_row)

    copy.wait()
    line = []
    for i in range(2):
        half = spread(block, (i,)).T
        picked = lax.broadcasted_iota(jnp.int32, (n, 256), 0) == neg_at % n
        line.append(jnp.sum(jnp.where(picked, half, 0.0), 0, keepdims=True))
    even = sub % 2 == 0
    send[pl.ds(0, n, stride=TILES1), :] = jnp.where(even, wide(line[0][:, :n]), wide(line[1][:, :n]))
    tile = jnp.where(even, wide(line[0][:, n:]), wide(line[1][:, n:]))
    for j, col in enumerate(columns):
        tile = jnp.where(lane == ASKS + j, col, tile)
    send[pl.ds(1, n, stride=TILES1), :] = tile


def ahead_kernel(table_t, relations, head_edge, *outs):
    whole = spread(table_t[...], (0, 1)).T
    for ref, piece in zip(outs[:PIECES], parts(whole, PIECES), strict=True):
        ref[...] = piece
    pad = jnp.zeros((64, 56), f32)
    whole = jnp.concatenate([relations[:, :200], pad, relations[:, 200:], pad], 1)
    whole = jnp.concatenate([quarter(whole, q) for q in range(4)], 1)
    pieces = parts(whole, PIECES)
    for ref, piece in zip(outs[PIECES:-1], pieces, strict=True):
        ref[...] = piece
    ids = jnp.concatenate([head_edge[:, 2:3], head_edge[:, 3:4]], 0)
    hot = jnp.where(lanes((2 * LANE, 64)).astype(f32) == ids, 1.0, 0.0).astype(bf16)
    outs[-1][...] = pick(hot, pieces, NN)


def pair_kernel(head_edge, tail_edge, rels, neg, out):
    n = 2 * LANE
    out[0:n, :] = rels[...]

    def stack(ref, by_rows):
        if by_rows:
            turned = ref[...].T
            return jnp.concatenate([turned[0:1, :], turned[1:2, :]], 1)
        return jnp.concatenate([ref[:, 0:1], ref[:, 1:2]], 0)

    for i, (one, other) in enumerate(((head_edge, tail_edge), (tail_edge, head_edge))):
        col, row = stack(one, False), stack(other, True)
        out[n : 2 * n, i * n : (i + 1) * n] = jnp.where(
            (col == row) & (col >= 0.0), 1.0, 0.0
        )
    out[2 * n :, 0:n] = neg[...]
    out[2 * n :, n:] = jnp.zeros((LANE, n), f32)


def rel_vectors(tile, slots, pieces):
    ids = jnp.concatenate([column(tile, ASKS + 2 * s + 1) for s in slots], 0)
    hot = jnp.where(lanes((ids.shape[0], 64)).astype(f32) == ids, 1.0, 0.0).astype(bf16)
    return pick(hot, [p[...] for p in pieces], NN)


def fetch_kernel(recv, *refs):
    n = LANE
    table, rel = refs[:PIECES], refs[PIECES : 2 * PIECES]
    send, rows, negs = refs[2 * PIECES :]
    negs[...] = recv[...]
    tile = recv[pl.ds(1, n, stride=TILES1), :]
    packed = []
    for side in range(2):
        slots = (2 * side, 2 * side + 1)
        at = jnp.concatenate([column(tile, ASKS + 2 * s) for s in slots], 0)
        hot = jnp.where(lanes((2 * n, 512)).astype(f32) == at, 1.0, 0.0).astype(bf16)
        vec = pick(hot, [p[...] for p in table], NN)
        if side == 0:
            vec = cmul(vec, rel_vectors(tile, slots, rel))
        packed += [vec[:n, :], vec[n:, :]]
        rows[2 * n * side : 2 * n * (side + 1), :] = vec
    pack(send, packed)


def negatives_kernel(odd, recv, rows, *refs):
    n = LANE
    rel = refs[:PIECES]
    mine, other, back, keep, give = refs[PIECES:]
    tile = recv[pl.ds(1, n, stride=TILES1), :]
    at = lanes((n, LANE))
    low = lanes((4 * n, LANE)) < 64

    def half(ref):
        first = [ref[pl.ds(TILES1 * n * j, n, stride=TILES1), :] for j in range(4)]
        second = [ref[pl.ds(TILES1 * n * j + 1, n, stride=TILES1), :] for j in range(4)]
        second = [jnp.where(at < ASKS, x, 0.0) for x in second]
        return jnp.concatenate(first, 0), jnp.concatenate(second, 0)

    flip = odd[0] > 0
    negs = []
    for own, got in zip(half(mine), half(other)):
        re, im = jnp.where(flip, got, own), jnp.where(flip, own, got)
        negs.append(jnp.where(low, re, pltpu.roll(im, 64, 1)))
        negs.append(jnp.where(low, pltpu.roll(re, 64, 1), im))
    negs = jnp.concatenate(negs, 1)
    probe = cmul(rows[2 * n :, :], rel_vectors(tile, (2, 3), rel), True)
    x = jnp.concatenate([rows[0 : 2 * n, :], probe], 0)
    valid = jnp.concatenate([column(tile, ASKS + 2 * s) for s in range(4)], 0)
    coef = sigmoid(dot3(x, negs, NT)) * (1.0 / math.sqrt(512.0))
    coef = jnp.where(valid >= 0.0, coef, 0.0)
    back[...] = dot3(coef, negs, NN)
    total = dot3(coef, x, TN)
    for i in range(2):
        first, second = tile_of(total, 2 * i), tile_of(total, 2 * i + 1)
        re = jnp.where(low, first, pltpu.roll(second, 64, 1))
        im = jnp.where(low, pltpu.roll(first, 64, 1), second)
        keep[:, i * n : (i + 1) * n] = jnp.where(flip, im, re)
        give[:, i * n : (i + 1) * n] = jnp.where(flip, re, im)


def fold_kernel(rep, keep, got, *outs):
    for i, ref in enumerate(outs):
        at = pl.ds(pl.multiple_of((rep[0] + i) % 4 * LANE, LANE), LANE)
        ref[...] = keep[at, :] + got[at, :]


def edge_kernel(recv, aids, sum1, sum2, sum3, send, token):
    n = LANE
    slots = unpack(recv, n)
    query, tails = jnp.concatenate(slots[:2], 0), jnp.concatenate(slots[2:], 0)
    met = pick(aids[2 * n : 4 * n, 0 : 2 * n].astype(bf16), parts(tails, PIECES), NN)
    pos = jnp.sum(query * met, 1, keepdims=True)
    coef = -sigmoid(-pos)
    to_head = cmul(coef * met, aids[0 : 2 * n, :], True)
    to_tail = pick(aids[2 * n : 4 * n, 2 * n :].astype(bf16), parts(coef * query, PIECES), NN)
    neg = aids[4 * n :, 0 : 2 * n] + sum1[...] + (sum2[...] + sum3[...])
    at = lanes((n, LANE))
    for q in range(4):
        words = tile_of(neg, q // 2)
        if q % 2:
            words = pltpu.roll(words, 64, 1)
        words = jnp.where(at < 64, words, pltpu.roll(words, 32, 1))
        for s, block in enumerate((to_head[:n], to_head[n:], to_tail[:n], to_tail[n:])):
            moved = pltpu.roll(words, 56 - 8 * s, 1)
            send[pl.ds(4 * q + s, n, stride=4 * TILES3), :] = jnp.where(
                at % 64 < 56, tile_of(block, q), moved
            )
    token[...] = neg[0:8, 0:128]


def local_kernel(rep, token, asks, back, *refs):
    n = 2 * LANE
    *rel, out0, out1, out2, out3, quarters = refs
    tile = asks[pl.ds(1, LANE, stride=TILES1), :]
    turned = tile.T
    sub = lax.broadcasted_iota(jnp.int32, (512, LANE), 0).astype(f32)
    hot = jnp.concatenate(
        [
            jnp.where(sub == turned[ASKS + 2 * s : ASKS + 2 * s + 1, :], 1.0, 0.0).astype(bf16)
            for s in range(4)
        ],
        1,
    )
    head = cmul(back[0:n, :], rel_vectors(tile, (0, 1), rel), True)
    tail = cmul(back[n:, :], rel_vectors(tile, (2, 3), rel))
    grad = jnp.concatenate([head, tail], 0)
    total = pick(hot, parts(grad, PIECES), NN)
    for q in range(4):
        turned = tile_of(total, q).T
        quarters[q, 0:56, :] = turned[0:56, :]
        quarters[q, 56:112, :] = turned[64:120, :]
    for i, ref in enumerate((out0, out1, out2, out3)):
        ref[...] = quarters[(rep[0] + i) % 4]


def gather_local_kernel(part0, part1, part2, part3, out):
    out[...] = part0[...] + part1[...] + (part2[...] + part3[...])


def place_kernel(neg_rows, asks, token, hot):
    n = LANE
    sub = lax.broadcasted_iota(jnp.int32, (512, n), 0).astype(f32)
    for x in range(4):
        turned = asks[pl.ds(x * TILES1 * n + 1, n, stride=TILES1), :].T
        for s in range(4):
            at = turned[ASKS + 2 * s : ASKS + 2 * s + 1, :]
            b = 4 * x + s
            hot[:, b * n : (b + 1) * n] = jnp.where(sub == at, 1.0, 0.0).astype(bf16)
    at = jnp.full((1, n), -1.0, f32)
    for x in range(4):
        at = jnp.where(lanes((1, n)) == x, neg_rows[x].astype(f32), at)
    hot[:, 16 * n :] = jnp.where(sub == at, 1.0, 0.0).astype(bf16)


def scatter_kernel(recv, hot, local, out):
    n = LANE
    even = lax.broadcasted_iota(jnp.int32, (n, n), 0) % 2 == 0
    which = lax.broadcasted_iota(jnp.int32, (8, n), 0)
    sums = [[jnp.zeros((8, n), f32) for _ in range(2)] for _ in range(4)]
    blocks = []
    for x in range(4):
        for s in range(4):
            tile = recv[pl.ds(4 * x + s, n, stride=4 * TILES3), :]
            reals = jnp.sum(jnp.where(even, tile, 0.0), 0, keepdims=True)
            imags = jnp.sum(jnp.where(even, 0.0, tile), 0, keepdims=True)
            sums[s] = [
                jnp.where(which == x, new, old) for old, new in zip(sums[s], (reals, imags))
            ]
            blocks.append(tile)
    neg = jnp.zeros((8, n), f32)
    lane = lanes((8, n))
    for s in range(4):
        for i in range(2):
            word = 32 * i + 8 * s
            if word < 56:
                for side in range(2):
                    goal = 64 * side + word
                    shift = (goal - (56 + 64 * i)) % n
                    moved = pltpu.roll(sums[s][side], shift, 1) if shift else sums[s][side]
                    neg = jnp.where((lane >= goal) & (lane < goal + 8), moved, neg)
    blocks += [neg, jnp.zeros((n - 8, n), f32)]
    both = jnp.concatenate(parts(jnp.concatenate(blocks, 0), 2), 1)
    total = dot(hot[...], both, NN)
    turned = (total[:, :n] + total[:, n:]).T
    out[0:56, :] = turned[0:56, :] + local[0:56, :]
    out[56:112, :] = turned[64:120, :] + local[56:112, :]


def finish_kernel(grads, table_t, state, table_new, state_new):
    spans = [
        (q * 112 + i * 56, i * 200 + STARTS[q], SIZES[q]) for q in range(4) for i in range(2)
    ]
    total = jnp.zeros((1, 512), f32)
    for at, _, size in spans:
        grad = grads[at : at + size, :]
        total = total + jnp.sum(grad * grad, 0, keepdims=True)
    new = state[...] + total * (1.0 / 400.0)
    state_new[...] = new
    step = learn_rate / jnp.sqrt(new)
    for at, to, size in spans:
        table_new[to : to + size, :] = table_t[to : to + size, :] - grads[at : at + size, :] * step


def call(kernel, outs, args, scalars=(), name=None, scratch=(), whole=0):
    space = pl.BlockSpec(memory_space=pltpu.VMEM)
    return pl.pallas_call(
        kernel,
        out_shape=[
            (pltpu.VMEM if near else pltpu.HBM)(shape, kind)
            for shape, kind, near in outs
        ],
        in_specs=[pl.BlockSpec(memory_space=pltpu.SMEM)] * len(scalars)
        + [space] * (len(args) - whole)
        + [pl.BlockSpec(memory_space=pltpu.HBM)] * whole,
        out_specs=[space] * len(outs),
        scratch_shapes=list(scratch),
        compiler_params=pltpu.CompilerParams(vmem_limit_bytes=24 << 20),
        name=name,
    )(*scalars, *args)


def near(x):
    return pltpu.with_memory_space_constraint(x, pltpu.VMEM)


def far(x):
    return pltpu.with_memory_space_constraint(x, pltpu.HBM)


def exchange(x, axis, tiles):
    n = x.shape[0] // tiles
    x = x.reshape(n, 1, tiles * LANE)
    x = lax.all_to_all(x, axis, split_axis=0, concat_axis=0, tiled=True)
    return x.reshape(n * tiles, LANE)


def shift(x, by):
    n = lax.axis_size("rep")
    return lax.ppermute(x, "rep", [(i, (i + by) % n) for i in range(n)])


def swap_cores(x):
    return lax.ppermute(x, "ent", [(i, i ^ 1) for i in range(lax.axis_size("ent"))])


def on_device(
    entity_table,
    adagrad_state,
    head_owner,
    head_row,
    relation_ids,
    tail_owner,
    tail_row,
    neg_rows,
    relations,
):
    rep = lax.axis_index("rep").reshape(1).astype(jnp.int32)
    odd = (lax.axis_index("ent") & 1).reshape(1).astype(jnp.int32)
    table_t = entity_table.T
    neg_rows = far(neg_rows)
    n = LANE

    def line(x):
        return far(x.reshape(1, n))

    send1, head_edge, tail_edge = call(
        ask_kernel,
        [((n * TILES1, n), f32, False), ((n, n), f32, False), ((n, n), f32, False)],
        (
            line(head_owner),
            line(head_row),
            line(relation_ids),
            line(tail_owner),
            line(tail_row),
            far(table_t),
        ),
        (rep, neg_rows),
        "ask",
        (pltpu.VMEM((400, n), f32), pltpu.SemaphoreType.DMA),
        1,
    )
    recv1 = exchange(send1, "ent", TILES1)
    *pieces, edge_rels = call(
        ahead_kernel,
        [((4 * n, 512), bf16, True)] * PIECES
        + [((64, 512), bf16, True)] * PIECES
        + [((2 * n, 512), f32, True)],
        (table_t, relations, far(head_edge)),
        name="ahead",
    )
    rel_pieces = pieces[PIECES:]
    send2, rows, own_negs = call(
        fetch_kernel,
        [
            ((n * TILES2, n), f32, False),
            ((4 * n, 512), f32, True),
            ((n * TILES1, n), f32, True),
        ],
        (near(recv1), *map(near, pieces)),
        name="fetch",
    )
    recv2 = exchange(send2, "ent", TILES2)
    mine = lax.all_gather(own_negs, "rep", axis=0, tiled=True)
    other = swap_cores(mine)
    back, keep, give = call(
        negatives_kernel,
        [((4 * n, 512), f32, True)] + [((4 * n, 256), f32, True)] * 2,
        (near(recv1), near(rows), *map(far, rel_pieces), near(mine), near(other)),
        (odd,),
        "negatives",
    )
    owned = call(
        fold_kernel,
        [((n, 256), f32, True)] * 4,
        (near(keep), near(swap_cores(give))),
        (rep,),
        "fold",
    )
    sums = [shift(owned[j], j) for j in (1, 2, 3)]
    (aids,) = call(
        pair_kernel,
        [((5 * n, 512), f32, True)],
        (far(head_edge), far(tail_edge), far(edge_rels), near(owned[0])),
        name="pair",
    )
    send3, token = call(
        edge_kernel,
        [((4 * n * TILES3, n), f32, False), ((8, n), f32, False)],
        (near(recv2), near(aids), *map(near, sums)),
        name="edge",
    )
    recv3 = exchange(send3, ("ent", "rep"), TILES3)
    token = far(token)
    local = call(
        local_kernel,
        [((112, 512), f32, True)] * 4,
        (token, recv1, far(back), *map(far, rel_pieces)),
        (rep,),
        "local",
        (pltpu.VMEM((4, 112, 512), f32),),
    )
    (local,) = call(
        gather_local_kernel,
        [((112, 512), f32, True)],
        [far(local[0])] + [far(shift(local[j], j)) for j in (1, 2, 3)],
        name="gather_local",
    )
    (hot,) = call(
        place_kernel, [((4 * n, 17 * n), bf16, True)], (far(mine), token), (neg_rows,), "place"
    )
    (grads,) = call(
        scatter_kernel,
        [((112, 512), f32, True)],
        (near(recv3), near(hot), near(local)),
        name="scatter",
    )
    grads = lax.all_gather(grads, "rep", axis=0, tiled=True)
    table_new, state_new = call(
        finish_kernel,
        [((400, 512), f32, False), ((1, 512), f32, False)],
        (near(grads), table_t, adagrad_state.reshape(1, 512)),
        name="finish",
    )
    return (table_new.T, state_new.reshape(512))


def solution(mesh):
    placed = (
        P("ent", None),
        P("ent"),
        P(("ent", "rep"), None),
        P(("ent", "rep")),
        P(("ent", "rep")),
        P(("ent", "rep"), None),
        P(("ent", "rep")),
        P("ent"),
        P(),
    )
    return jax.shard_map(
        on_device, mesh=mesh, in_specs=placed, out_specs=(P("ent", None), P("ent")), check_vma=False
    )
```

```python
import math

import jax
import jax.numpy as jnp
from jax import lax
from jax.experimental import pallas as pl
from jax.experimental.pallas import tpu as pltpu
from jax.sharding import PartitionSpec as P

learn_rate = 0.1

LANE = 128
f32 = jnp.float32
bf16 = jnp.bfloat16
NN = (((1,), (0,)), ((), ()))
NT = (((1,), (1,)), ((), ()))
TN = (((0,), (0,)), ((), ()))
PIECES = 2
TILES1 = 2
TILES2 = 13
TILES3 = 4
ASKS = 112
STARTS = (0, 56, 104, 152)
SIZES = (56, 48, 48, 48)


def dot(a, b, dims):
    return lax.dot_general(a, b, dims, preferred_element_type=f32)


def parts(x, count):
    out = []
    for _ in range(count):
        head = x.astype(bf16)
        out.append(head)
        x = x - head.astype(f32)
    return out


def pick(onehot, pieces, dims):
    total = dot(onehot, pieces[0], dims)
    for piece in pieces[1:]:
        total = total + dot(onehot, piece, dims)
    return total


def dot3(a, b, dims):
    a0, a1 = parts(a, 2)
    b0, b1 = parts(b, 2)
    return dot(a0, b0, dims) + (dot(a0, b1, dims) + dot(a1, b0, dims))


def lanes(shape):
    return lax.broadcasted_iota(jnp.int32, shape, len(shape) - 1)


def tile_of(x, q):
    return x[:, q * LANE : (q + 1) * LANE]


def turn(x):
    return jnp.concatenate([pltpu.roll(tile_of(x, q), 64, 1) for q in range(4)], 1)


def factors(b, conj=False):
    low = lanes(b.shape) % LANE < 64
    other = turn(b)
    second = jnp.where(low, other, -b) if conj else jnp.where(low, -other, b)
    return jnp.where(low, b, other), second


def cmul(a, b, conj=False):
    first, second = factors(b, conj)
    return a * first + turn(a) * second


def sigmoid(x):
    return 1.0 / (1.0 + jnp.exp(-x))


def column(tile, lane):
    return jnp.sum(jnp.where(lanes(tile.shape) == lane, tile, 0.0), 1, keepdims=True)


def pack(ref, slots):
    n = slots[0].shape[0]
    at = lanes((n, LANE)) % 64
    tail = jnp.zeros((n, LANE), f32)
    for s, slot in enumerate(slots):
        first = tile_of(slot, 0)
        for j in range(1, 4):
            moved = pltpu.roll(first, 64 - 16 * j, 1)
            ref[pl.ds(3 * s + j - 1, n, stride=TILES2), :] = jnp.where(
                at < 48, tile_of(slot, j), moved
            )
        moved = pltpu.roll(first, (8 * s - 48) % LANE, 1)
        tail = jnp.where((at >= 8 * s) & (at < 8 * s + 8), moved, tail)
    ref[pl.ds(12, n, stride=TILES2), :] = tail


def unpack(ref, n):
    at = lanes((n, LANE)) % 64
    tail = ref[pl.ds(12, n, stride=TILES2), :]
    out = []
    for s in range(4):
        first = jnp.where(at < 56, pltpu.roll(tail, 48 - 8 * s, 1), 0.0)
        others = []
        for j in range(3, 0, -1):
            dense = ref[pl.ds(3 * s + j - 1, n, stride=TILES2), :]
            first = jnp.where(at < 16 * j, pltpu.roll(dense, 64 + 16 * j, 1), first)
            others.append(jnp.where(at < 48, dense, 0.0))
        out.append(jnp.concatenate([first] + others[::-1], 1))
    return out


def window(into, low, high, start, size, dest):
    at = lanes(into.shape)
    for src, first in ((low, 0), (high, LANE)):
        begin, end = max(start, first), min(start + size, first + LANE)
        if begin < end:
            goal = dest + begin - start
            shift = (goal - (begin - first)) % LANE
            moved = pltpu.roll(src, shift, 1) if shift else src
            into = jnp.where((at >= goal) & (at < goal + end - begin), moved, into)
    return into


def quarter(wide, q):
    out = jnp.zeros((wide.shape[0], LANE), f32)
    for i in range(2):
        low, high = (wide[:, (2 * i + j) * LANE : (2 * i + j + 1) * LANE] for j in range(2))
        out = window(out, low, high, STARTS[q], SIZES[q], 64 * i)
    return out


def spread(rows, sides):
    out = []
    for q in range(4):
        for i in sides:
            at = 200 * i + STARTS[q]
            out.append(rows[at : at + SIZES[q], :])
            out.append(jnp.zeros((64 - SIZES[q], rows.shape[1]), f32))
    return jnp.concatenate(out, 0)


def ask_kernel(
    rep, neg_rows, head_owner, head_row, rel, tail_owner, tail_row, table_t,
    send, head_edge, tail_edge, block, done,
):
    n = LANE
    neg_at = neg_rows[rep[0]]
    copy = pltpu.make_async_copy(
        table_t.at[:, pl.ds(pl.multiple_of(neg_at // n * n, n), n)], block, done
    )
    copy.start()
    sub = lax.broadcasted_iota(jnp.int32, (n, n), 0)
    lane = lanes((n, n))

    def wide(x):
        return jnp.broadcast_to(x, (n, x.shape[1]))

    head_owner, head_row, rel, tail_owner, tail_row = (
        wide(ref[...].astype(f32)) for ref in (head_owner, head_row, rel, tail_owner, tail_row)
    )
    owner_id = sub.astype(f32)
    columns = []

    def slots(owner, named):
        owner_c = owner.T
        rank = jnp.sum(jnp.where((owner == owner_c) & (sub < lane), 1.0, 0.0), 0, keepdims=True)
        edges = []
        for s in range(2):
            here = (owner == owner_id) & (wide(rank) == float(s))
            columns.append(jnp.sum(jnp.where(here, named + 1.0, 0.0), 1, keepdims=True) - 1.0)
            columns.append(jnp.sum(jnp.where(here, rel, 0.0), 1, keepdims=True))
            edges.append(
                jnp.sum(jnp.where(here, lane.astype(f32) + 1.0, 0.0), 1, keepdims=True) - 1.0
            )
        return jnp.where(lane == 0, edges[0], jnp.where(lane == 1, edges[1], -1.0))

    edges = slots(head_owner, head_row)
    edges = jnp.where(lane == 2, columns[1], jnp.where(lane == 3, columns[3], edges))
    head_edge[...] = edges
    tail_edge[...] = slots(tail_owner, tail_row)

    copy.wait()
    line = []
    for i in range(2):
        half = spread(block, (i,)).T
        picked = lax.broadcasted_iota(jnp.int32, (n, 256), 0) == neg_at % n
        line.append(jnp.sum(jnp.where(picked, half, 0.0), 0, keepdims=True))
    even = sub % 2 == 0
    send[pl.ds(0, n, stride=TILES1), :] = jnp.where(even, wide(line[0][:, :n]), wide(line[1][:, :n]))
    tile = jnp.where(even, wide(line[0][:, n:]), wide(line[1][:, n:]))
    for j, col in enumerate(columns):
        tile = jnp.where(lane == ASKS + j, col, tile)
    send[pl.ds(1, n, stride=TILES1), :] = tile


def ahead_kernel(table_t, relations, head_edge, *outs):
    whole = spread(table_t[...], (0, 1)).T
    for ref, piece in zip(outs[:PIECES], parts(whole, PIECES), strict=True):
        ref[...] = piece
    pad = jnp.zeros((64, 56), f32)
    whole = jnp.concatenate([relations[:, :200], pad, relations[:, 200:], pad], 1)
    whole = jnp.concatenate([quarter(whole, q) for q in range(4)], 1)
    pieces = parts(whole, PIECES)
    for ref, piece in zip(outs[PIECES:-1], pieces, strict=True):
        ref[...] = piece
    ids = jnp.concatenate([head_edge[:, 2:3], head_edge[:, 3:4]], 0)
    hot = jnp.where(lanes((2 * LANE, 64)).astype(f32) == ids, 1.0, 0.0).astype(bf16)
    outs[-1][...] = pick(hot, pieces, NN)


def pair_kernel(head_edge, tail_edge, rels, neg, out):
    n = 2 * LANE
    out[0:n, :] = rels[...]

    def stack(ref, by_rows):
        if by_rows:
            turned = ref[...].T
            return jnp.concatenate([turned[0:1, :], turned[1:2, :]], 1)
        return jnp.concatenate([ref[:, 0:1], ref[:, 1:2]], 0)

    for i, (one, other) in enumerate(((head_edge, tail_edge), (tail_edge, head_edge))):
        col, row = stack(one, False), stack(other, True)
        out[n : 2 * n, i * n : (i + 1) * n] = jnp.where(
            (col == row) & (col >= 0.0), 1.0, 0.0
        )
    out[2 * n :, 0:n] = neg[...]
    out[2 * n :, n:] = jnp.zeros((LANE, n), f32)


def rel_vectors(tile, slots, pieces):
    ids = jnp.concatenate([column(tile, ASKS + 2 * s + 1) for s in slots], 0)
    hot = jnp.where(lanes((ids.shape[0], 64)).astype(f32) == ids, 1.0, 0.0).astype(bf16)
    return pick(hot, [p[...] for p in pieces], NN)


def fetch_kernel(recv, *refs):
    n = LANE
    table, rel = refs[:PIECES], refs[PIECES : 2 * PIECES]
    send, rows, negs = refs[2 * PIECES :]
    negs[...] = recv[...]
    tile = recv[pl.ds(1, n, stride=TILES1), :]
    at = jnp.concatenate([column(tile, ASKS + 2 * s) for s in range(4)], 0)
    hot = jnp.where(lanes((4 * n, 512)).astype(f32) == at, 1.0, 0.0).astype(bf16)
    vec = pick(hot, [p[...] for p in table], NN)
    query = cmul(vec[: 2 * n, :], rel_vectors(tile, (0, 1), rel))
    rows[0 : 2 * n, :] = query
    rows[2 * n :, :] = vec[2 * n :, :]
    packed = [query[:n, :], query[n:, :], vec[2 * n : 3 * n, :], vec[3 * n :, :]]
    pack(send, packed)


def negatives_kernel(odd, recv, rows, *refs):
    n = LANE
    rel = refs[:PIECES]
    mine, other, back, keep, give = refs[PIECES:]
    tile = recv[pl.ds(1, n, stride=TILES1), :]
    at = lanes((n, LANE))
    low = lanes((4 * n, LANE)) < 64

    def half(ref):
        first = [ref[pl.ds(TILES1 * n * j, n, stride=TILES1), :] for j in range(4)]
        second = [ref[pl.ds(TILES1 * n * j + 1, n, stride=TILES1), :] for j in range(4)]
        second = [jnp.where(at < ASKS, x, 0.0) for x in second]
        return jnp.concatenate(first, 0), jnp.concatenate(second, 0)

    flip = odd[0] > 0
    negs = []
    for own, got in zip(half(mine), half(other)):
        re, im = jnp.where(flip, got, own), jnp.where(flip, own, got)
        negs.append(jnp.where(low, re, pltpu.roll(im, 64, 1)))
        negs.append(jnp.where(low, pltpu.roll(re, 64, 1), im))
    negs = jnp.concatenate(negs, 1)
    probe = cmul(rows[2 * n :, :], rel_vectors(tile, (2, 3), rel), True)
    x = jnp.concatenate([rows[0 : 2 * n, :], probe], 0)
    valid = jnp.concatenate([column(tile, ASKS + 2 * s) for s in range(4)], 0)
    coef = sigmoid(dot3(x, negs, NT)) * (1.0 / math.sqrt(512.0))
    coef = jnp.where(valid >= 0.0, coef, 0.0)
    back[...] = dot3(coef, negs, NN)
    total = dot3(coef, x, TN)
    for i in range(2):
        first, second = tile_of(total, 2 * i), tile_of(total, 2 * i + 1)
        re = jnp.where(low, first, pltpu.roll(second, 64, 1))
        im = jnp.where(low, pltpu.roll(first, 64, 1), second)
        keep[:, i * n : (i + 1) * n] = jnp.where(flip, im, re)
        give[:, i * n : (i + 1) * n] = jnp.where(flip, re, im)


def fold_kernel(rep, keep, got, *outs):
    for i, ref in enumerate(outs):
        at = pl.ds(pl.multiple_of((rep[0] + i) % 4 * LANE, LANE), LANE)
        ref[...] = keep[at, :] + got[at, :]


def edge_kernel(recv, aids, sum1, sum2, sum3, send, token):
    n = LANE
    slots = unpack(recv, n)
    query, tails = jnp.concatenate(slots[:2], 0), jnp.concatenate(slots[2:], 0)
    met = pick(aids[2 * n : 4 * n, 0 : 2 * n].astype(bf16), parts(tails, PIECES), NN)
    pos = jnp.sum(query * met, 1, keepdims=True)
    coef = -sigmoid(-pos)
    to_head = cmul(coef * met, aids[0 : 2 * n, :], True)
    to_tail = pick(aids[2 * n : 4 * n, 2 * n :].astype(bf16), parts(coef * query, PIECES), NN)
    neg = aids[4 * n :, 0 : 2 * n] + sum1[...] + (sum2[...] + sum3[...])
    at = lanes((n, LANE))
    for q in range(4):
        words = tile_of(neg, q // 2)
        if q % 2:
            words = pltpu.roll(words, 64, 1)
        words = jnp.where(at < 64, words, pltpu.roll(words, 32, 1))
        for s, block in enumerate((to_head[:n], to_head[n:], to_tail[:n], to_tail[n:])):
            moved = pltpu.roll(words, 56 - 8 * s, 1)
            send[pl.ds(4 * q + s, n, stride=4 * TILES3), :] = jnp.where(
                at % 64 < 56, tile_of(block, q), moved
            )
    token[...] = neg[0:8, 0:128]


def local_kernel(rep, token, asks, back, *refs):
    n = 2 * LANE
    *rel, out0, out1, out2, out3, quarters = refs
    tile = asks[pl.ds(1, LANE, stride=TILES1), :]
    turned = tile.T
    sub = lax.broadcasted_iota(jnp.int32, (512, LANE), 0).astype(f32)
    hot = jnp.concatenate(
        [
            jnp.where(sub == turned[ASKS + 2 * s : ASKS + 2 * s + 1, :], 1.0, 0.0).astype(bf16)
            for s in range(4)
        ],
        1,
    )
    head = cmul(back[0:n, :], rel_vectors(tile, (0, 1), rel), True)
    tail = cmul(back[n:, :], rel_vectors(tile, (2, 3), rel))
    grad = jnp.concatenate([head, tail], 0)
    total = pick(hot, parts(grad, PIECES), NN)
    for q in range(4):
        quarters[q] = tile_of(total, q)
    for i, ref in enumerate((out0, out1, out2, out3)):
        ref[...] = quarters[(rep[0] + i) % 4]


def gather_local_kernel(part0, part1, part2, part3, out):
    out[...] = part0[...] + part1[...] + (part2[...] + part3[...])


def place_kernel(neg_rows, asks, token, hot):
    n = LANE
    sub = lax.broadcasted_iota(jnp.int32, (512, n), 0).astype(f32)
    for x in range(4):
        turned = asks[pl.ds(x * TILES1 * n + 1, n, stride=TILES1), :].T
        for s in range(4):
            at = turned[ASKS + 2 * s : ASKS + 2 * s + 1, :]
            b = 4 * x + s
            hot[:, b * n : (b + 1) * n] = jnp.where(sub == at, 1.0, 0.0).astype(bf16)
    at = jnp.full((1, n), -1.0, f32)
    for x in range(4):
        at = jnp.where(lanes((1, n)) == x, neg_rows[x].astype(f32), at)
    hot[:, 16 * n :] = jnp.where(sub == at, 1.0, 0.0).astype(bf16)


def scatter_kernel(recv, hot, local, out):
    n = LANE
    even = lax.broadcasted_iota(jnp.int32, (n, n), 0) % 2 == 0
    which = lax.broadcasted_iota(jnp.int32, (8, n), 0)
    sums = [[jnp.zeros((8, n), f32) for _ in range(2)] for _ in range(4)]
    blocks = []
    for x in range(4):
        for s in range(4):
            tile = recv[pl.ds(4 * x + s, n, stride=4 * TILES3), :]
            reals = jnp.sum(jnp.where(even, tile, 0.0), 0, keepdims=True)
            imags = jnp.sum(jnp.where(even, 0.0, tile), 0, keepdims=True)
            sums[s] = [
                jnp.where(which == x, new, old) for old, new in zip(sums[s], (reals, imags))
            ]
            blocks.append(tile)
    neg = jnp.zeros((8, n), f32)
    lane = lanes((8, n))
    for s in range(4):
        for i in range(2):
            word = 32 * i + 8 * s
            if word < 56:
                for side in range(2):
                    goal = 64 * side + word
                    shift = (goal - (56 + 64 * i)) % n
                    moved = pltpu.roll(sums[s][side], shift, 1) if shift else sums[s][side]
                    neg = jnp.where((lane >= goal) & (lane < goal + 8), moved, neg)
    blocks += [neg, jnp.zeros((n - 8, n), f32)]
    both = jnp.concatenate(parts(jnp.concatenate(blocks, 0), 2), 1)
    total = dot(hot[...], both, NN)
    turned = (total[:, :n] + total[:, n:] + local[...]).T
    out[0:56, :] = turned[0:56, :]
    out[56:112, :] = turned[64:120, :]


def finish_kernel(grads, table_t, state, table_new, state_new):
    spans = [
        (q * 112 + i * 56, i * 200 + STARTS[q], SIZES[q]) for q in range(4) for i in range(2)
    ]
    total = jnp.zeros((1, 512), f32)
    for at, _, size in spans:
        grad = grads[at : at + size, :]
        total = total + jnp.sum(grad * grad, 0, keepdims=True)
    new = state[...] + total * (1.0 / 400.0)
    state_new[...] = new
    step = learn_rate / jnp.sqrt(new)
    for at, to, size in spans:
        table_new[to : to + size, :] = table_t[to : to + size, :] - grads[at : at + size, :] * step


def call(kernel, outs, args, scalars=(), name=None, scratch=(), whole=0):
    space = pl.BlockSpec(memory_space=pltpu.VMEM)
    return pl.pallas_call(
        kernel,
        out_shape=[
            (pltpu.VMEM if near else pltpu.HBM)(shape, kind)
            for shape, kind, near in outs
        ],
        in_specs=[pl.BlockSpec(memory_space=pltpu.SMEM)] * len(scalars)
        + [space] * (len(args) - whole)
        + [pl.BlockSpec(memory_space=pltpu.HBM)] * whole,
        out_specs=[space] * len(outs),
        scratch_shapes=list(scratch),
        compiler_params=pltpu.CompilerParams(vmem_limit_bytes=24 << 20),
        name=name,
    )(*scalars, *args)


def near(x):
    return pltpu.with_memory_space_constraint(x, pltpu.VMEM)


def far(x):
    return pltpu.with_memory_space_constraint(x, pltpu.HBM)


def exchange(x, axis, tiles):
    n = x.shape[0] // tiles
    x = x.reshape(n, 1, tiles * LANE)
    x = lax.all_to_all(x, axis, split_axis=0, concat_axis=0, tiled=True)
    return x.reshape(n * tiles, LANE)


def shift(x, by):
    n = lax.axis_size("rep")
    return lax.ppermute(x, "rep", [(i, (i + by) % n) for i in range(n)])


def swap_cores(x):
    return lax.ppermute(x, "ent", [(i, i ^ 1) for i in range(lax.axis_size("ent"))])


def on_device(
    entity_table,
    adagrad_state,
    head_owner,
    head_row,
    relation_ids,
    tail_owner,
    tail_row,
    neg_rows,
    relations,
):
    rep = lax.axis_index("rep").reshape(1).astype(jnp.int32)
    odd = (lax.axis_index("ent") & 1).reshape(1).astype(jnp.int32)
    table_t = entity_table.T
    neg_rows = far(neg_rows)
    n = LANE

    def line(x):
        return far(x.reshape(1, n))

    send1, head_edge, tail_edge = call(
        ask_kernel,
        [((n * TILES1, n), f32, False), ((n, n), f32, False), ((n, n), f32, False)],
        (
            line(head_owner),
            line(head_row),
            line(relation_ids),
            line(tail_owner),
            line(tail_row),
            far(table_t),
        ),
        (rep, neg_rows),
        "ask",
        (pltpu.VMEM((400, n), f32), pltpu.SemaphoreType.DMA),
        1,
    )
    recv1 = exchange(send1, "ent", TILES1)
    *pieces, edge_rels = call(
        ahead_kernel,
        [((4 * n, 512), bf16, True)] * PIECES
        + [((64, 512), bf16, True)] * PIECES
        + [((2 * n, 512), f32, True)],
        (table_t, relations, far(head_edge)),
        name="ahead",
    )
    rel_pieces = pieces[PIECES:]
    send2, rows, own_negs = call(
        fetch_kernel,
        [
            ((n * TILES2, n), f32, False),
            ((4 * n, 512), f32, True),
            ((n * TILES1, n), f32, True),
        ],
        (near(recv1), *map(near, pieces)),
        name="fetch",
    )
    recv2 = exchange(send2, "ent", TILES2)
    mine = lax.all_gather(own_negs, "rep", axis=0, tiled=True)
    other = swap_cores(mine)
    back, keep, give = call(
        negatives_kernel,
        [((4 * n, 512), f32, True)] + [((4 * n, 256), f32, True)] * 2,
        (near(recv1), near(rows), *map(far, rel_pieces), near(mine), near(other)),
        (odd,),
        "negatives",
    )
    owned = call(
        fold_kernel,
        [((n, 256), f32, True)] * 4,
        (near(keep), near(swap_cores(give))),
        (rep,),
        "fold",
    )
    sums = [shift(owned[j], j) for j in (1, 2, 3)]
    (aids,) = call(
        pair_kernel,
        [((5 * n, 512), f32, True)],
        (far(head_edge), far(tail_edge), far(edge_rels), near(owned[0])),
        name="pair",
    )
    send3, token = call(
        edge_kernel,
        [((4 * n * TILES3, n), f32, False), ((8, n), f32, False)],
        (near(recv2), near(aids), *map(near, sums)),
        name="edge",
    )
    recv3 = exchange(send3, ("ent", "rep"), TILES3)
    token = far(token)
    local = call(
        local_kernel,
        [((4 * n, n), f32, True)] * 4,
        (token, recv1, far(back), *map(far, rel_pieces)),
        (rep,),
        "local",
        (pltpu.VMEM((4, 4 * n, n), f32),),
    )
    (local,) = call(
        gather_local_kernel,
        [((4 * n, n), f32, True)],
        [far(local[0])] + [far(shift(local[j], j)) for j in (1, 2, 3)],
        name="gather_local",
    )
    (hot,) = call(
        place_kernel, [((4 * n, 17 * n), bf16, True)], (far(mine), token), (neg_rows,), "place"
    )
    (grads,) = call(
        scatter_kernel,
        [((112, 512), f32, True)],
        (near(recv3), near(hot), near(local)),
        name="scatter",
    )
    grads = lax.all_gather(grads, "rep", axis=0, tiled=True)
    table_new, state_new = call(
        finish_kernel,
        [((400, 512), f32, False), ((1, 512), f32, False)],
        (near(grads), table_t, adagrad_state.reshape(1, 512)),
        name="finish",
    )
    return (table_new.T, state_new.reshape(512))


def solution(mesh):
    placed = (
        P("ent", None),
        P("ent"),
        P(("ent", "rep"), None),
        P(("ent", "rep")),
        P(("ent", "rep")),
        P(("ent", "rep"), None),
        P(("ent", "rep")),
        P("ent"),
        P(),
    )
    return jax.shard_map(
        on_device, mesh=mesh, in_specs=placed, out_specs=(P("ent", None), P("ent")), check_vma=False
    )
```
